32 devices in a mesh: dp: 4 (over z), fsdp: 8 (over y, x, core).
Axes of the slice: x: 2, y: 2, z: 4, core: 2. Of those that a mesh axis runs over, the one named last changes fastest.
Arguments:
- tokens: bfloat16 [2, 32, 1024, 1024], P(None, 'fsdp', 'dp'), may hold values from -6 to 6
- cotangent: bfloat16 [2, 32, 1024, 1024], P(None, 'fsdp', 'dp'), may hold values from -6 to 6
- teacher: bfloat16 [2, 32, 1024, 1024], P(None, ('dp', 'fsdp')), may hold values from -6 to 6
- lengths: int32 [2, 32], replicated, may hold values from 1 to 1024, 24576 in all within a row
- dealing: int32 [2, 32], replicated, may hold values from 0 to 3, as said below
- loss_mask: int32 [2, 32, 1024], P(None, ('dp', 'fsdp')), may hold values 0 or 1
- norm_gain: bfloat16 [1024], P(('dp', 'fsdp')), may hold values from 0.5 to 1.5
- norm_bias: bfloat16 [1024], P(('dp', 'fsdp')), may hold values from -2 to 2
- gate_weight: bfloat16 [1024, 3072], P(('dp', 'fsdp')), may hold values from -0.1875 to 0.1875
- reduce_weight: bfloat16 [1024, 512], P(('dp', 'fsdp')), may hold values from -0.1875 to 0.1875
- state_weight: float32 [2, 512, 512], P(None, ('dp', 'fsdp')), may hold values from -0.00390625 to 0.00390625
- decay_rate: float32 [512, 512], P(('dp', 'fsdp')), may hold values from -0.5 to -0.01
- frequency: float32 [512, 512], P(('dp', 'fsdp')), may hold values from -6 to 6
- log_step: float32 [512], P(('dp', 'fsdp')), may hold values from -5.3 to -0.7
- expand_weight: bfloat16 [512, 3072], P(('dp', 'fsdp')), may hold values from -0.25 to 0.25
- out_weight: bfloat16 [3072, 1024], P(('dp', 'fsdp')), may hold values from -0.21875 to 0.21875
Outputs:
- output: bfloat16 [2, 32, 1024, 1024], P(None, 'fsdp', 'dp')
- loss: float32 [], replicated
- tokens_grad: bfloat16 [2, 32, 1024, 1024], P(None, 'fsdp', 'dp')
- gain_grad: float32 [1024], P(('dp', 'fsdp'))
- bias_grad: float32 [1024], P(('dp', 'fsdp'))
- gate_weight_grad: float32 [1024, 3072], P(('dp', 'fsdp'))
- reduce_weight_grad: float32 [1024, 512], P(('dp', 'fsdp'))
- state_weight_grad: float32 [2, 512, 512], P(None, ('dp', 'fsdp'))
- decay_rate_grad: float32 [512, 512], P(('dp', 'fsdp'))
- frequency_grad: float32 [512, 512], P(('dp', 'fsdp'))
- log_step_grad: float32 [512], P(('dp', 'fsdp'))
- expand_weight_grad: float32 [512, 3072], P(('dp', 'fsdp'))
- out_weight_grad: float32 [3072, 1024], P(('dp', 'fsdp'))
The draws below stay inside these ranges and needn't reach their ends.
Inputs may be any that keep to these rules, and one draw needn't show every extreme that they name: `dealing`: in each micro-batch, the entries of sequences g * 4 to g * 4 + 3 are a permutation of 0 to 3. Each micro-batch's lengths sum to 24576, and the longest is 1024.
All inputs are finite; a program needn't handle non-finite values. No bound on the sum of `loss_mask` on one device may be relied on, other than what follows from the above.
Results may differ from the reference program's by a relative error of at most 0.0063.
Values may be sent and summed in bfloat16 or wider, within the bound.
A program may use at most 320 MiB of HBM per device.

```python
import math
import jax
import jax.numpy as jnp
import numpy as np
from jax import lax

D = 1024
F = 3072
H = 512
N = 512
LMAX = 1024
MB = 2
NSEQ = 32
N_DP = 4
N_FSDP = 8


def shuffle_one(single_key):
    return jax.random.permutation(single_key, N_DP)


def draw_dealing(key, part):
    key_list = jax.random.split(key, MB * N_FSDP)
    shuffled = jax.vmap(shuffle_one)(key_list)
    return shuffled.reshape(MB, N_FSDP * N_DP).astype(jnp.int32)


def plant(result, stream_key, least, largest):
    spot = [jax.random.randint(jax.random.fold_in(stream_key, axis), (), 0, length) for axis, length in enumerate(result.shape)]
    main_axis = result.shape.index(max(result.shape))
    beside = spot[:main_axis] + [(spot[main_axis] + 1) % result.shape[main_axis]] + spot[main_axis + 1:]
    return result.at[tuple(spot)].set(least).at[tuple(beside)].set(largest)


def levels(stream_key, dims, shards, least, largest):
    factor_of, own = 1.0, jax.random.fold_in(stream_key, 6)
    for axis_at, parts in shards:
        heights = jnp.exp(jax.random.uniform(jax.random.fold_in(own, axis_at), (parts,), jnp.float32, least / len(shards), largest / len(shards)))
        factor_of = factor_of * jnp.repeat(heights, dims[axis_at] // parts).reshape([-1 if axis == axis_at else 1 for axis in range(len(dims))])
    return factor_of


def profile(amount, total, most, slope):
    loads = [(1 << 20) // math.isqrt(grade ** slope) + 1 for grade in range(2, amount + 1)]
    spare, holding = total - most - (amount - 1), [1] * (amount - 1)
    while spare > 0:
        candidates = [i for i in range(amount - 1) if holding[i] < most]
        pool, left = sum([loads[i] for i in candidates]), spare
        for i in candidates:
            addition = min(most - holding[i], max(1, left * loads[i] // pool), spare)
            holding[i] = holding[i] + addition
            spare = spare - addition
    return np.array([most] + holding)


def uneven(rng, count, total, reach, lean):
    if count == 2:
        one = jax.random.randint(rng, (), max(1, total - reach), min(reach, total - 1) + 1)
        return jnp.stack([one, total - one])
    sizes = jnp.asarray(profile(count, total, reach, lean), jnp.int32)
    couples = (count - 1) // 2
    giver, sink = sizes[1:1 + 2 * couples:2], sizes[2:2 + 2 * couples:2]
    room = jnp.minimum(giver - 1, reach - sink)
    passed = jax.random.randint(jax.random.fold_in(rng, 1), (couples,), 0, 1 << 20) % (room + 1)
    sizes = sizes.at[1:1 + 2 * couples:2].set(giver - passed).at[2:2 + 2 * couples:2].set(sink + passed)
    return sizes[jax.random.permutation(jax.random.fold_in(rng, 2), count)]


def noise(stream_key, extent, deviation, bound, cuts=(), held_as=jnp.bfloat16):
    level = levels(stream_key, extent, cuts, -0.22, 0.18) if cuts else 1.0
    values = jax.random.normal(stream_key, extent, jnp.float32) * deviation * level
    return jnp.minimum(jnp.maximum(values, -bound), bound).astype(held_as)


def setup_inputs(seed: int = 0) -> dict:
    keys = jax.random.split(jax.random.key(seed), 17)
    return {
        "tokens": noise(keys[0], (MB, NSEQ, LMAX, D), 1.0, 6.0, ((1, 8), (2, 4))),
        "cotangent": noise(keys[1], (MB, NSEQ, LMAX, D), 1.0, 6.0, ((1, 8), (2, 4))),
        "teacher": noise(keys[2], (MB, NSEQ, LMAX, D), 1.0, 6.0, ((1, 32),)),
        "lengths": jax.vmap(lambda own: uneven(own, NSEQ, NSEQ * LMAX * 3 // 4, LMAX, 2))(jax.random.split(keys[3], MB)).reshape((MB, NSEQ)).astype(jnp.int32),
        "dealing": draw_dealing(jax.random.fold_in(keys[16], 71), 0),
        "loss_mask": plant((jax.random.randint(keys[5], (MB, NSEQ, LMAX), 0, 4) < 3).astype(jnp.int32), jax.random.fold_in(keys[5], 1), 0, 1),
        "norm_gain": jnp.clip(1.0 + 0.1 * jax.random.normal(keys[6], (D,), jnp.float32), 0.5, 1.5).astype(jnp.bfloat16),
        "norm_bias": noise(keys[7], (D,), 0.3, 2.0, ((0, 32),)),
        "gate_weight": noise(keys[8], (D, F), D ** -0.5, 0.1875, ((0, 32),)),
        "reduce_weight": noise(keys[9], (D, H), D ** -0.5, 0.1875, ((0, 32),)),
        "state_weight": noise(keys[10], (2, H, N), (N * LMAX * 4) ** -0.5, 0.00390625, ((1, 32),), jnp.float32),
        "decay_rate": jnp.clip(-0.5 + 0.49 * jax.random.uniform(keys[11], (H, N), jnp.float32) ** levels(keys[11], (H, N), ((0, 32),), -0.2, 0.2), -0.5, -0.01),
        "frequency": jnp.clip(jax.random.uniform(keys[12], (H, N), jnp.float32, -6.0, 6.0) * levels(keys[12], (H, N), ((0, 32),), -0.4, 0.0), -6.0, 6.0),
        "log_step": jnp.clip(-5.3 + 4.6000002 * jax.random.uniform(keys[13], (H,), jnp.float32) ** levels(keys[13], (H,), ((0, 32),), -0.2, 0.2), -5.3, -0.7),
        "expand_weight": noise(keys[14], (H, F), H ** -0.5, 0.25, ((0, 32),)),
        "out_weight": noise(keys[15], (F, D), (F // 4) ** -0.5, 0.21875, ((0, 32),)),
    }


epsilon = 1e-05
highest = lax.Precision.HIGHEST

@jax.custom_vjp
def low(v):
    return lax.optimization_barrier(v.astype(jnp.bfloat16)).astype(jnp.float32)

@jax.custom_vjp
def low_back(v):
    return v

def low_keep(v):
    return (low(v), None)

def low_pass(kept, grad):
    return (grad,)

def back_keep(v):
    return (v, None)

def back_low(kept, grad):
    return (low(grad),)
low.defvjp(low_keep, low_pass)
low_back.defvjp(back_keep, back_low)

def kernel_rows(weight_pair, decay, frequency, log_step, positions):
    step_size = jnp.exp(log_step)
    damping = jnp.exp((step_size[:, None] * decay)[:, :, None] * positions)
    angle = (step_size[:, None] * frequency)[:, :, None] * positions
    waves = weight_pair[0][:, :, None] * jnp.cos(angle) - weight_pair[1][:, :, None] * jnp.sin(angle)
    return lax.optimization_barrier(jnp.sum(damping * waves, axis=1))

def batched(left, right):
    return jnp.einsum('gtd,df->gtf', left, right, precision=highest)

def pick_rows(table_rows, index_rows):
    return jnp.take(table_rows, index_rows, axis=0)

def reference(tokens, cotangent, teacher, lengths, dealing, loss_mask, norm_gain, norm_bias, gate_weight, reduce_weight, state_weight, decay_rate, frequency, log_step, expand_weight, out_weight):
    positions = jnp.arange(LMAX, dtype=jnp.int32)
    float_positions = positions.astype(jnp.float32)
    seq_ids = jnp.arange(NSEQ, dtype=jnp.int32)
    slots = (dealing * N_FSDP + seq_ids[None, :] // N_DP).astype(jnp.int32)
    teach = jax.vmap(pick_rows)(teacher, slots).astype(jnp.float32)
    masked = jax.vmap(pick_rows)(loss_mask, slots).astype(jnp.float32)
    valid = (positions[None, None, :] < lengths[:, :, None]).astype(jnp.float32)
    keep = masked * valid
    count = jnp.sum(keep)
    groups = MB * NSEQ // 4
    blocks = H // 16

    def forward(inputs, gain, bias, w_gate, w_reduce, pair, decay, freq_values, step_logs, w_expand, w_out):

        def one_block(items):
            return kernel_rows(items[0], items[1], items[2], items[3], float_positions)
        kernel = lax.map(jax.checkpoint(one_block), (pair.reshape(2, blocks, 16, N).transpose(1, 0, 2, 3), decay.reshape(blocks, 16, N), freq_values.reshape(blocks, 16, N), step_logs.reshape(blocks, 16)))
        kernel = kernel.reshape(H, LMAX).T
        kernel_spec = jnp.fft.rfft(kernel, n=2 * LMAX, axis=0)

        def one_group(items):
            rows_in, valid_rows = items
            centre = lax.optimization_barrier(jnp.mean(rows_in, axis=-1, keepdims=True))
            centred = rows_in - centre
            variance = lax.optimization_barrier(jnp.mean(centred * centred, axis=-1, keepdims=True))
            normed = low(centred * lax.rsqrt(variance + epsilon) * gain + bias)
            pre_gate = low_back(batched(normed, w_gate))
            gate = jax.nn.gelu(pre_gate, approximate=False)
            pre_reduced = low_back(batched(normed, w_reduce))
            reduced = jax.nn.gelu(pre_reduced, approximate=False)
            spectrum = jnp.fft.rfft(reduced, n=2 * LMAX, axis=1)
            mixed = jnp.fft.irfft(spectrum * kernel_spec[None], n=2 * LMAX, axis=1)[:, :LMAX]
            state_out = low(mixed)
            expanded = low_back(batched(state_out, w_expand))
            product = low(expanded * gate)
            branch = low_back(batched(product, w_out))
            return rows_in + valid_rows[..., None] * branch
        full = lax.map(jax.checkpoint(one_group), (inputs.reshape(groups, 4, LMAX, D), valid.reshape(groups, 4, LMAX)))
        full = full.reshape(MB, NSEQ, LMAX, D)
        errors = full - teach
        loss_value = jnp.sum(keep[..., None] * errors * errors) / (D * count)
        return (full, loss_value)
    primals = (tokens.astype(jnp.float32), norm_gain.astype(jnp.float32), norm_bias.astype(jnp.float32), gate_weight.astype(jnp.float32), reduce_weight.astype(jnp.float32), state_weight, decay_rate, frequency, log_step, expand_weight.astype(jnp.float32), out_weight.astype(jnp.float32))
    (full, loss_value), pullback = jax.vjp(forward, *primals)
    grads = pullback((cotangent.astype(full.dtype), jnp.ones_like(loss_value)))
    return (full.astype(jnp.bfloat16), loss_value, grads[0].astype(jnp.bfloat16), grads[1], grads[2], grads[3], grads[4], grads[5], grads[6], grads[7], grads[8], grads[9], grads[10])
```

```python
import numpy as np
import jax
import jax.numpy as jnp
from jax import lax
from jax.sharding import PartitionSpec as P

epsilon = 1e-05
highest = lax.Precision.HIGHEST
high = lax.Precision.HIGH
bf16 = jnp.bfloat16
f32 = jnp.float32
both = ("dp", "fsdp")


def matmul(left, right):
    return jnp.dot(left, right, preferred_element_type=f32)


def rows_inner(left, right):
    return lax.dot_general(left, right, (((0,), (0,)), ((), ())), preferred_element_type=f32)


def cols_inner(left, right):
    return lax.dot_general(left, right, (((1,), (1,)), ((), ())), preferred_element_type=f32)


def gelu_and_slope(values):
    phi = 0.5 * (1.0 + lax.erf(values * 0.7071067811865476))
    return (
        values * phi,
        phi + values * jnp.exp(-0.5 * values * values) * 0.3989422804014327,
    )


def fourier_table(chunk):
    freq = np.arange(chunk)[:, None]
    time = np.arange(chunk)[None, :]
    angle = (freq * time % (2 * chunk)) * (np.pi / chunk)
    sines = -np.sin(angle)
    sines[0] = 1.0 - 2.0 * (np.arange(chunk) % 2)
    table = np.concatenate([np.cos(angle), sines], axis=0)
    scaling = np.full((2 * chunk, 1), 1.0 / chunk)
    scaling[0] = scaling[chunk] = 0.5 / chunk
    sign = np.tile(1.0 - 2.0 * (np.arange(chunk) % 2), 2)
    sign[chunk] = 1.0 - 2.0 * (chunk % 2)
    return table.astype(np.float32), (table * scaling).astype(np.float32), sign.astype(np.float32)


def packed_product(first, second, chunk, conjugate):
    a_re, a_im = first[..., :chunk, :, :], first[..., chunk:, :, :]
    b_re, b_im = second[..., :chunk, :, :], second[..., chunk:, :, :]
    edge = (jnp.arange(chunk) == 0)[:, None, None]
    crossed = a_im * b_im
    straight = a_re * b_re
    if conjugate:
        real = straight + jnp.where(edge, 0.0, crossed)
        imag = jnp.where(edge, crossed, a_re * b_im - a_im * b_re)
    else:
        real = straight - jnp.where(edge, 0.0, crossed)
        imag = jnp.where(edge, crossed, a_re * b_im + a_im * b_re)
    return jnp.concatenate([real, imag], axis=-3)


def kernel_factors(decay, frequency, log_step, length):
    fine = 32
    coarse = length // fine
    step_size = jnp.exp(log_step)[:, None]
    real = (step_size * decay)[:, None, :]
    imag = (step_size * frequency)[:, None, :]
    far = (jnp.arange(coarse, dtype=jnp.int32) * fine).astype(f32)[None, :, None]
    near = jnp.arange(fine, dtype=jnp.int32).astype(f32)[None, :, None]
    far_damp, near_damp = jnp.exp(real * far), jnp.exp(real * near)
    return (
        (far_damp * jnp.cos(imag * far), far_damp * jnp.sin(imag * far)),
        (near_damp * jnp.cos(imag * near), near_damp * jnp.sin(imag * near)),
        step_size,
    )


def kernel_forward(weight_pair, factors):
    (far_re, far_im), (near_re, near_im), _ = factors
    w_re, w_im = weight_pair[0][:, None, :], weight_pair[1][:, None, :]
    left = jnp.concatenate([far_re, -far_im], axis=2)
    right = jnp.concatenate(
        [w_re * near_re - w_im * near_im, w_re * near_im + w_im * near_re], axis=2
    )
    rows = jnp.einsum("han,hbn->hab", left, right, precision=highest)
    return rows.reshape(rows.shape[0], -1)


def kernel_backward(grad_rows, weight_pair, decay, frequency, factors):
    (far_re, far_im), (near_re, near_im), step_size = factors
    channels, coarse, states = far_re.shape
    fine = near_re.shape[1]
    tiles = grad_rows.reshape(channels, coarse, fine)
    near_index = jnp.arange(fine, dtype=jnp.int32).astype(f32)
    far_index = (jnp.arange(coarse, dtype=jnp.int32) * fine).astype(f32)[None, :, None]
    stacked = jnp.concatenate([tiles, tiles * near_index], axis=1)
    part = jnp.einsum(
        "hab,hbn->han", stacked, jnp.concatenate([near_re, near_im], axis=2), precision=highest
    )
    u_re, u_im = part[:, :coarse, :states], part[:, :coarse, states:]
    v_re = part[:, coarse:, :states] + far_index * u_re
    v_im = part[:, coarse:, states:] + far_index * u_im
    s_re = jnp.sum(far_re * u_re - far_im * u_im, axis=1)
    s_im = jnp.sum(far_re * u_im + far_im * u_re, axis=1)
    t_re = jnp.sum(far_re * v_re - far_im * v_im, axis=1)
    t_im = jnp.sum(far_re * v_im + far_im * v_re, axis=1)
    w_re, w_im = weight_pair[0], weight_pair[1]
    along_re = step_size * (w_re * t_re - w_im * t_im)
    along_im = -step_size * (w_re * t_im + w_im * t_re)
    return (
        jnp.stack([s_re, -s_im]),
        along_re,
        along_im,
        jnp.sum(decay * along_re + frequency * along_im, axis=1),
    )


def exchange(values):
    return lax.all_to_all(values, "dp", split_axis=0, concat_axis=0, tiled=True)


def scatter_sum(values):
    dp_count, fsdp_count = lax.axis_size("dp"), lax.axis_size("fsdp")
    _, height, width = values.shape
    tiles = values.reshape(dp_count, fsdp_count, height, width).transpose(1, 0, 2, 3)
    part = lax.psum_scatter(
        tiles.reshape(-1, width), "fsdp", scatter_dimension=0, tiled=True
    )
    return lax.psum_scatter(part, "dp", scatter_dimension=0, tiled=True)


def shards(
    tokens,
    cotangent,
    teacher,
    lengths,
    dealing,
    loss_mask,
    norm_gain,
    norm_bias,
    gate_weight,
    reduce_weight,
    state_weight,
    decay_rate,
    frequency,
    log_step,
    expand_weight,
    out_weight,
):
    dp_count = lax.axis_size("dp")
    devices = dp_count * lax.axis_size("fsdp")
    group_index = lax.axis_index("fsdp")
    dp_place = lax.axis_index("dp")
    micro_count, seqs, chunk, model_width = tokens.shape
    rows = seqs * chunk
    seq_length = chunk * dp_count
    gate_width = gate_weight.shape[1]
    reduced_width = reduce_weight.shape[1]
    own_width = reduced_width // dp_count
    table_np, inverse_np, sign_np = fourier_table(chunk)
    table, inverse, sign = jnp.asarray(table_np), jnp.asarray(inverse_np), jnp.asarray(sign_np)

    teach = lax.all_to_all(
        teacher.reshape(micro_count, dp_count, chunk, model_width), "dp", split_axis=1, concat_axis=1, tiled=True
    )
    masked = lax.all_to_all(
        loss_mask.reshape(micro_count, dp_count, chunk), "dp", split_axis=1, concat_axis=1, tiled=True
    )
    local_ids = group_index * seqs + jnp.arange(seqs, dtype=jnp.int32)
    targets = jnp.take(dealing, local_ids, axis=1)
    own_lengths = jnp.take(lengths, local_ids, axis=1)
    positions = dp_place * chunk + jnp.arange(chunk, dtype=jnp.int32)
    valid = (positions[None, None, :] < own_lengths[:, :, None]).astype(f32)
    keep = jnp.stack([jnp.take(masked[m], targets[m], axis=0) for m in range(micro_count)]).astype(f32) * valid
    teach = [jnp.take(teach[m], targets[m], axis=0).reshape(rows, model_width) for m in range(micro_count)]
    count = lax.psum(jnp.sum(keep), both)
    valid = valid.reshape(micro_count, rows, 1)
    keep = keep.reshape(micro_count, rows, 1)

    share = gate_weight.shape[0]
    extra = jnp.concatenate(
        [norm_gain[:, None], norm_bias[:, None], jnp.zeros((share, 126), bf16)], axis=1
    )
    first = lax.all_gather(
        jnp.concatenate([gate_weight, reduce_weight, extra], axis=1), both, axis=0, tiled=True
    )
    w_expand = lax.all_gather(expand_weight, both, axis=0, tiled=True)
    w_out = lax.all_gather(out_weight, both, axis=0, tiled=True)
    w_gate = first[:, :gate_width]
    w_reduce = first[:, gate_width : gate_width + reduced_width]
    gain_values = first[:, gate_width + reduced_width].astype(f32)
    bias_values = first[:, gate_width + reduced_width + 1].astype(f32)

    factors = kernel_factors(decay_rate, frequency, log_step, seq_length)
    own_kernel = kernel_forward(state_weight, factors)
    kernel = lax.all_gather(own_kernel, "fsdp", axis=0, tiled=True)
    segments = jnp.einsum(
        "kt,hct->ckh", table, kernel.reshape(own_width, dp_count, chunk), precision=highest
    )
    previous = jnp.concatenate([jnp.zeros_like(segments[:1]), segments[:-1]], axis=0)
    kernel_spec = (segments + sign[:, None] * previous)[:, :, None, :]

    def spectrum(values):
        flat = values.reshape(dp_count, chunk, seqs * own_width).astype(f32)
        spec = jnp.einsum("kt,ctn->ckn", table, flat, precision=high)
        return spec.reshape(dp_count, 2 * chunk, seqs, own_width)

    def back_to_time(spec):
        flat = spec.reshape(dp_count, 2 * chunk, seqs * own_width)
        return jnp.einsum("kt,ckn->ctn", inverse, flat, precision=high)

    def to_channels(values):
        split = values.reshape(seqs, chunk, dp_count, own_width).transpose(2, 1, 0, 3)
        return exchange(split.astype(bf16).reshape(dp_count, chunk, seqs * own_width))

    def to_rows(values):
        back = exchange(values.astype(bf16))
        return back.reshape(dp_count, chunk, seqs, own_width).transpose(2, 1, 0, 3).reshape(rows, reduced_width)

    error_total = jnp.zeros((), f32)
    outputs, returned, saved = [], [], []
    for m in range(micro_count):
        inputs = tokens[m].reshape(rows, model_width).astype(f32)
        centre = jnp.mean(inputs, axis=1, keepdims=True)
        centred = inputs - centre
        variance = jnp.mean(centred * centred, axis=1, keepdims=True)
        inverse_std = lax.rsqrt(variance + epsilon)
        unit = centred * inverse_std
        normed = (unit * gain_values + bias_values).astype(bf16)
        pre_reduced = matmul(normed, w_reduce)
        reduced, slope_reduced = gelu_and_slope(pre_reduced)
        channel_rows = to_channels(reduced)
        pre_gate = matmul(normed, w_gate)
        gate, slope_gate = gelu_and_slope(pre_gate)
        saved.append((inputs, inverse_std, unit, normed, slope_reduced, channel_rows, gate, slope_gate))

    middle = []
    for m in range(micro_count):
        channel_rows = saved[m][5]
        reduced_spec = spectrum(channel_rows)
        mixed_spec = [
            sum(
                packed_product(kernel_spec[k], reduced_spec[c - k], chunk, False)
                for k in range(c + 1)
            )
            for c in range(dp_count)
        ]
        middle.append((reduced_spec, to_rows(back_to_time(jnp.stack(mixed_spec)))))

    kernel_total = jnp.zeros((dp_count, 2 * chunk, own_width), f32)
    later = []
    out_total, expand_total = 0.0, 0.0
    for m in range(micro_count):
        inputs, inverse_std, unit, normed, slope_reduced, channel_rows, gate, slope_gate = saved[m]
        reduced_spec, state_out = middle[m]
        expanded = matmul(state_out, w_expand)
        product = (expanded * gate).astype(bf16)
        branch = matmul(product, w_out)
        full = inputs + valid[m] * branch
        outputs.append(full.astype(bf16).reshape(seqs, chunk, model_width))
        errors = full - teach[m].astype(f32)
        error_total = error_total + jnp.sum(keep[m] * errors * errors)
        grad_full = cotangent[m].reshape(rows, model_width).astype(f32) + keep[m] * errors * (
            2.0 / (model_width * count)
        )
        grad_branch = (valid[m] * grad_full).astype(bf16)
        grad_product = cols_inner(grad_branch, w_out)
        grad_expanded = (grad_product * gate).astype(bf16)
        grad_pre_gate = (grad_product * expanded * slope_gate).astype(bf16)
        grad_mixed = cols_inner(grad_expanded, w_expand)
        grad_rows = to_channels(grad_mixed)
        out_total = out_total + rows_inner(product, grad_branch)
        expand_total = expand_total + rows_inner(state_out, grad_expanded)
        later.append((grad_full, grad_pre_gate, grad_rows))
    late_sum = scatter_sum(
        jnp.concatenate([out_total.reshape(devices, -1), expand_total.reshape(devices, -1)], axis=1).reshape(
            devices, -1, 1024
        )
    )

    gate_total, reduce_total = 0.0, 0.0
    gain_total, bias_total = 0.0, 0.0
    ends = []
    for m in range(micro_count):
        inputs, inverse_std, unit, normed, slope_reduced, channel_rows, gate, slope_gate = saved[m]
        reduced_spec = middle[m][0]
        grad_full, grad_pre_gate, grad_rows = later[m]
        grad_spec = spectrum(grad_rows)
        back_spec = [
            sum(
                packed_product(kernel_spec[c - k], grad_spec[c], chunk, True)
                for c in range(k, dp_count)
            )
            for k in range(dp_count)
        ]
        grad_reduced = to_rows(back_to_time(jnp.stack(back_spec)))
        cross = [
            sum(
                packed_product(reduced_spec[c - k], grad_spec[c], chunk, True)
                for c in range(k, dp_count)
            )
            for k in range(dp_count)
        ]
        kernel_total = kernel_total + jnp.sum(jnp.stack(cross), axis=2)
        gate_total = gate_total + rows_inner(normed, grad_pre_gate)
        ends.append((grad_full, grad_pre_gate, grad_reduced))
    for m in range(micro_count):
        inputs, inverse_std, unit, normed, slope_reduced, channel_rows, gate, slope_gate = saved[m]
        grad_full, grad_pre_gate, grad_reduced = ends[m]
        grad_pre_reduced = (grad_reduced.astype(f32) * slope_reduced).astype(bf16)
        reduce_total = reduce_total + rows_inner(normed, grad_pre_reduced)
        grad_normed = cols_inner(grad_pre_gate, w_gate) + cols_inner(grad_pre_reduced, w_reduce)
        gain_total = gain_total + jnp.sum(grad_normed * unit, axis=0)
        bias_total = bias_total + jnp.sum(grad_normed, axis=0)
        grad_unit = grad_normed * gain_values
        grad_inputs = grad_full + inverse_std * (
            grad_unit
            - jnp.mean(grad_unit, axis=1, keepdims=True)
            - unit * jnp.mean(grad_unit * unit, axis=1, keepdims=True)
        )
        returned.append(grad_inputs.astype(bf16).reshape(seqs, chunk, model_width))

    following = jnp.concatenate([kernel_total[1:], jnp.zeros_like(kernel_total[:1])], axis=0)
    kernel_grad = jnp.einsum(
        "kt,ckh->hct", inverse, kernel_total + sign[:, None] * following, precision=highest
    ).reshape(reduced_width // dp_count, seq_length)
    kernel_grad = lax.psum_scatter(kernel_grad, "fsdp", scatter_dimension=0, tiled=True)
    pair_grad, decay_grad, frequency_grad, step_grad = kernel_backward(
        kernel_grad, state_weight, decay_rate, frequency, factors
    )
    last_sum = scatter_sum(
        jnp.concatenate([gate_total.reshape(devices, -1), reduce_total.reshape(devices, -1)], axis=1).reshape(
            devices, -1, 1024
        )
    )
    sums = lax.psum(jnp.concatenate([gain_total, bias_total, jnp.full((128,), error_total)]), both)
    place = (dp_place * lax.axis_size("fsdp") + group_index) * share
    loss_value = sums[2 * model_width] / (model_width * count)
    late_flat, last_flat = late_sum.reshape(-1), last_sum.reshape(-1)
    out_size, gate_size = out_weight.size, gate_weight.size
    return (
        jnp.stack(outputs),
        loss_value,
        jnp.stack(returned),
        lax.dynamic_slice(sums, (place,), (share,)),
        lax.dynamic_slice(sums, (model_width + place,), (share,)),
        last_flat[:gate_size].reshape(gate_weight.shape),
        last_flat[gate_size:].reshape(reduce_weight.shape),
        pair_grad,
        decay_grad,
        frequency_grad,
        step_grad,
        late_flat[out_size:].reshape(expand_weight.shape),
        late_flat[:out_size].reshape(out_weight.shape),
    )


def solution(mesh):
    in_specs = (
        P(None, "fsdp", "dp", None),
        P(None, "fsdp", "dp", None),
        P(None, ("dp", "fsdp"), None, None),
        P(),
        P(),
        P(None, ("dp", "fsdp"), None),
        P(("dp", "fsdp")),
        P(("dp", "fsdp")),
        P(("dp", "fsdp"), None),
        P(("dp", "fsdp"), None),
        P(None, ("dp", "fsdp"), None),
        P(("dp", "fsdp"), None),
        P(("dp", "fsdp"), None),
        P(("dp", "fsdp")),
        P(("dp", "fsdp"), None),
        P(("dp", "fsdp"), None),
    )
    out_specs = (
        P(None, "fsdp", "dp", None),
        P(),
        P(None, "fsdp", "dp", None),
        P(("dp", "fsdp")),
        P(("dp", "fsdp")),
        P(("dp", "fsdp"), None),
        P(("dp", "fsdp"), None),
        P(None, ("dp", "fsdp"), None),
        P(("dp", "fsdp"), None),
        P(("dp", "fsdp"), None),
        P(("dp", "fsdp")),
        P(("dp", "fsdp"), None),
        P(("dp", "fsdp"), None),
    )
    return jax.shard_map(shards, mesh=mesh, in_specs=in_specs, out_specs=out_specs, check_vma=False)
```

```python
import functools

import numpy as np
import jax
import jax.numpy as jnp
from jax import lax
from jax.experimental import pallas as pl
from jax.experimental.pallas import tpu as pltpu
from jax.sharding import PartitionSpec as P

epsilon = 1e-05
highest = lax.Precision.HIGHEST
bf16 = jnp.bfloat16
f32 = jnp.float32
MESH = pl.DeviceIdType.MESH
ANY = pl.BlockSpec(memory_space=pl.ANY)


def bit_of(index, bit):
    return lax.rem(lax.div(index, 1 << bit), 2)


def flip(index, bit):
    return index + (1 << bit) - 2 * (1 << bit) * bit_of(index, bit)


def greet(dp_count, bits):
    d, f = lax.axis_index("dp"), lax.axis_index("fsdp")
    barrier = pltpu.get_barrier_semaphore()
    for o in range(1, dp_count):
        peer = lax.rem(d + o, dp_count)
        pl.semaphore_signal(barrier, inc=1, device_id={"dp": peer}, device_id_type=MESH)
    for b in range(bits):
        pl.semaphore_signal(barrier, inc=1, device_id={"fsdp": flip(f, b)}, device_id_type=MESH)
    pl.semaphore_wait(barrier, dp_count - 1 + bits)


def near_first(count):
    order = [0]
    for k in range(1, count // 2 + 1):
        order += [k] if k == count - k else [k, count - k]
    return order


def gather_body(dp_count, bits, n, *refs):
    ins, outs = refs[:n], refs[n : 2 * n]
    z_send, z_recv, send, recv, own_sem = refs[2 * n :]
    d, f = lax.axis_index("dp"), lax.axis_index("fsdp")
    cuts = []
    for x in ins:
        cut = x.shape[1] // 256 * 128
        cuts.append(((0, cut), (cut, x.shape[1] - cut)))
    greet(dp_count, bits)
    own = [
        pltpu.make_async_copy(ins[a], outs[a].at[d, f], own_sem.at[a]) for a in range(n)
    ]
    for copy in own:
        copy.start()
    started, arrived, waited = [], {}, set()
    order = near_first(dp_count)
    for o in order[1:]:
        for h in range(2):
            for a in range(n):
                lo, size = cuts[a][h]
                copy = pltpu.make_async_remote_copy(
                    src_ref=ins[a].at[:, pl.ds(lo, size)],
                    dst_ref=outs[a].at[d, f, :, pl.ds(lo, size)],
                    send_sem=z_send.at[o - 1, h, a],
                    recv_sem=z_recv.at[o - 1, h, a],
                    device_id={"dp": lax.rem(d + o, dp_count)},
                    device_id_type=MESH,
                )
                copy.start()
                started.append(copy)
                arrived[(o, 0, h, a)] = copy
    for copy in own:
        copy.wait()
    upper = list(range(1, bits))
    stages = [upper + [0], upper[::-1] + [0]]
    held = [[0], [0]]
    slot = 0
    for s in range(bits):
        fresh = [[], []]
        for mi in range(len(held[0])):
            for o in order:
                for h in range(2):
                    mask, b = held[h][mi], stages[h][s]
                    src_d = lax.rem(d - o + dp_count, dp_count)
                    src_f = f
                    for bb in range(bits):
                        if mask >> bb & 1:
                            src_f = flip(src_f, bb)
                    for a in range(n):
                        key = (o, mask, h, a)
                        if key in arrived and key not in waited:
                            arrived[key].wait_recv()
                            waited.add(key)
                        lo, size = cuts[a][h]
                        piece = outs[a].at[src_d, src_f, :, pl.ds(lo, size)]
                        copy = pltpu.make_async_remote_copy(
                            src_ref=piece,
                            dst_ref=piece,
                            send_sem=send.at[slot],
                            recv_sem=recv.at[slot],
                            device_id={"fsdp": flip(f, b)},
                            device_id_type=MESH,
                        )
                        copy.start()
                        started.append(copy)
                        arrived[(o, mask ^ (1 << b), h, a)] = copy
                        slot += 1
                    if o == 0:
                        fresh[h].append(mask ^ (1 << b))
        held = [held[h] + fresh[h] for h in range(2)]
    for key, copy in arrived.items():
        if key not in waited:
            copy.wait_recv()
    for copy in started:
        copy.wait_send()


def gather_all(arrays, collective_id):
    dp_count, fsdp_count = lax.axis_size("dp"), lax.axis_size("fsdp")
    bits = fsdp_count.bit_length() - 1
    n = len(arrays)
    slots = 2 * dp_count * (fsdp_count - 1) * n
    return pl.pallas_call(
        functools.partial(gather_body, dp_count, bits, n),
        out_shape=[
            jax.ShapeDtypeStruct((dp_count, fsdp_count, *x.shape), x.dtype) for x in arrays
        ],
        in_specs=[ANY] * n,
        out_specs=[ANY] * n,
        scratch_shapes=[
            pltpu.SemaphoreType.DMA((dp_count - 1, 2, n)),
            pltpu.SemaphoreType.DMA((dp_count - 1, 2, n)),
            pltpu.SemaphoreType.DMA((slots,)),
            pltpu.SemaphoreType.DMA((slots,)),
            pltpu.SemaphoreType.DMA((n,)),
        ],
        compiler_params=pltpu.CompilerParams(collective_id=collective_id, has_side_effects=True),
    )(*arrays)


def scatter_body(dp_count, bits, pieces, kinds, *refs):
    n_in, n = len(kinds), len(pieces)
    ins, outs = refs[:n_in], refs[n_in : 2 * n_in]
    per = 6 + 2 * (bits - 1)
    scratch = [refs[2 * n_in + i * per : 2 * n_in + (i + 1) * per] for i in range(n)]
    load_sem, send, recv, store_sem = refs[2 * n_in + n * per :]
    d, f = lax.axis_index("dp"), lax.axis_index("fsdp")
    my = [bit_of(f, b) for b in range(bits)]
    upper = list(range(bits - 1, 0, -1))
    waits, fixed, ends = [None] * n, [{} for _ in range(n)], []
    greet(dp_count, bits)

    def region(i, other=None):
        return (slice(None),) + tuple(
            1 - my[b] if b == other else fixed[i].get(b, slice(None)) for b in upper
        )

    def push(i, at, src, dst, device_id):
        copy = pltpu.make_async_remote_copy(
            src_ref=src,
            dst_ref=dst,
            send_sem=send.at[i, at],
            recv_sem=recv.at[i, at],
            device_id=device_id,
            device_id_type=MESH,
        )
        copy.start()
        ends.append(copy)
        return copy

    def first(i):
        op, lo, cols = pieces[i]
        lead = (slice(None),) * bits
        own = ins[op].at[(*lead, my[0], slice(None), pl.ds(lo, cols))]
        other = ins[op].at[(*lead, 1 - my[0], slice(None), pl.ds(lo, cols))]
        load = pltpu.make_async_copy(own, scratch[i][0], load_sem.at[i])
        load.start()
        waits[i] = (load, push(i, 0, other, scratch[i][1], {"fsdp": flip(f, 0)}))

    def arrive(i, s):
        acc = scratch[i][2]
        if s == 0:
            waits[i][0].wait()
            waits[i][1].wait_recv()
            acc[...] = scratch[i][0][...].astype(f32) + scratch[i][1][...].astype(f32)
        else:
            waits[i].wait_recv()
            here = region(i)
            acc[here] = acc[here] + scratch[i][5 + 2 * s][...].astype(f32)

    def middle(i, s):
        arrive(i, s - 1)
        b = (upper if i % 2 == 0 else upper[::-1])[s - 1]
        out_buf, in_buf = scratch[i][4 + 2 * s], scratch[i][5 + 2 * s]
        out_buf[...] = scratch[i][2][region(i, b)].astype(out_buf.dtype)
        waits[i] = push(i, s, out_buf, in_buf, {"fsdp": flip(f, b)})
        fixed[i][b] = my[b]

    def last(i):
        arrive(i, bits - 1)
        out_buf, in_buf = scratch[i][3], scratch[i][4]
        waits[i] = []
        for o in near_first(dp_count)[1:]:
            peer = lax.rem(d + o, dp_count)
            out_buf[o - 1] = scratch[i][2][(peer, *region(i)[1:])].astype(out_buf.dtype)
            waits[i].append(
                push(i, bits - 1 + o, out_buf.at[o - 1], in_buf.at[o - 1], {"dp": peer})
            )

    def finish(i):
        op, lo, cols = pieces[i]
        for copy in waits[i]:
            copy.wait_recv()
        total = scratch[i][2][(d, *region(i)[1:])]
        for o in range(1, dp_count):
            total = total + scratch[i][4][o - 1].astype(f32)
        scratch[i][5][...] = total
        store = pltpu.make_async_copy(
            scratch[i][5], outs[op].at[:, pl.ds(lo, cols)], store_sem.at[i]
        )
        store.start()
        return store

    stores = []
    for t in range((n + 1) // 2 + bits + 1):
        for i in range(n):
            s = t - i // 2
            if s == 0:
                first(i)
            elif 1 <= s < bits:
                middle(i, s)
            elif s == bits:
                last(i)
            elif s == bits + 1:
                stores.append(finish(i))
    for copy in ends:
        copy.wait_send()
    for store in stores:
        store.wait()


def scatter_all(arrays, splits, collective_id):
    dp_count, fsdp_count = lax.axis_size("dp"), lax.axis_size("fsdp")
    bits = fsdp_count.bit_length() - 1
    arrays = [a.reshape(dp_count, *(2,) * bits, *a.shape[1:]) for a in arrays]
    pieces, scratch = [], []
    for op, (a, k) in enumerate(zip(arrays, splits)):
        rows, cols = a.shape[-2], a.shape[-1] // k
        half = (dp_count, *(2,) * (bits - 1), rows, cols)
        for j in range(k):
            pieces.append((op, j * cols, cols))
            scratch += [pltpu.VMEM(half, a.dtype)] * 2 + [pltpu.VMEM(half, f32)]
            scratch += [pltpu.VMEM((dp_count - 1, rows, cols), a.dtype)] * 2
            scratch += [pltpu.VMEM((rows, cols), f32)]
            for s in range(1, bits):
                shape = (dp_count, *(2,) * (bits - 1 - s), rows, cols)
                scratch += [pltpu.VMEM(shape, a.dtype)] * 2
    n, steps = len(pieces), bits - 1 + dp_count
    return pl.pallas_call(
        functools.partial(scatter_body, dp_count, bits, pieces, [a.dtype for a in arrays]),
        out_shape=[jax.ShapeDtypeStruct(a.shape[-2:], f32) for a in arrays],
        in_specs=[ANY] * len(arrays),
        out_specs=[ANY] * len(arrays),
        scratch_shapes=scratch
        + [
            pltpu.SemaphoreType.DMA((n,)),
            pltpu.SemaphoreType.DMA((n, steps)),
            pltpu.SemaphoreType.DMA((n, steps)),
            pltpu.SemaphoreType.DMA((n,)),
        ],
        compiler_params=pltpu.CompilerParams(
            collective_id=collective_id, has_side_effects=True, vmem_limit_bytes=60 << 20
        ),
    )(*arrays)


def exchange(values):
    return lax.all_to_all(values, "dp", split_axis=0, concat_axis=0, tiled=True)


def params(limit_mib=60):
    return pltpu.CompilerParams(vmem_limit_bytes=limit_mib << 20)


def whole(shape):
    return pl.BlockSpec(shape, lambda i: (0,) * len(shape), pipeline_mode=pl.Buffered(1))


def matmul(left, right):
    return jnp.dot(left, right, preferred_element_type=f32)


def rows_inner(left, right):
    return lax.dot_general(left, right, (((0,), (0,)), ((), ())), preferred_element_type=f32)


def cols_inner(left, right):
    return lax.dot_general(left, right, (((1,), (1,)), ((), ())), preferred_element_type=f32)


def gelu_and_slope(values):
    phi = 0.5 * (1.0 + lax.erf(values * 0.7071067811865476))
    return (
        values * phi,
        phi + values * jnp.exp(-0.5 * values * values) * 0.3989422804014327,
    )


def centred_rows(tokens_ref, rows):
    inputs = tokens_ref[...].reshape(rows, tokens_ref.shape[-1]).astype(f32)
    centred = inputs - jnp.mean(inputs, axis=1, keepdims=True)
    variance = jnp.mean(centred * centred, axis=1, keepdims=True)
    return inputs, centred, lax.rsqrt(variance + epsilon)


def channels_from_rows(ref, values, seqs, chunk, own):
    for place in range(ref.shape[0]):
        for s in range(seqs):
            ref[place, :, s * own : (s + 1) * own] = values[
                s * chunk : (s + 1) * chunk, place * own : (place + 1) * own
            ].astype(ref.dtype)


def rows_from_channels(ref, scratch, seqs, chunk, own):
    for place in range(ref.shape[0]):
        for s in range(seqs):
            scratch[s * chunk : (s + 1) * chunk, place * own : (place + 1) * own] = ref[
                place, :, s * own : (s + 1) * own
            ]


def reduce_body(dims, tokens_ref, gain_ref, bias_ref, weight_ref, normed_ref, out_ref, slope_ref):
    seqs, chunk, own = dims
    _, centred, inverse_std = centred_rows(tokens_ref, seqs * chunk)
    normed = (centred * inverse_std * gain_ref[...] + bias_ref[...]).astype(bf16)
    normed_ref[...] = normed
    reduced, slope = gelu_and_slope(matmul(normed, weight_ref[...]))
    slope_ref[...] = slope
    channels_from_rows(out_ref, reduced, seqs, chunk, own)


def gate_body(tile, normed_ref, weight_ref, gate_ref, slope_ref):
    for j in range(gate_ref.shape[1] // tile):
        at = slice(j * tile, (j + 1) * tile)
        gate, slope = gelu_and_slope(matmul(normed_ref[...], weight_ref[:, at]))
        gate_ref[:, at] = gate.astype(bf16)
        slope_ref[:, at] = slope.astype(bf16)


def middle_body(
    dims, teachers, tile, order_ref, scale_ref, state_ref, gate_ref, slope_ref, expand_ref, weight_ref,
    tokens_ref, cotangent_ref, valid_ref, keep_ref, *refs,
):
    seqs, chunk, own = dims
    teach_refs, refs = refs[:teachers], refs[teachers:]
    (state_out_ref, product_ref, branch_grad_ref, expanded_grad_ref, gate_grad_ref, out_ref,
     full_grad_ref, error_ref, mixed_grad_ref, expanded_ref) = refs
    rows, width = seqs * chunk, tokens_ref.shape[-1]
    rows_from_channels(state_ref, state_out_ref, seqs, chunk, own)
    state_out = state_out_ref[...]
    tiles = [slice(j * tile, (j + 1) * tile) for j in range(gate_ref.shape[1] // tile)]
    branch = jnp.zeros((rows, width), f32)
    for at in tiles:
        expanded = matmul(state_out, expand_ref[:, at])
        expanded_ref[:, at] = expanded
        product = (expanded * gate_ref[:, at].astype(f32)).astype(bf16)
        product_ref[:, at] = product
        branch = branch + matmul(product, weight_ref[at, :])
    valid, keep = valid_ref[...], keep_ref[...]
    full = tokens_ref[...].reshape(rows, width).astype(f32) + valid * branch
    out_ref[...] = full.astype(bf16).reshape(out_ref.shape)
    errors = full - jnp.concatenate([t[0] for t in teach_refs], axis=0).astype(f32)
    error_ref[0] = jnp.sum((keep * errors * errors).reshape(rows // 8, 8, width), axis=0)
    full_grad = cotangent_ref[...].reshape(rows, width).astype(f32) + keep * errors * scale_ref[0]
    full_grad_ref[...] = full_grad
    branch_grad = (valid * full_grad).astype(bf16)
    branch_grad_ref[...] = branch_grad
    mixed_grad = jnp.zeros((rows, state_out.shape[1]), f32)
    for at in tiles:
        product_grad = cols_inner(branch_grad, weight_ref[at, :])
        expanded_grad = (product_grad * gate_ref[:, at].astype(f32)).astype(bf16)
        expanded_grad_ref[:, at] = expanded_grad
        gate_grad_ref[:, at] = (
            product_grad * expanded_ref[:, at] * slope_ref[:, at].astype(f32)
        ).astype(bf16)
        mixed_grad = mixed_grad + cols_inner(expanded_grad, expand_ref[:, at])
    channels_from_rows(mixed_grad_ref, mixed_grad, seqs, chunk, own)


def input_body(
    dims, back_ref, slope_ref, gate_grad_ref, gate_weight_ref, reduce_weight_ref, tokens_ref,
    gain_ref, full_grad_ref, out_ref, reduced_grad_ref, gain_grad_ref, bias_grad_ref, back_rows_ref,
):
    seqs, chunk, own = dims
    rows, width = seqs * chunk, tokens_ref.shape[-1]
    rows_from_channels(back_ref, back_rows_ref, seqs, chunk, own)
    reduced_grad = (back_rows_ref[...].astype(f32) * slope_ref[...]).astype(bf16)
    reduced_grad_ref[...] = reduced_grad
    normed_grad = cols_inner(gate_grad_ref[...], gate_weight_ref[...]) + cols_inner(
        reduced_grad, reduce_weight_ref[...]
    )
    _, centred, inverse_std = centred_rows(tokens_ref, rows)
    unit = centred * inverse_std
    gain_grad_ref[0] = jnp.sum((normed_grad * unit).reshape(rows // 8, 8, width), axis=0)
    bias_grad_ref[0] = jnp.sum(normed_grad.reshape(rows // 8, 8, width), axis=0)
    unit_grad = normed_grad * gain_ref[...]
    result = full_grad_ref[...] + inverse_std * (
        unit_grad
        - jnp.mean(unit_grad, axis=1, keepdims=True)
        - unit * jnp.mean(unit_grad * unit, axis=1, keepdims=True)
    )
    out_ref[...] = result.astype(bf16).reshape(out_ref.shape)


def weight_grad_body(n, *refs):
    lefts, rights, out_ref = refs[:n], refs[n : 2 * n], refs[2 * n]
    total = rows_inner(lefts[0][...], rights[0][...])
    for left, right in zip(lefts[1:], rights[1:]):
        total = total + rows_inner(left[...], right[...])
    out_ref[...] = total.astype(out_ref.dtype)


def weight_grad(lefts, rights, row_tile):
    n, (rows, height), width = len(lefts), lefts[0].shape, rights[0].shape[1]
    return pl.pallas_call(
        functools.partial(weight_grad_body, n),
        grid=(height // row_tile,),
        out_shape=jax.ShapeDtypeStruct((height, width), bf16),
        in_specs=[pl.BlockSpec((rows, row_tile), lambda i: (0, i))] * n + [whole((rows, width))] * n,
        out_specs=pl.BlockSpec((row_tile, width), lambda i: (i, 0)),
        compiler_params=params(),
        cost_estimate=pl.CostEstimate(
            flops=2 * n * rows * height * width,
            bytes_accessed=2 * (n * rows * (height + width) + height * width),
            transcendentals=0,
        ),
    )(*lefts, *rights)


def fourier_table(chunk):
    freq = np.arange(chunk)[:, None]
    time = np.arange(chunk)[None, :]
    angle = (freq * time % (2 * chunk)) * (np.pi / chunk)
    sines = -np.sin(angle)
    sines[0] = 1.0 - 2.0 * (np.arange(chunk) % 2)
    table = np.concatenate([np.cos(angle), sines], axis=0)
    scaling = np.full((2 * chunk, 1), 1.0 / chunk)
    scaling[0] = scaling[chunk] = 0.5 / chunk
    sign = np.tile(1.0 - 2.0 * (np.arange(chunk) % 2), 2)
    sign[chunk] = 1.0 - 2.0 * (chunk % 2)
    return table.astype(np.float32), (table * scaling).astype(np.float32), sign.astype(np.float32)


def high_and_low(table):
    high = table.astype(jnp.bfloat16)
    return np.stack([high, (table - high.astype(np.float32)).astype(jnp.bfloat16)])


def spectrum(table_ref, values):
    return matmul(table_ref[0], values) + matmul(table_ref[1], values)


def to_time(inverse_ref, spec):
    high = spec.astype(bf16)
    low = (spec - high.astype(f32)).astype(bf16)
    return (
        rows_inner(inverse_ref[0], high)
        + rows_inner(inverse_ref[1], high)
        + rows_inner(inverse_ref[0], low)
    )


def packed_product(first, second, edge, conjugate):
    (a_re, a_im), (b_re, b_im) = first, second
    straight, crossed = a_re * b_re, a_im * b_im
    if conjugate:
        real = straight + jnp.where(edge, 0.0, crossed)
        imag = jnp.where(edge, crossed, a_re * b_im - a_im * b_re)
    else:
        real = straight - jnp.where(edge, 0.0, crossed)
        imag = jnp.where(edge, crossed, a_re * b_im + a_im * b_re)
    return real, imag


def pair_sum(pairs, edge, conjugate):
    real, imag = packed_product(*pairs[0], edge, conjugate)
    for first, second in pairs[1:]:
        more = packed_product(first, second, edge, conjugate)
        real, imag = real + more[0], imag + more[1]
    return real, imag


def halves(ref, block, at, chunk):
    return ref[block, :chunk, at], ref[block, chunk:, at]


def convolve_body(table_ref, inverse_ref, kernel_ref, rows_ref, out_ref, spec_ref, back_ref):
    blocks, chunk, columns = rows_ref.shape
    lanes = kernel_ref.shape[2]
    edge = lax.broadcasted_iota(jnp.int32, (chunk, lanes), 0) == 0
    for c in range(blocks):
        spec_ref[c] = spectrum(table_ref, rows_ref[c])
        for g in range(columns // lanes):
            at = slice(g * lanes, (g + 1) * lanes)
            everything = slice(None)
            real, imag = pair_sum(
                [
                    (halves(kernel_ref, k, everything, chunk), halves(spec_ref, c - k, at, chunk))
                    for k in range(c + 1)
                ],
                edge,
                False,
            )
            back_ref[:chunk, at], back_ref[chunk:, at] = real, imag
        out_ref[c] = to_time(inverse_ref, back_ref[...]).astype(out_ref.dtype)


def convolve_back_body(
    table_ref, inverse_ref, kernel_ref, rows_ref, grad_ref, out_ref, kernel_grad_ref,
    spec_ref, grad_spec_ref, back_ref,
):
    blocks, chunk, columns = rows_ref.shape
    lanes = kernel_ref.shape[2]
    edge = lax.broadcasted_iota(jnp.int32, (chunk, lanes), 0) == 0
    everything = slice(None)
    groups = [slice(g * lanes, (g + 1) * lanes) for g in range(columns // lanes)]
    for c in range(blocks):
        spec_ref[c] = spectrum(table_ref, rows_ref[c])
    for c in reversed(range(blocks)):
        grad_spec_ref[c] = spectrum(table_ref, grad_ref[c])
        for at in groups:
            real, imag = pair_sum(
                [
                    (
                        halves(kernel_ref, late - c, everything, chunk),
                        halves(grad_spec_ref, late, at, chunk),
                    )
                    for late in range(c, blocks)
                ],
                edge,
                True,
            )
            back_ref[:chunk, at], back_ref[chunk:, at] = real, imag
        out_ref[c] = to_time(inverse_ref, back_ref[...]).astype(out_ref.dtype)
    for k in range(blocks):
        real, imag = pair_sum(
            [
                (halves(spec_ref, c - k, at, chunk), halves(grad_spec_ref, c, at, chunk))
                for c in range(k, blocks)
                for at in groups
            ],
            edge,
            True,
        )
        kernel_grad_ref[k, :chunk], kernel_grad_ref[k, chunk:] = real, imag


def kernel_factors(decay, frequency, log_step, length):
    fine = 32
    coarse = length // fine
    step_size = jnp.exp(log_step)[:, None]
    real = (step_size * decay)[:, None, :]
    imag = (step_size * frequency)[:, None, :]
    far = (jnp.arange(coarse, dtype=jnp.int32) * fine).astype(f32)[None, :, None]
    near = jnp.arange(fine, dtype=jnp.int32).astype(f32)[None, :, None]
    far_damp, near_damp = jnp.exp(real * far), jnp.exp(real * near)
    return (
        (far_damp * jnp.cos(imag * far), far_damp * jnp.sin(imag * far)),
        (near_damp * jnp.cos(imag * near), near_damp * jnp.sin(imag * near)),
        step_size,
    )


def kernel_forward(weight_pair, factors):
    (far_re, far_im), (near_re, near_im), _ = factors
    w_re, w_im = weight_pair[0][:, None, :], weight_pair[1][:, None, :]
    left = jnp.concatenate([far_re, -far_im], axis=2)
    right = jnp.concatenate(
        [w_re * near_re - w_im * near_im, w_re * near_im + w_im * near_re], axis=2
    )
    rows = jnp.einsum("han,hbn->hab", left, right, precision=highest)
    return rows.reshape(rows.shape[0], -1)


def kernel_backward(grad_rows, weight_pair, decay, frequency, factors):
    (far_re, far_im), (near_re, near_im), step_size = factors
    channels, coarse, states = far_re.shape
    fine = near_re.shape[1]
    tiles = grad_rows.reshape(channels, coarse, fine)
    near_index = jnp.arange(fine, dtype=jnp.int32).astype(f32)
    far_index = (jnp.arange(coarse, dtype=jnp.int32) * fine).astype(f32)[None, :, None]
    stacked = jnp.concatenate([tiles, tiles * near_index], axis=1)
    part = jnp.einsum(
        "hab,hbn->han", stacked, jnp.concatenate([near_re, near_im], axis=2), precision=highest
    )
    u_re, u_im = part[:, :coarse, :states], part[:, :coarse, states:]
    v_re = part[:, coarse:, :states] + far_index * u_re
    v_im = part[:, coarse:, states:] + far_index * u_im
    s_re = jnp.sum(far_re * u_re - far_im * u_im, axis=1)
    s_im = jnp.sum(far_re * u_im + far_im * u_re, axis=1)
    t_re = jnp.sum(far_re * v_re - far_im * v_im, axis=1)
    t_im = jnp.sum(far_re * v_im + far_im * v_re, axis=1)
    w_re, w_im = weight_pair[0], weight_pair[1]
    along_re = step_size * (w_re * t_re - w_im * t_im)
    along_im = -step_size * (w_re * t_im + w_im * t_re)
    return (
        jnp.stack([s_re, -s_im]),
        along_re,
        along_im,
        jnp.sum(decay * along_re + frequency * along_im, axis=1),
    )


def shards(
    tokens,
    cotangent,
    teacher,
    lengths,
    dealing,
    loss_mask,
    norm_gain,
    norm_bias,
    gate_weight,
    reduce_weight,
    state_weight,
    decay_rate,
    frequency,
    log_step,
    expand_weight,
    out_weight,
):
    dp_count, fsdp_count = lax.axis_size("dp"), lax.axis_size("fsdp")
    devices = dp_count * fsdp_count
    group_index = lax.axis_index("fsdp")
    dp_place = lax.axis_index("dp")
    micro_count, seqs, chunk, width = tokens.shape
    rows = seqs * chunk
    seq_length = chunk * dp_count
    gate_width = gate_weight.shape[1]
    reduced_width = reduce_weight.shape[1]
    own = reduced_width // dp_count
    lanes = max(own, 128)
    share = norm_gain.shape[0]
    micros = range(micro_count)
    direct = own % 128 == 0

    small = jnp.zeros((16, 256), bf16).at[0, :share].set(norm_gain).at[1, :share].set(norm_bias)
    first, small = gather_all([jnp.concatenate([gate_weight, reduce_weight], axis=1), small], 1)
    first = first.reshape(width, gate_width + reduced_width)
    gain_row = small[:, :, 0, :share].reshape(1, width).astype(f32)
    bias_row = small[:, :, 1, :share].reshape(1, width).astype(f32)

    per_block = max(1, 512 // chunk)
    steps = seqs // per_block
    middle_block = max(1, 256 // chunk)
    middle_steps = seqs // middle_block

    def sequence_spec(count):
        return pl.BlockSpec((count, chunk, width), lambda i, *_: (i, 0, 0))

    def row_spec(columns, count=per_block):
        return pl.BlockSpec((count * chunk, columns), lambda i, *_: (i, 0))

    def shared(shape, block):
        return pl.BlockSpec(shape, lambda i, *_: block, pipeline_mode=pl.Buffered(1))

    lane_shape = (dp_count, chunk, seqs * own)
    if not direct:
        lane_shape = (1, rows, reduced_width)

    def dims(count):
        return (count, chunk, own) if direct else (1, count * chunk, reduced_width)

    def lane_spec(count):
        if direct:
            return pl.BlockSpec((dp_count, chunk, count * own), lambda i, *_: (0, 0, i))
        return pl.BlockSpec((1, count * chunk, reduced_width), lambda i, *_: (0, i, 0))

    def tokens_spec(m, count):
        return pl.BlockSpec((None, count, chunk, width), lambda i, *_: (m, i, 0, 0))

    def send_lanes(values):
        if not direct:
            values = values.reshape(seqs, chunk, dp_count, own).transpose(2, 1, 0, 3)
            values = values.reshape(dp_count, chunk, seqs * own)
        return exchange(values)

    def receive_lanes(values):
        values = exchange(values)
        if not direct:
            values = values.reshape(dp_count, chunk, seqs, own).transpose(2, 1, 0, 3)
            values = values.reshape(1, rows, reduced_width)
        return values

    def reduce_rows(m):
        return pl.pallas_call(
            functools.partial(reduce_body, dims(per_block)),
            grid=(steps,),
            out_shape=[
                jax.ShapeDtypeStruct((rows, width), bf16),
                jax.ShapeDtypeStruct(lane_shape, bf16),
                jax.ShapeDtypeStruct((rows, reduced_width), f32),
            ],
            in_specs=[
                tokens_spec(m, per_block),
                whole((1, width)),
                whole((1, width)),
                shared((width, reduced_width), (0, gate_width // reduced_width)),
            ],
            out_specs=[row_spec(width), lane_spec(per_block), row_spec(reduced_width)],
            compiler_params=params(),
            cost_estimate=pl.CostEstimate(
                flops=2 * rows * width * reduced_width,
                bytes_accessed=8 * rows * width,
                transcendentals=2 * rows * reduced_width,
            ),
        )(tokens, gain_row, bias_row, first)

    def gate_rows(normed):
        return pl.pallas_call(
            functools.partial(gate_body, 512),
            grid=(steps,),
            out_shape=[jax.ShapeDtypeStruct((rows, gate_width), bf16)] * 2,
            in_specs=[row_spec(width), shared((width, gate_width), (0, 0))],
            out_specs=[row_spec(gate_width)] * 2,
            compiler_params=params(),
            cost_estimate=pl.CostEstimate(
                flops=2 * rows * width * gate_width,
                bytes_accessed=4 * rows * gate_width + 2 * width * gate_width,
                transcendentals=2 * rows * gate_width,
            ),
        )(normed, first)

    normed, lanes_out, slope_reduced = zip(*[reduce_rows(m) for m in micros])
    lanes_in = [send_lanes(x) for x in lanes_out]

    teach = [
        exchange(teacher[m].reshape(dp_count, chunk, width)) for m in micros
    ]
    masked = lax.all_to_all(
        loss_mask.reshape(micro_count, dp_count, chunk), "dp", split_axis=1, concat_axis=1, tiled=True
    )
    local_ids = group_index * seqs + jnp.arange(seqs, dtype=jnp.int32)
    targets = jnp.take(dealing, local_ids, axis=1)
    own_lengths = jnp.take(lengths, local_ids, axis=1)
    positions = dp_place * chunk + jnp.arange(chunk, dtype=jnp.int32)
    valid = (positions[None, None, :] < own_lengths[:, :, None]).astype(f32)
    keep = jnp.take_along_axis(masked, targets[:, :, None], axis=1).astype(f32) * valid
    own_count = jnp.sum(keep)
    valid = valid.reshape(micro_count, rows, 1)
    keep = keep.reshape(micro_count, rows, 1)

    w_expand, w_out, counts = gather_all(
        [expand_weight, out_weight, jnp.full((8, 256), own_count, f32)], 2
    )
    w_expand = w_expand.reshape(reduced_width, gate_width)
    w_out = w_out.reshape(gate_width, width)
    count = jnp.sum(counts[:, :, 0, 0])
    error_scale = (2.0 / (width * count)).reshape(1)

    table_np, inverse_np, sign_np = fourier_table(chunk)
    sign = jnp.asarray(sign_np)[:, None]
    table2, inverse2 = jnp.asarray(high_and_low(table_np)), jnp.asarray(high_and_low(inverse_np))
    factors = kernel_factors(decay_rate, frequency, log_step, seq_length)
    own_kernel = kernel_forward(state_weight, factors)
    kernel = lax.all_gather(own_kernel, "fsdp", axis=0, tiled=True)
    segments = jnp.einsum(
        "kt,hct->ckh", jnp.asarray(table_np), kernel.reshape(own, dp_count, chunk), precision=highest
    )
    previous = jnp.concatenate([jnp.zeros_like(segments[:1]), segments[:-1]], axis=0)
    kernel_spec = jnp.tile(segments + sign * previous, (1, 1, lanes // own))

    blocks = (dp_count, chunk, seqs * own)
    spec_scratch = pltpu.VMEM((dp_count, 2 * chunk, seqs * own), f32)
    back_scratch = pltpu.VMEM((2 * chunk, seqs * own), f32)
    transform_flops = 8 * chunk * chunk * dp_count * seqs * own

    def convolve(values):
        return pl.pallas_call(
            convolve_body,
            out_shape=jax.ShapeDtypeStruct(blocks, bf16),
            scratch_shapes=[spec_scratch, back_scratch],
            compiler_params=params(),
            cost_estimate=pl.CostEstimate(
                flops=5 * transform_flops // 2, bytes_accessed=8 << 20, transcendentals=0
            ),
        )(table2, inverse2, kernel_spec, values)

    def convolve_back(values, grads):
        return pl.pallas_call(
            convolve_back_body,
            out_shape=[
                jax.ShapeDtypeStruct(blocks, bf16),
                jax.ShapeDtypeStruct((dp_count, 2 * chunk, lanes), f32),
            ],
            scratch_shapes=[spec_scratch, spec_scratch, back_scratch],
            compiler_params=params(),
            cost_estimate=pl.CostEstimate(
                flops=7 * transform_flops // 2, bytes_accessed=8 << 20, transcendentals=0
            ),
        )(table2, inverse2, kernel_spec, values, grads)

    mixed = [receive_lanes(convolve(x)) for x in lanes_in]
    gates = [gate_rows(x) for x in normed]

    def middle_rows(m):
        teach_specs = [
            pl.BlockSpec((1, chunk, width), functools.partial(teach_block, s)) for s in range(middle_block)
        ]
        wide, narrow = row_spec(gate_width, middle_block), row_spec(width, middle_block)
        return pl.pallas_call(
            functools.partial(middle_body, dims(middle_block), middle_block, 768),
            grid_spec=pltpu.PrefetchScalarGridSpec(
                num_scalar_prefetch=2,
                grid=(middle_steps,),
                in_specs=[
                    lane_spec(middle_block),
                    wide,
                    wide,
                    shared((reduced_width, gate_width), (0, 0)),
                    shared((gate_width, width), (0, 0)),
                    tokens_spec(m, middle_block),
                    tokens_spec(m, middle_block),
                    row_spec(1, middle_block),
                    row_spec(1, middle_block),
                    *teach_specs,
                ],
                out_specs=[
                    row_spec(reduced_width, middle_block),
                    wide,
                    narrow,
                    wide,
                    wide,
                    sequence_spec(middle_block),
                    narrow,
                    pl.BlockSpec((1, 8, width), lambda i, *_: (i, 0, 0)),
                    lane_spec(middle_block),
                ],
                scratch_shapes=[pltpu.VMEM((middle_block * chunk, gate_width), f32)],
            ),
            out_shape=[
                jax.ShapeDtypeStruct((rows, reduced_width), bf16),
                jax.ShapeDtypeStruct((rows, gate_width), bf16),
                jax.ShapeDtypeStruct((rows, width), bf16),
                jax.ShapeDtypeStruct((rows, gate_width), bf16),
                jax.ShapeDtypeStruct((rows, gate_width), bf16),
                jax.ShapeDtypeStruct((seqs, chunk, width), bf16),
                jax.ShapeDtypeStruct((rows, width), f32),
                jax.ShapeDtypeStruct((middle_steps, 8, width), f32),
                jax.ShapeDtypeStruct(lane_shape, bf16),
            ],
            compiler_params=params(),
            cost_estimate=pl.CostEstimate(
                flops=4 * rows * gate_width * (width + reduced_width),
                bytes_accessed=10 * rows * gate_width + 16 * rows * width,
                transcendentals=0,
            ),
        )(
            targets[m], error_scale, mixed[m], *gates[m], w_expand, w_out, tokens, cotangent,
            valid[m], keep[m], *[teach[m]] * middle_block,
        )

    def teach_block(s, i, order, scale):
        return (order[i * middle_block + s], 0, 0)

    def input_rows(m, back, gate_grad, full_grad):
        eight = pl.BlockSpec((1, 8, width), lambda i, *_: (i, 0, 0))
        return pl.pallas_call(
            functools.partial(input_body, dims(per_block)),
            grid=(steps,),
            in_specs=[
                lane_spec(per_block),
                row_spec(reduced_width),
                row_spec(gate_width),
                shared((width, gate_width), (0, 0)),
                shared((width, reduced_width), (0, gate_width // reduced_width)),
                tokens_spec(m, per_block),
                whole((1, width)),
                row_spec(width),
            ],
            out_specs=[sequence_spec(per_block), row_spec(reduced_width), eight, eight],
            out_shape=[
                jax.ShapeDtypeStruct((seqs, chunk, width), bf16),
                jax.ShapeDtypeStruct((rows, reduced_width), bf16),
                jax.ShapeDtypeStruct((steps, 8, width), f32),
                jax.ShapeDtypeStruct((steps, 8, width), f32),
            ],
            scratch_shapes=[pltpu.VMEM((per_block * chunk, reduced_width), bf16)],
            compiler_params=params(),
            cost_estimate=pl.CostEstimate(
                flops=2 * rows * width * (gate_width + reduced_width),
                bytes_accessed=4 * rows * gate_width + 8 * rows * width,
                transcendentals=0,
            ),
        )(back, slope_reduced[m], gate_grad, first, first, tokens, gain_row, full_grad)

    middle = [middle_rows(m) for m in micros]
    state_out, product, branch_grad, expanded_grad, gate_grad, outputs, full_grad, error_rows, lane_grad = zip(*middle)
    grads_in = [send_lanes(x) for x in lane_grad]
    back, kernel_grads = zip(*[convolve_back(lanes_in[m], grads_in[m]) for m in micros])
    back = [receive_lanes(x) for x in back]
    out_grad = weight_grad(product, branch_grad, 512)
    expand_grad = weight_grad(state_out, expanded_grad, 256)
    gate_weight_grad = weight_grad(normed, gate_grad, 256)
    ends = [input_rows(m, back[m], gate_grad[m], full_grad[m]) for m in micros]
    returned, reduced_grad, gain_rows, bias_rows = zip(*ends)
    reduce_grad = weight_grad(normed, reduced_grad, 512)

    kernel_total = sum(kernel_grads)
    if not direct:
        kernel_total = kernel_total.reshape(dp_count, 2 * chunk, lanes // own, own).sum(axis=2)
    following = jnp.concatenate([kernel_total[1:], jnp.zeros_like(kernel_total[:1])], axis=0)
    kernel_grad = jnp.einsum(
        "kt,ckh->hct", jnp.asarray(inverse_np), kernel_total + sign * following, precision=highest
    ).reshape(own, seq_length)
    kernel_grad = lax.psum_scatter(kernel_grad, "fsdp", scatter_dimension=0, tiled=True)
    pair_grad, decay_grad, frequency_grad, step_grad = kernel_backward(
        kernel_grad, state_weight, decay_rate, frequency, factors
    )

    gain_total = jnp.sum(sum(gain_rows), axis=(0, 1)).reshape(devices, 1, share)
    bias_total = jnp.sum(sum(bias_rows), axis=(0, 1)).reshape(devices, 1, share)
    error_total = jnp.full((devices, 1, share), jnp.sum(sum(error_rows)))
    sums = jnp.concatenate([gain_total, bias_total, error_total], axis=1)
    sums = jnp.pad(sums, ((0, 0), (0, 5), (0, 128 - share)))
    out_sum, expand_sum, gate_sum, reduce_sum, sums = scatter_all(
        [
            out_grad.reshape(devices, -1, width),
            expand_grad.reshape(devices, -1, gate_width),
            gate_weight_grad.reshape(devices, -1, gate_width),
            reduce_grad.reshape(devices, -1, reduced_width),
            sums,
        ],
        [4, 2, 4, 1, 1],
        3,
    )
    loss_value = sums[2, 0] / (width * count)
    return (
        jnp.stack(outputs),
        loss_value,
        jnp.stack(returned),
        sums[0, :share],
        sums[1, :share],
        gate_sum,
        reduce_sum,
        pair_grad,
        decay_grad,
        frequency_grad,
        step_grad,
        expand_sum,
        out_sum,
    )


def solution(mesh):
    in_specs = (
        P(None, "fsdp", "dp", None),
        P(None, "fsdp", "dp", None),
        P(None, ("dp", "fsdp"), None, None),
        P(),
        P(),
        P(None, ("dp", "fsdp"), None),
        P(("dp", "fsdp")),
        P(("dp", "fsdp")),
        P(("dp", "fsdp"), None),
        P(("dp", "fsdp"), None),
        P(None, ("dp", "fsdp"), None),
        P(("dp", "fsdp"), None),
        P(("dp", "fsdp"), None),
        P(("dp", "fsdp")),
        P(("dp", "fsdp"), None),
        P(("dp", "fsdp"), None),
    )
    out_specs = (
        P(None, "fsdp", "dp", None),
        P(),
        P(None, "fsdp", "dp", None),
        P(("dp", "fsdp")),
        P(("dp", "fsdp")),
        P(("dp", "fsdp"), None),
        P(("dp", "fsdp"), None),
        P(None, ("dp", "fsdp"), None),
        P(("dp", "fsdp"), None),
        P(("dp", "fsdp"), None),
        P(("dp", "fsdp")),
        P(("dp", "fsdp"), None),
        P(("dp", "fsdp"), None),
    )
    return jax.shard_map(shards, mesh=mesh, in_specs=in_specs, out_specs=out_specs, check_vma=False)
```

```python
import functools

import numpy as np
import jax
import jax.numpy as jnp
from jax import lax
from jax.experimental import pallas as pl
from jax.experimental.pallas import tpu as pltpu
from jax.sharding import PartitionSpec as P

epsilon = 1e-05
highest = lax.Precision.HIGHEST
bf16 = jnp.bfloat16
f32 = jnp.float32
MESH = pl.DeviceIdType.MESH
ANY = pl.BlockSpec(memory_space=pl.ANY)


def bit_of(index, bit):
    return lax.rem(lax.div(index, 1 << bit), 2)


def flip(index, bit):
    return index + (1 << bit) - 2 * (1 << bit) * bit_of(index, bit)


def greet(dp_count, bits):
    d, f = lax.axis_index("dp"), lax.axis_index("fsdp")
    barrier = pltpu.get_barrier_semaphore()
    for o in range(1, dp_count):
        peer = lax.rem(d + o, dp_count)
        pl.semaphore_signal(barrier, inc=1, device_id={"dp": peer}, device_id_type=MESH)
    for b in range(bits):
        pl.semaphore_signal(barrier, inc=1, device_id={"fsdp": flip(f, b)}, device_id_type=MESH)
    pl.semaphore_wait(barrier, dp_count - 1 + bits)


def near_first(count):
    order = [0]
    for k in range(1, count // 2 + 1):
        order += [k] if k == count - k else [k, count - k]
    return order


def gather_body(dp_count, bits, n, n_swap, work, *refs):
    n_work_in, n_work_out, n_work_scratch = work[0] if work else (0, 0, 0)
    moved = n + n_swap
    ins, refs = refs[:moved], refs[moved:]
    work_ins, refs = refs[:n_work_in], refs[n_work_in:]
    outs, refs = refs[:moved], refs[moved:]
    work_outs, refs = refs[:n_work_out], refs[n_work_out:]
    z_send, z_recv, send, recv, own_sem, swap_send, swap_recv = refs[:7]
    begin, tick, end = work[1](work_ins, work_outs, refs[7:]) if work else (None, None, None)
    d, f = lax.axis_index("dp"), lax.axis_index("fsdp")
    cuts = []
    for x in ins[:n]:
        cut = x.shape[1] // 256 * 128
        cuts.append(((0, cut), (cut, x.shape[1] - cut)))
    order = near_first(dp_count)
    if work:
        begin()
    greet(dp_count, bits)
    own = [pltpu.make_async_copy(ins[a], outs[a].at[d, f], own_sem.at[a]) for a in range(n)]
    own += [
        pltpu.make_async_copy(ins[a].at[d], outs[a].at[d], own_sem.at[a])
        for a in range(n, n + n_swap)
    ]
    for copy in own:
        copy.start()
    started, arrived, waited = [], {}, set()

    def push(src, dst, send_sem, recv_sem, device_id):
        copy = pltpu.make_async_remote_copy(
            src_ref=src,
            dst_ref=dst,
            send_sem=send_sem,
            recv_sem=recv_sem,
            device_id=device_id,
            device_id_type=MESH,
        )
        copy.start()
        started.append(copy)
        return copy

    for o in order[1:]:
        for h in range(2):
            for a in range(n):
                lo, size = cuts[a][h]
                arrived[(o, 0, h, a)] = push(
                    ins[a].at[:, pl.ds(lo, size)],
                    outs[a].at[d, f, :, pl.ds(lo, size)],
                    z_send.at[o - 1, h, a],
                    z_recv.at[o - 1, h, a],
                    {"dp": lax.rem(d + o, dp_count)},
                )
    for copy in own:
        copy.wait()
    upper = list(range(1, bits))
    stages = [upper + [0], upper[::-1] + [0]]
    masks = [[[0]], [[0]]]
    for h in range(2):
        for s in range(bits):
            masks[h].append(masks[h][s] + [m ^ (1 << stages[h][s]) for m in masks[h][s]])
    slot, group = 0, 0
    for t in range(dp_count + bits - 1):
        for i in range(dp_count):
            s, o = t - i, order[i]
            if not 0 <= s < bits:
                continue
            if work:
                tick(group, dp_count * bits)
                group += 1
            for k in range(len(masks[0][s])):
                for h in range(2):
                    mask, b = masks[h][s][k], stages[h][s]
                    src_f = f
                    for bb in range(bits):
                        if mask >> bb & 1:
                            src_f = flip(src_f, bb)
                    for a in range(n):
                        key = (o, mask, h, a)
                        if key in arrived and key not in waited:
                            arrived[key].wait_recv()
                            waited.add(key)
                        lo, size = cuts[a][h]
                        src_d = lax.rem(d - o + dp_count, dp_count)
                        piece = outs[a].at[src_d, src_f, :, pl.ds(lo, size)]
                        arrived[(o, mask ^ (1 << b), h, a)] = push(
                            piece, piece, send.at[slot], recv.at[slot], {"fsdp": flip(f, b)}
                        )
                        slot += 1
        if t == 0:
            for o in order[1:]:
                peer = lax.rem(d + o, dp_count)
                for e in range(n_swap):
                    arrived[(o, e)] = push(
                        ins[n + e].at[peer],
                        outs[n + e].at[d],
                        swap_send.at[o - 1, e],
                        swap_recv.at[o - 1, e],
                        {"dp": peer},
                    )
    if work:
        end()
    for key, copy in arrived.items():
        if key not in waited:
            copy.wait_recv()
    for copy in started:
        copy.wait_send()


def gather_all(arrays, swaps, collective_id, work=None):
    work_in, work_out, work_scratch, work_body = work or ((), (), (), None)
    sizes = (len(work_in), len(work_out), len(work_scratch))
    dp_count, fsdp_count = lax.axis_size("dp"), lax.axis_size("fsdp")
    bits = fsdp_count.bit_length() - 1
    n, n_swap = len(arrays), len(swaps)
    slots = 2 * dp_count * (fsdp_count - 1) * n
    total = dp_count * fsdp_count * sum(x.size * x.dtype.itemsize for x in arrays)
    return pl.pallas_call(
        functools.partial(gather_body, dp_count, bits, n, n_swap, (sizes, work_body) if work else None),
        out_shape=[
            jax.ShapeDtypeStruct((dp_count, fsdp_count, *x.shape), x.dtype) for x in arrays
        ]
        + [jax.ShapeDtypeStruct(x.shape, x.dtype) for x in swaps]
        + list(work_out),
        in_specs=[ANY] * (n + n_swap + sizes[0]),
        out_specs=[ANY] * (n + n_swap + sizes[1]),
        scratch_shapes=[
            pltpu.SemaphoreType.DMA((dp_count - 1, 2, n)),
            pltpu.SemaphoreType.DMA((dp_count - 1, 2, n)),
            pltpu.SemaphoreType.DMA((slots,)),
            pltpu.SemaphoreType.DMA((slots,)),
            pltpu.SemaphoreType.DMA((n + n_swap,)),
            pltpu.SemaphoreType.DMA((dp_count - 1, max(n_swap, 1))),
            pltpu.SemaphoreType.DMA((dp_count - 1, max(n_swap, 1))),
            *work_scratch,
        ],
        compiler_params=pltpu.CompilerParams(
            collective_id=collective_id, has_side_effects=True, vmem_limit_bytes=40 << 20
        ),
        cost_estimate=pl.CostEstimate(flops=0, bytes_accessed=20 * total, transcendentals=0),
    )(*arrays, *swaps, *work_in)


def scatter_body(dp_count, bits, pieces, kinds, *refs):
    n_in, n = len(kinds), len(pieces)
    ins, outs = refs[:n_in], refs[n_in : 2 * n_in]
    per = 6 + 2 * (bits - 1)
    scratch = [refs[2 * n_in + i * per : 2 * n_in + (i + 1) * per] for i in range(n)]
    load_sem, send, recv, store_sem = refs[2 * n_in + n * per :]
    d, f = lax.axis_index("dp"), lax.axis_index("fsdp")
    my = [bit_of(f, b) for b in range(bits)]
    upper = list(range(bits - 1, 0, -1))
    waits, fixed, ends = [None] * n, [{} for _ in range(n)], []
    greet(dp_count, bits)

    def region(i, other=None):
        return (slice(None),) + tuple(
            1 - my[b] if b == other else fixed[i].get(b, slice(None)) for b in upper
        )

    def push(i, at, src, dst, device_id):
        copy = pltpu.make_async_remote_copy(
            src_ref=src,
            dst_ref=dst,
            send_sem=send.at[i, at],
            recv_sem=recv.at[i, at],
            device_id=device_id,
            device_id_type=MESH,
        )
        copy.start()
        ends.append(copy)
        return copy

    def first(i):
        op, lo, cols = pieces[i]
        lead = (slice(None),) * bits
        own = ins[op].at[(*lead, my[0], slice(None), pl.ds(lo, cols))]
        other = ins[op].at[(*lead, 1 - my[0], slice(None), pl.ds(lo, cols))]
        load = pltpu.make_async_copy(own, scratch[i][0], load_sem.at[i])
        load.start()
        waits[i] = (load, push(i, 0, other, scratch[i][1], {"fsdp": flip(f, 0)}))

    def arrive(i, s):
        acc = scratch[i][2]
        if s == 0:
            waits[i][0].wait()
            waits[i][1].wait_recv()
            acc[...] = scratch[i][0][...].astype(f32) + scratch[i][1][...].astype(f32)
        else:
            waits[i].wait_recv()
            here = region(i)
            acc[here] = acc[here] + scratch[i][5 + 2 * s][...].astype(f32)

    def middle(i, s):
        arrive(i, s - 1)
        b = (upper if i % 2 == 0 else upper[::-1])[s - 1]
        out_buf, in_buf = scratch[i][4 + 2 * s], scratch[i][5 + 2 * s]
        out_buf[...] = scratch[i][2][region(i, b)].astype(out_buf.dtype)
        waits[i] = push(i, s, out_buf, in_buf, {"fsdp": flip(f, b)})
        fixed[i][b] = my[b]

    def last(i):
        arrive(i, bits - 1)
        out_buf, in_buf = scratch[i][3], scratch[i][4]
        waits[i] = []
        for o in near_first(dp_count)[1:]:
            peer = lax.rem(d + o, dp_count)
            out_buf[o - 1] = scratch[i][2][(peer, *region(i)[1:])].astype(out_buf.dtype)
            waits[i].append(
                push(i, bits - 1 + o, out_buf.at[o - 1], in_buf.at[o - 1], {"dp": peer})
            )

    def finish(i):
        op, lo, cols = pieces[i]
        for copy in waits[i]:
            copy.wait_recv()
        total = scratch[i][2][(d, *region(i)[1:])]
        for o in range(1, dp_count):
            total = total + scratch[i][4][o - 1].astype(f32)
        scratch[i][5][...] = total
        store = pltpu.make_async_copy(
            scratch[i][5], outs[op].at[:, pl.ds(lo, cols)], store_sem.at[i]
        )
        store.start()
        return store

    stores = []
    for t in range((n + 1) // 2 + bits + 1):
        for i in range(n):
            s = t - i // 2
            if s == 0:
                first(i)
            elif 1 <= s < bits:
                middle(i, s)
            elif s == bits:
                last(i)
            elif s == bits + 1:
                stores.append(finish(i))
    for copy in ends:
        copy.wait_send()
    for store in stores:
        store.wait()


def scatter_all(arrays, splits, collective_id):
    dp_count, fsdp_count = lax.axis_size("dp"), lax.axis_size("fsdp")
    bits = fsdp_count.bit_length() - 1
    arrays = [a.reshape(dp_count, *(2,) * bits, *a.shape[1:]) for a in arrays]
    pieces, scratch = [], []
    for op, (a, k) in enumerate(zip(arrays, splits)):
        rows, cols = a.shape[-2], a.shape[-1] // k
        half = (dp_count, *(2,) * (bits - 1), rows, cols)
        for j in range(k):
            pieces.append((op, j * cols, cols))
            scratch += [pltpu.VMEM(half, a.dtype)] * 2 + [pltpu.VMEM(half, f32)]
            scratch += [pltpu.VMEM((dp_count - 1, rows, cols), a.dtype)] * 2
            scratch += [pltpu.VMEM((rows, cols), f32)]
            for s in range(1, bits):
                shape = (dp_count, *(2,) * (bits - 1 - s), rows, cols)
                scratch += [pltpu.VMEM(shape, a.dtype)] * 2
    n, steps = len(pieces), bits - 1 + dp_count
    return pl.pallas_call(
        functools.partial(scatter_body, dp_count, bits, pieces, [a.dtype for a in arrays]),
        out_shape=[jax.ShapeDtypeStruct(a.shape[-2:], f32) for a in arrays],
        in_specs=[ANY] * len(arrays),
        out_specs=[ANY] * len(arrays),
        scratch_shapes=scratch
        + [
            pltpu.SemaphoreType.DMA((n,)),
            pltpu.SemaphoreType.DMA((n, steps)),
            pltpu.SemaphoreType.DMA((n, steps)),
            pltpu.SemaphoreType.DMA((n,)),
        ],
        compiler_params=pltpu.CompilerParams(
            collective_id=collective_id, has_side_effects=True, vmem_limit_bytes=60 << 20
        ),
    )(*arrays)


def exchange(values):
    return lax.all_to_all(values, "dp", split_axis=0, concat_axis=0, tiled=True)


def params(limit_mib=60):
    return pltpu.CompilerParams(vmem_limit_bytes=limit_mib << 20)


def whole(shape):
    return pl.BlockSpec(shape, lambda i: (0,) * len(shape), pipeline_mode=pl.Buffered(1))


def matmul(left, right):
    return jnp.dot(left, right, preferred_element_type=f32)


def rows_inner(left, right):
    return lax.dot_general(left, right, (((0,), (0,)), ((), ())), preferred_element_type=f32)


def cols_inner(left, right):
    return lax.dot_general(left, right, (((1,), (1,)), ((), ())), preferred_element_type=f32)


def gelu_and_slope(values):
    phi = 0.5 * (1.0 + lax.erf(values * 0.7071067811865476))
    return (
        values * phi,
        phi + values * jnp.exp(-0.5 * values * values) * 0.3989422804014327,
    )


def centred_rows(tokens_ref, rows):
    inputs = tokens_ref[...].reshape(rows, tokens_ref.shape[-1]).astype(f32)
    centred = inputs - jnp.mean(inputs, axis=1, keepdims=True)
    variance = jnp.mean(centred * centred, axis=1, keepdims=True)
    return inputs, centred, lax.rsqrt(variance + epsilon)


def channels_from_rows(ref, values, seqs, chunk, own):
    for place in range(ref.shape[0]):
        for s in range(seqs):
            ref[place, :, s * own : (s + 1) * own] = values[
                s * chunk : (s + 1) * chunk, place * own : (place + 1) * own
            ].astype(ref.dtype)


def rows_from_channels(ref, scratch, seqs, chunk, own):
    for place in range(ref.shape[0]):
        for s in range(seqs):
            scratch[s * chunk : (s + 1) * chunk, place * own : (place + 1) * own] = ref[
                place, :, s * own : (s + 1) * own
            ]


def reduce_body(dims, tokens_ref, gain_ref, bias_ref, weight_ref, normed_ref, out_ref, slope_ref):
    seqs, chunk, own = dims
    _, centred, inverse_std = centred_rows(tokens_ref, seqs * chunk)
    normed = (centred * inverse_std * gain_ref[...] + bias_ref[...]).astype(bf16)
    normed_ref[...] = normed
    reduced, slope = gelu_and_slope(matmul(normed, weight_ref[...]))
    slope_ref[...] = slope
    channels_from_rows(out_ref, reduced, seqs, chunk, own)


def gate_work(normed, first, gate_width):
    rows, width = normed[0].shape
    micro_count, tile = len(normed), 512
    across, down = gate_width // tile, rows // tile
    count = micro_count * across * down

    def body(ins, outs, scratch):
        rows_refs, weight_ref = ins[:-1], ins[-1]
        rows_buf, weight_buf, out_buf, load_sem, store_sem = scratch
        loads = [
            pltpu.make_async_copy(rows_refs[m], rows_buf.at[pl.ds(m * rows, rows)], load_sem.at[m])
            for m in range(micro_count)
        ]
        loads.append(
            pltpu.make_async_copy(
                weight_ref.at[:, pl.ds(0, gate_width)], weight_buf, load_sem.at[micro_count]
            )
        )
        loaded = []

        def stores(k):
            at = (
                pl.ds(pl.multiple_of(lax.div(k, across) * tile, tile), tile),
                pl.ds(pl.multiple_of(lax.rem(k, across) * tile, tile), tile),
            )
            slot = lax.rem(k, 2)
            return [
                pltpu.make_async_copy(out_buf.at[slot, r], outs[r].at[at], store_sem.at[slot, r])
                for r in range(2)
            ]

        def begin():
            for copy in loads:
                copy.start()

        def step(k, carry):
            @pl.when(k >= 2)
            def _():
                for copy in stores(k - 2):
                    copy.wait()

            slot = lax.rem(k, 2)
            left = rows_buf[pl.ds(pl.multiple_of(lax.div(k, across) * tile, tile), tile), :]
            right = weight_buf[:, pl.ds(pl.multiple_of(lax.rem(k, across) * tile, tile), tile)]
            gate, slope = gelu_and_slope(matmul(left, right))
            out_buf[slot, 0] = gate.astype(bf16)
            out_buf[slot, 1] = slope.astype(bf16)
            for copy in stores(k):
                copy.start()
            return carry

        def tick(group, groups):
            if not loaded:
                for copy in loads:
                    copy.wait()
                loaded.append(True)
            lax.fori_loop(count * group // groups, count * (group + 1) // groups, step, 0)

        def end():
            for k in (count - 2, count - 1):
                for copy in stores(k):
                    copy.wait()

        return begin, tick, end

    shape = jax.ShapeDtypeStruct((micro_count * rows, gate_width), bf16)
    scratch = [
        pltpu.VMEM((micro_count * rows, width), bf16),
        pltpu.VMEM((width, gate_width), bf16),
        pltpu.VMEM((2, 2, tile, tile), bf16),
        pltpu.SemaphoreType.DMA((micro_count + 1,)),
        pltpu.SemaphoreType.DMA((2, 2)),
    ]
    return [*normed, first], [shape, shape], scratch, body


def middle_body(
    dims, teachers, tile, order_ref, scale_ref, state_ref, gate_ref, slope_ref, expand_ref, weight_ref,
    tokens_ref, cotangent_ref, weights_ref, *refs,
):
    seqs, chunk, own = dims
    teach_refs, refs = refs[:teachers], refs[teachers:]
    (state_out_ref, product_ref, branch_grad_ref, expanded_grad_ref, gate_grad_ref, out_ref,
     full_grad_ref, error_ref, mixed_grad_ref, expanded_ref) = refs[-10:]
    rows, width = seqs * chunk, tokens_ref.shape[-1]
    rows_from_channels(state_ref, state_out_ref, seqs, chunk, own)
    state_out = state_out_ref[...]
    tiles = [slice(j * tile, (j + 1) * tile) for j in range(gate_ref.shape[1] // tile)]
    branch = jnp.zeros((rows, width), f32)
    for at in tiles:
        expanded = matmul(state_out, expand_ref[:, at])
        expanded_ref[:, at] = expanded
        product = (expanded * gate_ref[:, at].astype(f32)).astype(bf16)
        product_ref[:, at] = product
        branch = branch + matmul(product, weight_ref[at, :])
    valid, keep = weights_ref[:, :1], weights_ref[:, 1:]
    full = tokens_ref[...].reshape(rows, width).astype(f32) + valid * branch
    out_ref[...] = full.astype(bf16).reshape(out_ref.shape)
    errors = full - jnp.concatenate([t[0] for t in teach_refs], axis=0).astype(f32)
    error_ref[0] = jnp.sum((keep * errors * errors).reshape(rows // 8, 8, width), axis=0)
    full_grad = cotangent_ref[...].reshape(rows, width).astype(f32) + keep * errors * scale_ref[0]
    full_grad_ref[...] = full_grad.astype(bf16)
    branch_grad = (valid * full_grad).astype(bf16)
    branch_grad_ref[...] = branch_grad
    mixed_grad = jnp.zeros((rows, state_out.shape[1]), f32)
    for at in tiles:
        product_grad = cols_inner(branch_grad, weight_ref[at, :])
        expanded_grad = (product_grad * gate_ref[:, at].astype(f32)).astype(bf16)
        expanded_grad_ref[:, at] = expanded_grad
        gate_grad_ref[:, at] = (
            product_grad * expanded_ref[:, at] * slope_ref[:, at].astype(f32)
        ).astype(bf16)
        mixed_grad = mixed_grad + cols_inner(expanded_grad, expand_ref[:, at])
    channels_from_rows(mixed_grad_ref, mixed_grad, seqs, chunk, own)


def input_body(
    dims, back_ref, slope_ref, gate_grad_ref, gate_weight_ref, reduce_weight_ref, tokens_ref,
    gain_ref, full_grad_ref, *refs,
):
    out_ref, reduced_grad_ref, gain_grad_ref, bias_grad_ref, back_rows_ref = refs[-5:]
    seqs, chunk, own = dims
    rows, width = seqs * chunk, tokens_ref.shape[-1]
    rows_from_channels(back_ref, back_rows_ref, seqs, chunk, own)
    reduced_grad = (back_rows_ref[...].astype(f32) * slope_ref[...]).astype(bf16)
    reduced_grad_ref[...] = reduced_grad
    normed_grad = cols_inner(gate_grad_ref[...], gate_weight_ref[...]) + cols_inner(
        reduced_grad, reduce_weight_ref[...]
    )
    _, centred, inverse_std = centred_rows(tokens_ref, rows)
    unit = centred * inverse_std
    gain_grad_ref[0] = jnp.sum((normed_grad * unit).reshape(rows // 8, 8, width), axis=0)
    bias_grad_ref[0] = jnp.sum(normed_grad.reshape(rows // 8, 8, width), axis=0)
    unit_grad = normed_grad * gain_ref[...]
    result = full_grad_ref[...].astype(f32) + inverse_std * (
        unit_grad
        - jnp.mean(unit_grad, axis=1, keepdims=True)
        - unit * jnp.mean(unit_grad * unit, axis=1, keepdims=True)
    )
    out_ref[...] = result.astype(bf16).reshape(out_ref.shape)


def product_scatter_body(dp_count, bits, plan, n_left, n_right, *refs):
    pieces, slots, lane, micros = plan["pieces"], plan["slots"], plan["lane"], plan["micros"]
    n = len(pieces)
    lefts, refs = refs[: n_left * micros], refs[n_left * micros :]
    rights, refs = refs[: n_right * micros], refs[n_right * micros :]
    small_ref, refs = refs[0], refs[1:]
    outs, refs = refs[: plan["outputs"]], refs[plan["outputs"] :]
    left_bufs, refs = refs[:n_left], refs[n_left:]
    right_buf, left_sem, right_sem, load_sem, send, recv, store_sem = refs[:7]
    sets = [refs[7 : 7 + 5 + 3 * (bits - 1)], refs[7 + 5 + 3 * (bits - 1) :]]
    d, f = lax.axis_index("dp"), lax.axis_index("fsdp")
    my = [bit_of(f, b) for b in range(bits)]
    upper = list(range(bits - 1, 0, -1))
    small = n - 1

    def buffers(i):
        if i == small:
            return list(sets[1])
        _, rows, groups, _ = pieces[i]
        height, slot = rows * groups, i % slots
        views = []
        for k, ref in enumerate(sets[0]):
            arriving = k in (1, 3) or (k >= 5 and (k - 5) % 3 == 2)
            lead = (slice(None),) * (len(ref.shape) - 3)
            views.append(ref.at[(i if arriving else slot, *lead, pl.ds(0, height), slice(None))])
        return views

    bufs = [buffers(i) for i in range(n)]
    orders = [upper if i % 2 == 0 else upper[::-1] for i in range(n)]
    pushed, drained, waits, stores = {}, set(), [None] * n, {}

    def push(i, at, src, dst, device_id):
        copy = pltpu.make_async_remote_copy(
            src_ref=src,
            dst_ref=dst,
            send_sem=send.at[i, at],
            recv_sem=recv.at[i, at],
            device_id=device_id,
            device_id_type=MESH,
        )
        copy.start()
        pushed[(i, at)] = copy
        return copy

    def drain(i, *ats):
        for at in ats:
            if i >= 0 and i != small and (i, at) in pushed and (i, at) not in drained:
                pushed[(i, at)].wait_send()
                drained.add((i, at))

    jobs = [(i, *job) for i in range(n) if i != small for job in pieces[i][3]]
    loads = {}

    def fetch(j):
        if j < len(jobs):
            _, _, right, lo, cols, _ = jobs[j]
            loads[j] = [
                pltpu.make_async_copy(
                    rights[right * micros + m].at[:, pl.ds(lo, cols)],
                    right_buf.at[j % 2, m, :, pl.ds(0, cols)],
                    right_sem.at[j % 2, m],
                )
                for m in range(micros)
            ]
            for copy in loads[j]:
                copy.start()

    left_waited = set()
    left_loads = [
        [
            pltpu.make_async_copy(lefts[a * micros + m], left_bufs[a].at[m], left_sem.at[a, m])
            for m in range(micros)
        ]
        for a in range(n_left)
    ]
    small_load = pltpu.make_async_copy(small_ref, sets[1][0], load_sem)
    small_load.start()
    for a in range(n_left):
        for copy in left_loads[a]:
            copy.start()
        if a < 2:
            fetch(a)
    greet(dp_count, bits)

    def make(i):
        _, rows, groups, piece_jobs = pieces[i]
        made = bufs[i][0]
        drain(i - slots, 0)
        for j, job in enumerate(jobs):
            if job[0] != i:
                continue
            _, left, right, lo, cols, at_group = job
            if left not in left_waited:
                for copy in left_loads[left]:
                    copy.wait()
                left_waited.add(left)
            for copy in loads[j]:
                copy.wait()
            height = rows << bits

            def tile(p, carry, left=left, cols=cols, at_group=at_group, j=j, height=height):
                total = None
                for m in range(left_bufs[left].shape[0]):
                    part = rows_inner(
                        left_bufs[left][m, :, pl.ds(pl.multiple_of(p * height, 128), height)],
                        right_buf[j % 2, m, :, :cols],
                    )
                    total = part if total is None else total + part
                total = total.astype(bf16)
                for g in range(cols // lane):
                    block = total[:, g * lane : (g + 1) * lane].reshape(*(2,) * bits, rows, lane)
                    lead = (slice(None),) * bits
                    made[(p, *lead, pl.ds((at_group + g) * rows, rows), slice(None))] = block
                return carry

            lax.fori_loop(0, dp_count, tile, 0)
            fetch(j + 2)

    def first(i):
        made, got = bufs[i][0], bufs[i][1]
        if i == small:
            small_load.wait()
        else:
            make(i)
        lead = (slice(None),) * bits
        waits[i] = push(i, 0, made.at[(*lead, 1 - my[0])], got, {"fsdp": flip(f, 0)})

    def held(i, s):
        waits[i].wait_recv()
        if s == 0:
            lead = (slice(None),) * bits
            return bufs[i][0].at[(*lead, my[0])], bufs[i][1]
        return bufs[i][5 + 3 * (s - 1)], bufs[i][5 + 3 * (s - 1) + 2]

    def middle(i, s):
        own, more = held(i, s - 1)
        b = orders[i][s - 1]
        left = [q for q in upper if q not in orders[i][: s - 1]]
        kept, sent, arriving = bufs[i][5 + 3 * (s - 1) : 8 + 3 * (s - 1)]

        def side(value):
            return (slice(None),) + tuple(value if q == b else slice(None) for q in left)

        drain(i - slots, s)
        theirs, mine = side(1 - my[b]), side(my[b])
        sent[...] = (own[theirs].astype(f32) + more[theirs].astype(f32)).astype(sent.dtype)
        waits[i] = push(i, s, sent, arriving, {"fsdp": flip(f, b)})
        kept[...] = own[mine].astype(f32) + more[mine].astype(f32)

    def last(i):
        own, more = held(i, bits - 1)
        to_dp, from_dp = bufs[i][2], bufs[i][3]
        drain(i - slots, *range(bits, bits + dp_count - 1))
        copies = []
        for o in near_first(dp_count)[1:]:
            peer = lax.rem(d + o, dp_count)
            to_dp[o - 1] = (own[peer] + more[peer].astype(f32)).astype(to_dp.dtype)
            copies.append(
                push(i, bits - 1 + o, to_dp.at[o - 1], from_dp.at[o - 1], {"dp": peer})
            )
        waits[i] = (copies, own, more)

    def finish(i):
        copies, own, more = waits[i]
        result, from_dp = bufs[i][4], bufs[i][3]
        for copy in copies:
            copy.wait_recv()
        for store in stores.pop(i - slots, []):
            store.wait()
        total = own[d] + more[d].astype(f32)
        for o in range(1, dp_count):
            total = total + from_dp[o - 1].astype(f32)
        result[...] = total
        out, rows, groups, piece_jobs = pieces[i]
        stores[i] = []
        if i == small:
            stores[i].append(pltpu.make_async_copy(result, outs[out], store_sem.at[i, 0]))
        else:
            lo = piece_jobs[0][2]
            for g in range(groups):
                stores[i].append(
                    pltpu.make_async_copy(
                        result.at[pl.ds(g * rows, rows)],
                        outs[out].at[:, pl.ds(lo + g * lane, lane)],
                        store_sem.at[i, g],
                    )
                )
        for store in stores[i]:
            store.start()

    for t in range((n + 1) // 2 + bits + 1):
        for i in range(n):
            s = t - i // 2
            if s == 0:
                first(i)
            elif 1 <= s < bits:
                middle(i, s)
            elif s == bits:
                last(i)
            elif s == bits + 1:
                finish(i)
    for key, copy in pushed.items():
        if key not in drained:
            copy.wait_send()
    for group in stores.values():
        for store in group:
            store.wait()


def product_scatter(lefts, rights, small, collective_id):
    dp_count, fsdp_count = lax.axis_size("dp"), lax.axis_size("fsdp")
    bits = fsdp_count.bit_length() - 1
    devices = dp_count * fsdp_count
    lane, slots, height = 256, 4, 96
    unique = []
    for left in lefts:
        if not any(left is u for u in unique):
            unique.append(left)
    pieces = []
    for k, (left, right) in enumerate(zip(lefts, rights)):
        at = next(a for a, u in enumerate(unique) if u is left)
        rows, width = left[0].shape[1] // devices, right[0].shape[1]
        per_piece = min(height // rows, width // lane)
        for lo in range(0, width, per_piece * lane):
            groups = min(per_piece, (width - lo) // lane)
            jobs = [
                (at, k, lo + g * lane, min(3, groups - g) * lane, g) for g in range(0, groups, 3)
            ]
            pieces.append((k, rows, groups, jobs))
    pieces.append((len(lefts), small.shape[1], 1, []))
    n = len(pieces)
    plan = {
        "pieces": pieces,
        "slots": slots,
        "lane": lane,
        "outputs": len(lefts) + 1,
        "micros": len(lefts[0]),
    }

    def buffer_set(count, lead, rows, columns, dtype):
        def shaped(many, *dims):
            return (many, *dims, rows, columns) if lead else (*dims, rows, columns)

        halved = [(2,) * (bits - 1 - s) for s in range(bits)]
        result = [
            pltpu.VMEM(shaped(slots, dp_count, *(2,) * bits), dtype),
            pltpu.VMEM(shaped(count, dp_count, *halved[0]), dtype),
            pltpu.VMEM(shaped(slots, dp_count - 1), dtype),
            pltpu.VMEM(shaped(count, dp_count - 1), dtype),
            pltpu.VMEM(shaped(slots), f32),
        ]
        for s in range(1, bits):
            result += [
                pltpu.VMEM(shaped(slots, dp_count, *halved[s]), f32),
                pltpu.VMEM(shaped(slots, dp_count, *halved[s]), dtype),
                pltpu.VMEM(shaped(count, dp_count, *halved[s]), dtype),
            ]
        return result

    micro_count, rows = len(lefts[0]), lefts[0][0].shape[0]
    steps = bits - 1 + dp_count
    small = small.reshape(dp_count, *(2,) * bits, *small.shape[1:])
    widths = [(a[0].shape[1], b[0].shape[1]) for a, b in zip(lefts, rights)]
    flops = sum(2 * micro_count * rows * a * b for a, b in widths)
    return pl.pallas_call(
        functools.partial(product_scatter_body, dp_count, bits, plan, len(unique), len(rights)),
        out_shape=[jax.ShapeDtypeStruct((a // devices, b), f32) for a, b in widths]
        + [jax.ShapeDtypeStruct(small.shape[-2:], f32)],
        in_specs=[ANY] * ((len(unique) + len(rights)) * micro_count + 1),
        out_specs=[ANY] * (len(lefts) + 1),
        scratch_shapes=[pltpu.VMEM((micro_count, *u[0].shape), bf16) for u in unique]
        + [
            pltpu.VMEM((2, micro_count, rows, 3 * lane), bf16),
            pltpu.SemaphoreType.DMA((len(unique), micro_count)),
            pltpu.SemaphoreType.DMA((2, micro_count)),
            pltpu.SemaphoreType.DMA,
            pltpu.SemaphoreType.DMA((n, steps)),
            pltpu.SemaphoreType.DMA((n, steps)),
            pltpu.SemaphoreType.DMA((n, height // 16)),
        ]
        + buffer_set(n - 1, True, height, lane, bf16)
        + buffer_set(1, False, *small.shape[-2:], f32),
        compiler_params=pltpu.CompilerParams(
            collective_id=collective_id, has_side_effects=True, vmem_limit_bytes=62 << 20
        ),
        cost_estimate=pl.CostEstimate(flops=flops, bytes_accessed=100 << 20, transcendentals=0),
    )(*[x for u in unique for x in u], *[x for r in rights for x in r], small)


def weight_grad_body(n, *refs):
    lefts, rights, out_ref = refs[:n], refs[n : 2 * n], refs[2 * n]
    total = rows_inner(lefts[0][...], rights[0][...])
    for left, right in zip(lefts[1:], rights[1:]):
        total = total + rows_inner(left[...], right[...])
    out_ref[...] = total.astype(out_ref.dtype)


def weight_grad(lefts, rights, row_tile):
    n, (rows, height), width = len(lefts), lefts[0].shape, rights[0].shape[1]
    return pl.pallas_call(
        functools.partial(weight_grad_body, n),
        grid=(height // row_tile,),
        out_shape=jax.ShapeDtypeStruct((height, width), bf16),
        in_specs=[pl.BlockSpec((rows, row_tile), lambda i: (0, i))] * n + [whole((rows, width))] * n,
        out_specs=pl.BlockSpec((row_tile, width), lambda i: (i, 0)),
        compiler_params=params(),
        cost_estimate=pl.CostEstimate(
            flops=2 * n * rows * height * width,
            bytes_accessed=2 * (n * rows * (height + width) + height * width),
            transcendentals=0,
        ),
    )(*lefts, *rights)


def fourier_table(chunk):
    freq = np.arange(chunk)[:, None]
    time = np.arange(chunk)[None, :]
    angle = (freq * time % (2 * chunk)) * (np.pi / chunk)
    sines = -np.sin(angle)
    sines[0] = 1.0 - 2.0 * (np.arange(chunk) % 2)
    table = np.concatenate([np.cos(angle), sines], axis=0)
    scaling = np.full((2 * chunk, 1), 1.0 / chunk)
    scaling[0] = scaling[chunk] = 0.5 / chunk
    sign = np.tile(1.0 - 2.0 * (np.arange(chunk) % 2), 2)
    sign[chunk] = 1.0 - 2.0 * (chunk % 2)
    return table.astype(np.float32), (table * scaling).astype(np.float32), sign.astype(np.float32)


def high_and_low(table):
    high = table.astype(jnp.bfloat16)
    return np.stack([high, (table - high.astype(np.float32)).astype(jnp.bfloat16)])


def spectrum(table_ref, values):
    return matmul(table_ref[0], values) + matmul(table_ref[1], values)


def to_time(inverse_ref, spec):
    high = spec.astype(bf16)
    low = (spec - high.astype(f32)).astype(bf16)
    return (
        rows_inner(inverse_ref[0], high)
        + rows_inner(inverse_ref[1], high)
        + rows_inner(inverse_ref[0], low)
    )


def packed_product(first, second, edge, conjugate):
    (a_re, a_im), (b_re, b_im) = first, second
    straight, crossed = a_re * b_re, a_im * b_im
    if conjugate:
        real = straight + jnp.where(edge, 0.0, crossed)
        imag = jnp.where(edge, crossed, a_re * b_im - a_im * b_re)
    else:
        real = straight - jnp.where(edge, 0.0, crossed)
        imag = jnp.where(edge, crossed, a_re * b_im + a_im * b_re)
    return real, imag


def pair_sum(pairs, edge, conjugate):
    real, imag = packed_product(*pairs[0], edge, conjugate)
    for first, second in pairs[1:]:
        more = packed_product(first, second, edge, conjugate)
        real, imag = real + more[0], imag + more[1]
    return real, imag


def halves(ref, block, at, chunk):
    return ref[block, :chunk, at], ref[block, chunk:, at]


def convolve_body(table_ref, inverse_ref, kernel_ref, rows_ref, out_ref, spec_ref, back_ref):
    blocks, chunk, columns = rows_ref.shape
    lanes = kernel_ref.shape[2]
    edge = lax.broadcasted_iota(jnp.int32, (chunk, lanes), 0) == 0
    for c in range(blocks):
        spec_ref[c] = spectrum(table_ref, rows_ref[c])
        for g in range(columns // lanes):
            at = slice(g * lanes, (g + 1) * lanes)
            everything = slice(None)
            real, imag = pair_sum(
                [
                    (halves(kernel_ref, k, everything, chunk), halves(spec_ref, c - k, at, chunk))
                    for k in range(c + 1)
                ],
                edge,
                False,
            )
            back_ref[:chunk, at], back_ref[chunk:, at] = real, imag
        out_ref[c] = to_time(inverse_ref, back_ref[...]).astype(out_ref.dtype)


def convolve_back_body(
    table_ref, inverse_ref, kernel_ref, rows_ref, grad_ref, out_ref, kernel_grad_ref,
    spec_ref, grad_spec_ref, back_ref,
):
    blocks, chunk, columns = rows_ref.shape
    lanes = kernel_ref.shape[2]
    edge = lax.broadcasted_iota(jnp.int32, (chunk, lanes), 0) == 0
    everything = slice(None)
    groups = [slice(g * lanes, (g + 1) * lanes) for g in range(columns // lanes)]
    for c in range(blocks):
        spec_ref[c] = spectrum(table_ref, rows_ref[c])
    for c in reversed(range(blocks)):
        grad_spec_ref[c] = spectrum(table_ref, grad_ref[c])
        for at in groups:
            real, imag = pair_sum(
                [
                    (
                        halves(kernel_ref, late - c, everything, chunk),
                        halves(grad_spec_ref, late, at, chunk),
                    )
                    for late in range(c, blocks)
                ],
                edge,
                True,
            )
            back_ref[:chunk, at], back_ref[chunk:, at] = real, imag
        out_ref[c] = to_time(inverse_ref, back_ref[...]).astype(out_ref.dtype)
    for k in range(blocks):
        real, imag = pair_sum(
            [
                (halves(spec_ref, c - k, at, chunk), halves(grad_spec_ref, c, at, chunk))
                for c in range(k, blocks)
                for at in groups
            ],
            edge,
            True,
        )
        kernel_grad_ref[k, :chunk], kernel_grad_ref[k, chunk:] = real, imag


def kernel_factors(decay, frequency, log_step, length):
    fine = 32
    coarse = length // fine
    step_size = jnp.exp(log_step)[:, None]
    real = (step_size * decay)[:, None, :]
    imag = (step_size * frequency)[:, None, :]
    far = (jnp.arange(coarse, dtype=jnp.int32) * fine).astype(f32)[None, :, None]
    near = jnp.arange(fine, dtype=jnp.int32).astype(f32)[None, :, None]
    far_damp, near_damp = jnp.exp(real * far), jnp.exp(real * near)
    return (
        (far_damp * jnp.cos(imag * far), far_damp * jnp.sin(imag * far)),
        (near_damp * jnp.cos(imag * near), near_damp * jnp.sin(imag * near)),
        step_size,
    )


def kernel_forward(weight_pair, factors):
    (far_re, far_im), (near_re, near_im), _ = factors
    w_re, w_im = weight_pair[0][:, None, :], weight_pair[1][:, None, :]
    left = jnp.concatenate([far_re, -far_im], axis=2)
    right = jnp.concatenate(
        [w_re * near_re - w_im * near_im, w_re * near_im + w_im * near_re], axis=2
    )
    rows = jnp.einsum("han,hbn->hab", left, right, precision=highest)
    return rows.reshape(rows.shape[0], -1)


def kernel_backward(grad_rows, weight_pair, decay, frequency, factors):
    (far_re, far_im), (near_re, near_im), step_size = factors
    channels, coarse, states = far_re.shape
    fine = near_re.shape[1]
    tiles = grad_rows.reshape(channels, coarse, fine)
    near_index = jnp.arange(fine, dtype=jnp.int32).astype(f32)
    far_index = (jnp.arange(coarse, dtype=jnp.int32) * fine).astype(f32)[None, :, None]
    stacked = jnp.concatenate([tiles, tiles * near_index], axis=1)
    part = jnp.einsum(
        "hab,hbn->han", stacked, jnp.concatenate([near_re, near_im], axis=2), precision=highest
    )
    u_re, u_im = part[:, :coarse, :states], part[:, :coarse, states:]
    v_re = part[:, coarse:, :states] + far_index * u_re
    v_im = part[:, coarse:, states:] + far_index * u_im
    s_re = jnp.sum(far_re * u_re - far_im * u_im, axis=1)
    s_im = jnp.sum(far_re * u_im + far_im * u_re, axis=1)
    t_re = jnp.sum(far_re * v_re - far_im * v_im, axis=1)
    t_im = jnp.sum(far_re * v_im + far_im * v_re, axis=1)
    w_re, w_im = weight_pair[0], weight_pair[1]
    along_re = step_size * (w_re * t_re - w_im * t_im)
    along_im = -step_size * (w_re * t_im + w_im * t_re)
    return (
        jnp.stack([s_re, -s_im]),
        along_re,
        along_im,
        jnp.sum(decay * along_re + frequency * along_im, axis=1),
    )


def shards(
    tokens,
    cotangent,
    teacher,
    lengths,
    dealing,
    loss_mask,
    norm_gain,
    norm_bias,
    gate_weight,
    reduce_weight,
    state_weight,
    decay_rate,
    frequency,
    log_step,
    expand_weight,
    out_weight,
):
    dp_count, fsdp_count = lax.axis_size("dp"), lax.axis_size("fsdp")
    devices = dp_count * fsdp_count
    group_index = lax.axis_index("fsdp")
    dp_place = lax.axis_index("dp")
    micro_count, seqs, chunk, width = tokens.shape
    rows = seqs * chunk
    seq_length = chunk * dp_count
    gate_width = gate_weight.shape[1]
    reduced_width = reduce_weight.shape[1]
    own = reduced_width // dp_count
    lanes = max(own, 128)
    share = norm_gain.shape[0]
    micros = range(micro_count)
    direct = own % 128 == 0

    small = jnp.zeros((16, 256), bf16).at[0, :share].set(norm_gain).at[1, :share].set(norm_bias)
    mask_rows = loss_mask.reshape(micro_count, dp_count, chunk).transpose(1, 0, 2)
    mask_rows = jnp.pad(mask_rows, ((0, 0), (0, 8 - micro_count), (0, 0)))
    teacher_rows = [teacher[m].reshape(dp_count, chunk, width) for m in micros]
    first, small, *swapped = gather_all(
        [jnp.concatenate([gate_weight, reduce_weight], axis=1), small],
        [mask_rows, *teacher_rows[1:]],
        1,
    )
    masked = swapped[0].transpose(1, 0, 2)[:micro_count]
    first = first.reshape(width, gate_width + reduced_width)
    gain_row = small[:, :, 0, :share].reshape(1, width).astype(f32)
    bias_row = small[:, :, 1, :share].reshape(1, width).astype(f32)

    per_block = max(1, 512 // chunk)
    steps = seqs // per_block
    middle_block = max(1, 256 // chunk)
    middle_steps = seqs // middle_block

    def row_spec(columns, count=per_block):
        return pl.BlockSpec((count * chunk, columns), lambda i, *_: (i, 0))

    def shared(shape, block):
        return pl.BlockSpec(shape, lambda i, *_: block, pipeline_mode=pl.Buffered(1))

    lane_shape = (dp_count, chunk, seqs * own)
    if not direct:
        lane_shape = (1, rows, reduced_width)

    def dims(count):
        return (count, chunk, own) if direct else (1, count * chunk, reduced_width)

    def lane_spec(count):
        if direct:
            return pl.BlockSpec((dp_count, chunk, count * own), lambda i, *_: (0, 0, i))
        return pl.BlockSpec((1, count * chunk, reduced_width), lambda i, *_: (0, i, 0))

    def tokens_spec(m, count):
        return pl.BlockSpec((None, count, chunk, width), lambda i, *_: (m, i, 0, 0))

    def send_lanes(values):
        if not direct:
            values = values.reshape(seqs, chunk, dp_count, own).transpose(2, 1, 0, 3)
            values = values.reshape(dp_count, chunk, seqs * own)
        return exchange(values)

    def receive_lanes(values):
        values = exchange(values)
        if not direct:
            values = values.reshape(dp_count, chunk, seqs, own).transpose(2, 1, 0, 3)
            values = values.reshape(1, rows, reduced_width)
        return values

    def reduce_rows(m):
        return pl.pallas_call(
            functools.partial(reduce_body, dims(per_block)),
            grid=(steps,),
            out_shape=[
                jax.ShapeDtypeStruct((rows, width), bf16),
                jax.ShapeDtypeStruct(lane_shape, bf16),
                jax.ShapeDtypeStruct((rows, reduced_width), f32),
            ],
            in_specs=[
                tokens_spec(m, per_block),
                whole((1, width)),
                whole((1, width)),
                shared((width, reduced_width), (0, gate_width // reduced_width)),
            ],
            out_specs=[row_spec(width), lane_spec(per_block), row_spec(reduced_width)],
            compiler_params=params(),
            cost_estimate=pl.CostEstimate(
                flops=2 * rows * width * reduced_width,
                bytes_accessed=8 * rows * width,
                transcendentals=2 * rows * reduced_width,
            ),
        )(tokens, gain_row, bias_row, first)

    normed, lanes_out, slope_reduced = zip(*[reduce_rows(m) for m in micros])
    lanes_in = [send_lanes(x) for x in lanes_out]

    local_ids = group_index * seqs + jnp.arange(seqs, dtype=jnp.int32)
    targets = jnp.take(dealing, local_ids, axis=1)
    own_lengths = jnp.take(lengths, local_ids, axis=1)
    positions = dp_place * chunk + jnp.arange(chunk, dtype=jnp.int32)
    valid = (positions[None, None, :] < own_lengths[:, :, None]).astype(f32)
    keep = jnp.take_along_axis(masked, targets[:, :, None], axis=1).astype(f32) * valid
    own_count = jnp.sum(keep)
    row_weights = jnp.stack([valid, keep], axis=-1).reshape(micro_count, rows, 2)

    table_np, inverse_np, sign_np = fourier_table(chunk)
    sign = jnp.asarray(sign_np)[:, None]
    table2, inverse2 = jnp.asarray(high_and_low(table_np)), jnp.asarray(high_and_low(inverse_np))
    factors = kernel_factors(decay_rate, frequency, log_step, seq_length)
    own_kernel = kernel_forward(state_weight, factors)
    kernel = lax.all_gather(own_kernel, "fsdp", axis=0, tiled=True)
    segments = jnp.einsum(
        "kt,hct->ckh", jnp.asarray(table_np), kernel.reshape(own, dp_count, chunk), precision=highest
    )
    previous = jnp.concatenate([jnp.zeros_like(segments[:1]), segments[:-1]], axis=0)
    kernel_spec = jnp.tile(segments + sign * previous, (1, 1, lanes // own))

    blocks = (dp_count, chunk, seqs * own)
    spec_scratch = pltpu.VMEM((dp_count, 2 * chunk, seqs * own), f32)
    back_scratch = pltpu.VMEM((2 * chunk, seqs * own), f32)
    transform_flops = 8 * chunk * chunk * dp_count * seqs * own

    def convolve(values):
        return pl.pallas_call(
            convolve_body,
            out_shape=jax.ShapeDtypeStruct(blocks, bf16),
            scratch_shapes=[spec_scratch, back_scratch],
            compiler_params=params(),
            cost_estimate=pl.CostEstimate(
                flops=5 * transform_flops // 2, bytes_accessed=8 << 20, transcendentals=0
            ),
        )(table2, inverse2, kernel_spec, values)

    def convolve_back(values, grads):
        return pl.pallas_call(
            convolve_back_body,
            out_shape=[
                jax.ShapeDtypeStruct(blocks, bf16),
                jax.ShapeDtypeStruct((dp_count, 2 * chunk, lanes), f32),
            ],
            scratch_shapes=[spec_scratch, spec_scratch, back_scratch],
            compiler_params=params(),
            cost_estimate=pl.CostEstimate(
                flops=7 * transform_flops // 2, bytes_accessed=8 << 20, transcendentals=0
            ),
        )(table2, inverse2, kernel_spec, values, grads)

    convolved = [convolve(x) for x in lanes_in]
    late = lax.optimization_barrier((expand_weight, out_weight, teacher_rows[0], *convolved))
    w_expand, w_out, counts, *more, gate, slope = gather_all(
        [late[0], late[1], jnp.full((8, 256), own_count, f32)],
        [late[2]],
        2,
        gate_work(normed, first, gate_width),
    )
    teach = [*more, *swapped[1:]]
    w_expand = w_expand.reshape(reduced_width, gate_width)
    w_out = w_out.reshape(gate_width, width)
    count = jnp.sum(counts[:, :, 0, 0])
    error_scale = (2.0 / (width * count)).reshape(1)
    mixed = [receive_lanes(x) for x in convolved]
    def middle_rows(m, *earlier):
        teach_specs = [
            pl.BlockSpec((1, chunk, width), functools.partial(teach_block, s)) for s in range(middle_block)
        ]
        gate_spec = pl.BlockSpec(
            (middle_block * chunk, gate_width), lambda i, *_: (m * middle_steps + i, 0)
        )
        wide, narrow = row_spec(gate_width, middle_block), row_spec(width, middle_block)
        return pl.pallas_call(
            functools.partial(middle_body, dims(middle_block), middle_block, 768),
            grid_spec=pltpu.PrefetchScalarGridSpec(
                num_scalar_prefetch=2,
                grid=(middle_steps,),
                in_specs=[
                    lane_spec(middle_block),
                    gate_spec,
                    gate_spec,
                    shared((reduced_width, gate_width), (0, 0)),
                    shared((gate_width, width), (0, 0)),
                    tokens_spec(m, middle_block),
                    tokens_spec(m, middle_block),
                    row_spec(2, middle_block),
                    *teach_specs,
                    *[ANY] * len(earlier),
                ],
                out_specs=[
                    row_spec(reduced_width, middle_block),
                    wide,
                    narrow,
                    wide,
                    wide,
                    tokens_spec(m, middle_block),
                    narrow,
                    pl.BlockSpec((1, 8, width), lambda i, *_: (i, 0, 0)),
                    lane_spec(middle_block),
                ],
                scratch_shapes=[pltpu.VMEM((middle_block * chunk, gate_width), f32)],
            ),
            out_shape=[
                jax.ShapeDtypeStruct((rows, reduced_width), bf16),
                jax.ShapeDtypeStruct((rows, gate_width), bf16),
                jax.ShapeDtypeStruct((rows, width), bf16),
                jax.ShapeDtypeStruct((rows, gate_width), bf16),
                jax.ShapeDtypeStruct((rows, gate_width), bf16),
                jax.ShapeDtypeStruct(tokens.shape, bf16),
                jax.ShapeDtypeStruct((rows, width), bf16),
                jax.ShapeDtypeStruct((middle_steps, 8, width), f32),
                jax.ShapeDtypeStruct(lane_shape, bf16),
            ],
            input_output_aliases={10 + middle_block: 5} if earlier else {},
            compiler_params=params(),
            cost_estimate=pl.CostEstimate(
                flops=4 * rows * gate_width * (width + reduced_width),
                bytes_accessed=10 * rows * gate_width + 16 * rows * width,
                transcendentals=0,
            ),
        )(
            targets[m], error_scale, mixed[m], gate, slope, w_expand, w_out, tokens, cotangent,
            row_weights[m], *[teach[m]] * middle_block, *earlier,
        )

    def teach_block(s, i, order, scale):
        return (order[i * middle_block + s], 0, 0)

    def input_rows(m, back, gate_grad, full_grad, *earlier):
        eight = pl.BlockSpec((1, 8, width), lambda i, *_: (i, 0, 0))
        return pl.pallas_call(
            functools.partial(input_body, dims(per_block)),
            grid=(steps,),
            in_specs=[
                lane_spec(per_block),
                row_spec(reduced_width),
                row_spec(gate_width),
                shared((width, gate_width), (0, 0)),
                shared((width, reduced_width), (0, gate_width // reduced_width)),
                tokens_spec(m, per_block),
                whole((1, width)),
                row_spec(width),
                *[ANY] * len(earlier),
            ],
            out_specs=[tokens_spec(m, per_block), row_spec(reduced_width), eight, eight],
            out_shape=[
                jax.ShapeDtypeStruct(tokens.shape, bf16),
                jax.ShapeDtypeStruct((rows, reduced_width), bf16),
                jax.ShapeDtypeStruct((steps, 8, width), f32),
                jax.ShapeDtypeStruct((steps, 8, width), f32),
            ],
            scratch_shapes=[pltpu.VMEM((per_block * chunk, reduced_width), bf16)],
            input_output_aliases={8: 0} if earlier else {},
            compiler_params=params(),
            cost_estimate=pl.CostEstimate(
                flops=2 * rows * width * (gate_width + reduced_width),
                bytes_accessed=4 * rows * gate_width + 8 * rows * width,
                transcendentals=0,
            ),
        )(back, slope_reduced[m], gate_grad, first, first, tokens, gain_row, full_grad, *earlier)

    middle = []
    for m in micros:
        middle.append(middle_rows(m, *[x[5] for x in middle[-1:]]))
    outputs = middle[-1][5]
    state_out, product, branch_grad, expanded_grad, gate_grad, _, full_grad, error_rows, lane_grad = zip(*middle)
    grads_in = [send_lanes(x) for x in lane_grad]
    back, kernel_grads = zip(*[convolve_back(lanes_in[m], grads_in[m]) for m in micros])
    back = [receive_lanes(x) for x in back]
    ends = []
    for m in micros:
        ends.append(input_rows(m, back[m], gate_grad[m], full_grad[m], *[x[0] for x in ends[-1:]]))
    returned = ends[-1][0]
    _, reduced_grad, gain_rows, bias_rows = zip(*ends)

    kernel_total = sum(kernel_grads)
    if not direct:
        kernel_total = kernel_total.reshape(dp_count, 2 * chunk, lanes // own, own).sum(axis=2)
    following = jnp.concatenate([kernel_total[1:], jnp.zeros_like(kernel_total[:1])], axis=0)
    kernel_grad = jnp.einsum(
        "kt,ckh->hct", jnp.asarray(inverse_np), kernel_total + sign * following, precision=highest
    ).reshape(own, seq_length)
    kernel_grad, _ = lax.optimization_barrier((kernel_grad, reduced_grad))
    kernel_grad = lax.psum_scatter(kernel_grad, "fsdp", scatter_dimension=0, tiled=True)
    pair_grad, decay_grad, frequency_grad, step_grad = kernel_backward(
        kernel_grad, state_weight, decay_rate, frequency, factors
    )

    gain_total = jnp.sum(sum(gain_rows), axis=(0, 1)).reshape(devices, 1, share)
    bias_total = jnp.sum(sum(bias_rows), axis=(0, 1)).reshape(devices, 1, share)
    error_total = jnp.full((devices, 1, share), jnp.sum(sum(error_rows)))
    sums = jnp.concatenate([gain_total, bias_total, error_total], axis=1)
    sums = jnp.pad(sums, ((0, 0), (0, 5), (0, 128 - share)))
    pairs = [
        (normed, gate_grad),
        (state_out, expanded_grad),
        (product, branch_grad),
        (normed, reduced_grad),
    ]
    if all(left[0].shape[1] // devices % 16 == 0 for left, _ in pairs):
        lefts, rights = zip(*pairs)
        gate_sum, expand_sum, out_sum, reduce_sum, sums = product_scatter(lefts, rights, sums, 3)
    else:
        made = [weight_grad(left, right, 256) for left, right in pairs]
        gate_sum, expand_sum, out_sum, reduce_sum, sums = scatter_all(
            [x.reshape(devices, -1, x.shape[1]) for x in made] + [sums], [4, 2, 4, 1, 1], 3
        )
    loss_value = sums[2, 0] / (width * count)
    return (
        outputs,
        loss_value,
        returned,
        sums[0, :share],
        sums[1, :share],
        gate_sum,
        reduce_sum,
        pair_grad,
        decay_grad,
        frequency_grad,
        step_grad,
        expand_sum,
        out_sum,
    )


def solution(mesh):
    in_specs = (
        P(None, "fsdp", "dp", None),
        P(None, "fsdp", "dp", None),
        P(None, ("dp", "fsdp"), None, None),
        P(),
        P(),
        P(None, ("dp", "fsdp"), None),
        P(("dp", "fsdp")),
        P(("dp", "fsdp")),
        P(("dp", "fsdp"), None),
        P(("dp", "fsdp"), None),
        P(None, ("dp", "fsdp"), None),
        P(("dp", "fsdp"), None),
        P(("dp", "fsdp"), None),
        P(("dp", "fsdp")),
        P(("dp", "fsdp"), None),
        P(("dp", "fsdp"), None),
    )
    out_specs = (
        P(None, "fsdp", "dp", None),
        P(),
        P(None, "fsdp", "dp", None),
        P(("dp", "fsdp")),
        P(("dp", "fsdp")),
        P(("dp", "fsdp"), None),
        P(("dp", "fsdp"), None),
        P(None, ("dp", "fsdp"), None),
        P(("dp", "fsdp"), None),
        P(("dp", "fsdp"), None),
        P(("dp", "fsdp")),
        P(("dp", "fsdp"), None),
        P(("dp", "fsdp"), None),
    )
    return jax.shard_map(shards, mesh=mesh, in_specs=in_specs, out_specs=out_specs, check_vma=False)
```

```python
import functools

import numpy as np
import jax
import jax.numpy as jnp
from jax import lax
from jax.experimental import pallas as pl
from jax.experimental.pallas import tpu as pltpu
from jax.sharding import PartitionSpec as P

epsilon = 1e-05
highest = lax.Precision.HIGHEST
bf16 = jnp.bfloat16
f32 = jnp.float32
MESH = pl.DeviceIdType.MESH
ANY = pl.BlockSpec(memory_space=pltpu.HBM)


def bit_of(index, bit):
    return lax.rem(lax.div(index, 1 << bit), 2)


def flip(index, bit):
    return index + (1 << bit) - 2 * (1 << bit) * bit_of(index, bit)


def greet(dp_count, bits):
    d, f = lax.axis_index("dp"), lax.axis_index("fsdp")
    barrier = pltpu.get_barrier_semaphore()
    for o in range(1, dp_count):
        peer = lax.rem(d + o, dp_count)
        pl.semaphore_signal(barrier, inc=1, device_id={"dp": peer}, device_id_type=MESH)
    for b in range(bits):
        pl.semaphore_signal(barrier, inc=1, device_id={"fsdp": flip(f, b)}, device_id_type=MESH)
    pl.semaphore_wait(barrier, dp_count - 1 + bits)


def near_first(count):
    order = [0]
    for k in range(1, count // 2 + 1):
        order += [k] if k == count - k else [k, count - k]
    return order


def gather_body(dp_count, bits, n, leads, work, *refs):
    n_swap = len(leads)
    n_work_in, n_work_out = work[0] if work else (0, 0)
    moved = n + n_swap
    ins, refs = list(refs[:moved]), refs[moved:]
    for e, lead in enumerate(leads):
        ins[n + e] = ins[n + e].at[lead]
    work_ins, refs = refs[:n_work_in], refs[n_work_in:]
    outs, refs = refs[:moved], refs[moved:]
    work_outs, refs = refs[:n_work_out], refs[n_work_out:]
    z_send, z_recv, send, recv, own_sem, swap_send, swap_recv = refs[:7]
    begin, tick, end = work[1](work_ins, work_outs, refs[7:]) if work else (None, None, None)
    d, f = lax.axis_index("dp"), lax.axis_index("fsdp")
    cuts = []
    for x in ins[:n]:
        cut = x.shape[1] // 256 * 128
        cuts.append(((0, cut), (cut, x.shape[1] - cut)))
    order = near_first(dp_count)
    if work:
        begin()
    greet(dp_count, bits)
    own = [pltpu.make_async_copy(ins[a], outs[a].at[d, f], own_sem.at[a]) for a in range(n)]
    own += [
        pltpu.make_async_copy(ins[a].at[d], outs[a].at[d], own_sem.at[a])
        for a in range(n, n + n_swap)
    ]
    for copy in own:
        copy.start()
    started, arrived, waited = [], {}, set()

    def push(src, dst, send_sem, recv_sem, device_id):
        copy = pltpu.make_async_remote_copy(
            src_ref=src,
            dst_ref=dst,
            send_sem=send_sem,
            recv_sem=recv_sem,
            device_id=device_id,
            device_id_type=MESH,
        )
        copy.start()
        started.append(copy)
        return copy

    for o in order[1:]:
        for h in range(2):
            for a in range(n):
                lo, size = cuts[a][h]
                arrived[(o, 0, h, a)] = push(
                    ins[a].at[:, pl.ds(lo, size)],
                    outs[a].at[d, f, :, pl.ds(lo, size)],
                    z_send.at[o - 1, h, a],
                    z_recv.at[o - 1, h, a],
                    {"dp": lax.rem(d + o, dp_count)},
                )
    for copy in own:
        copy.wait()
    upper = list(range(1, bits))
    stages = [upper + [0], upper[::-1] + [0]]
    masks = [[[0]], [[0]]]
    for h in range(2):
        for s in range(bits):
            masks[h].append(masks[h][s] + [m ^ (1 << stages[h][s]) for m in masks[h][s]])
    slot, group = 0, 0
    for t in range(dp_count + bits - 1):
        for i in range(dp_count):
            s, o = t - i, order[i]
            if not 0 <= s < bits:
                continue
            if work:
                tick(group, dp_count * bits)
                group += 1
            for k in range(len(masks[0][s])):
                for h in range(2):
                    mask, b = masks[h][s][k], stages[h][s]
                    src_f = f
                    for bb in range(bits):
                        if mask >> bb & 1:
                            src_f = flip(src_f, bb)
                    for a in range(n):
                        key = (o, mask, h, a)
                        if key in arrived and key not in waited:
                            arrived[key].wait_recv()
                            waited.add(key)
                        lo, size = cuts[a][h]
                        src_d = lax.rem(d - o + dp_count, dp_count)
                        piece = outs[a].at[src_d, src_f, :, pl.ds(lo, size)]
                        arrived[(o, mask ^ (1 << b), h, a)] = push(
                            piece, piece, send.at[slot], recv.at[slot], {"fsdp": flip(f, b)}
                        )
                        slot += 1
        if t == 0:
            for o in order[1:]:
                peer = lax.rem(d + o, dp_count)
                for e in range(n_swap):
                    arrived[(o, e)] = push(
                        ins[n + e].at[peer],
                        outs[n + e].at[d],
                        swap_send.at[o - 1, e],
                        swap_recv.at[o - 1, e],
                        {"dp": peer},
                    )
    if work:
        end()
    for key, copy in arrived.items():
        if key not in waited:
            copy.wait_recv()
    for copy in started:
        copy.wait_send()


def gather_all(arrays, swaps, collective_id, work=None):
    work_in, work_out, work_scratch, work_body = work or ((), (), (), None)
    sizes = (len(work_in), len(work_out))
    leads, swaps = [lead for lead, _ in swaps], [x for _, x in swaps]
    dp_count, fsdp_count = lax.axis_size("dp"), lax.axis_size("fsdp")
    bits = fsdp_count.bit_length() - 1
    n, n_swap = len(arrays), len(swaps)
    slots = 2 * dp_count * (fsdp_count - 1) * n
    total = dp_count * fsdp_count * sum(x.size * x.dtype.itemsize for x in arrays)
    return pl.pallas_call(
        functools.partial(gather_body, dp_count, bits, n, leads, (sizes, work_body) if work else None),
        out_shape=[
            jax.ShapeDtypeStruct((dp_count, fsdp_count, *x.shape), x.dtype) for x in arrays
        ]
        + [jax.ShapeDtypeStruct(x.shape[1:], x.dtype) for x in swaps]
        + list(work_out),
        in_specs=[ANY] * (n + n_swap + sizes[0]),
        out_specs=[ANY] * (n + n_swap + sizes[1]),
        scratch_shapes=[
            pltpu.SemaphoreType.DMA((dp_count - 1, 2, n)),
            pltpu.SemaphoreType.DMA((dp_count - 1, 2, n)),
            pltpu.SemaphoreType.DMA((slots,)),
            pltpu.SemaphoreType.DMA((slots,)),
            pltpu.SemaphoreType.DMA((n + n_swap,)),
            pltpu.SemaphoreType.DMA((dp_count - 1, max(n_swap, 1))),
            pltpu.SemaphoreType.DMA((dp_count - 1, max(n_swap, 1))),
            *work_scratch,
        ],
        compiler_params=pltpu.CompilerParams(
            collective_id=collective_id, has_side_effects=True, vmem_limit_bytes=62 << 20
        ),
        cost_estimate=pl.CostEstimate(flops=0, bytes_accessed=20 * total, transcendentals=0),
    )(*arrays, *swaps, *work_in)


def scatter_body(dp_count, bits, pieces, kinds, *refs):
    n_in, n = len(kinds), len(pieces)
    ins, outs = refs[:n_in], refs[n_in : 2 * n_in]
    per = 6 + 2 * (bits - 1)
    scratch = [refs[2 * n_in + i * per : 2 * n_in + (i + 1) * per] for i in range(n)]
    load_sem, send, recv, store_sem = refs[2 * n_in + n * per :]
    d, f = lax.axis_index("dp"), lax.axis_index("fsdp")
    my = [bit_of(f, b) for b in range(bits)]
    upper = list(range(bits - 1, 0, -1))
    waits, fixed, ends = [None] * n, [{} for _ in range(n)], []
    greet(dp_count, bits)

    def region(i, other=None):
        return (slice(None),) + tuple(
            1 - my[b] if b == other else fixed[i].get(b, slice(None)) for b in upper
        )

    def push(i, at, src, dst, device_id):
        copy = pltpu.make_async_remote_copy(
            src_ref=src,
            dst_ref=dst,
            send_sem=send.at[i, at],
            recv_sem=recv.at[i, at],
            device_id=device_id,
            device_id_type=MESH,
        )
        copy.start()
        ends.append(copy)
        return copy

    def first(i):
        op, lo, cols = pieces[i]
        lead = (slice(None),) * bits
        own = ins[op].at[(*lead, my[0], slice(None), pl.ds(lo, cols))]
        other = ins[op].at[(*lead, 1 - my[0], slice(None), pl.ds(lo, cols))]
        load = pltpu.make_async_copy(own, scratch[i][0], load_sem.at[i])
        load.start()
        waits[i] = (load, push(i, 0, other, scratch[i][1], {"fsdp": flip(f, 0)}))

    def arrive(i, s):
        acc = scratch[i][2]
        if s == 0:
            waits[i][0].wait()
            waits[i][1].wait_recv()
            acc[...] = scratch[i][0][...].astype(f32) + scratch[i][1][...].astype(f32)
        else:
            waits[i].wait_recv()
            here = region(i)
            acc[here] = acc[here] + scratch[i][5 + 2 * s][...].astype(f32)

    def middle(i, s):
        arrive(i, s - 1)
        b = (upper if i % 2 == 0 else upper[::-1])[s - 1]
        out_buf, in_buf = scratch[i][4 + 2 * s], scratch[i][5 + 2 * s]
        out_buf[...] = scratch[i][2][region(i, b)].astype(out_buf.dtype)
        waits[i] = push(i, s, out_buf, in_buf, {"fsdp": flip(f, b)})
        fixed[i][b] = my[b]

    def last(i):
        arrive(i, bits - 1)
        out_buf, in_buf = scratch[i][3], scratch[i][4]
        waits[i] = []
        for o in near_first(dp_count)[1:]:
            peer = lax.rem(d + o, dp_count)
            out_buf[o - 1] = scratch[i][2][(peer, *region(i)[1:])].astype(out_buf.dtype)
            waits[i].append(
                push(i, bits - 1 + o, out_buf.at[o - 1], in_buf.at[o - 1], {"dp": peer})
            )

    def finish(i):
        op, lo, cols = pieces[i]
        for copy in waits[i]:
            copy.wait_recv()
        total = scratch[i][2][(d, *region(i)[1:])]
        for o in range(1, dp_count):
            total = total + scratch[i][4][o - 1].astype(f32)
        scratch[i][5][...] = total
        store = pltpu.make_async_copy(
            scratch[i][5], outs[op].at[:, pl.ds(lo, cols)], store_sem.at[i]
        )
        store.start()
        return store

    stores = []
    for t in range((n + 1) // 2 + bits + 1):
        for i in range(n):
            s = t - i // 2
            if s == 0:
                first(i)
            elif 1 <= s < bits:
                middle(i, s)
            elif s == bits:
                last(i)
            elif s == bits + 1:
                stores.append(finish(i))
    for copy in ends:
        copy.wait_send()
    for store in stores:
        store.wait()


def scatter_all(arrays, splits, collective_id):
    dp_count, fsdp_count = lax.axis_size("dp"), lax.axis_size("fsdp")
    bits = fsdp_count.bit_length() - 1
    arrays = [a.reshape(dp_count, *(2,) * bits, *a.shape[1:]) for a in arrays]
    pieces, scratch = [], []
    for op, (a, k) in enumerate(zip(arrays, splits)):
        rows, cols = a.shape[-2], a.shape[-1] // k
        half = (dp_count, *(2,) * (bits - 1), rows, cols)
        for j in range(k):
            pieces.append((op, j * cols, cols))
            scratch += [pltpu.VMEM(half, a.dtype)] * 2 + [pltpu.VMEM(half, f32)]
            scratch += [pltpu.VMEM((dp_count - 1, rows, cols), a.dtype)] * 2
            scratch += [pltpu.VMEM((rows, cols), f32)]
            for s in range(1, bits):
                shape = (dp_count, *(2,) * (bits - 1 - s), rows, cols)
                scratch += [pltpu.VMEM(shape, a.dtype)] * 2
    n, steps = len(pieces), bits - 1 + dp_count
    return pl.pallas_call(
        functools.partial(scatter_body, dp_count, bits, pieces, [a.dtype for a in arrays]),
        out_shape=[jax.ShapeDtypeStruct(a.shape[-2:], f32) for a in arrays],
        in_specs=[ANY] * len(arrays),
        out_specs=[ANY] * len(arrays),
        scratch_shapes=scratch
        + [
            pltpu.SemaphoreType.DMA((n,)),
            pltpu.SemaphoreType.DMA((n, steps)),
            pltpu.SemaphoreType.DMA((n, steps)),
            pltpu.SemaphoreType.DMA((n,)),
        ],
        compiler_params=pltpu.CompilerParams(
            collective_id=collective_id, has_side_effects=True, vmem_limit_bytes=60 << 20
        ),
    )(*arrays)


def exchange(values):
    return lax.all_to_all(values, "dp", split_axis=0, concat_axis=0, tiled=True)


def params(limit_mib=60):
    return pltpu.CompilerParams(vmem_limit_bytes=limit_mib << 20)


def whole(shape):
    return pl.BlockSpec(shape, lambda i: (0,) * len(shape), pipeline_mode=pl.Buffered(1))


def matmul(left, right):
    return jnp.dot(left, right, preferred_element_type=f32)


def rows_inner(left, right):
    return lax.dot_general(left, right, (((0,), (0,)), ((), ())), preferred_element_type=f32)


def cols_inner(left, right):
    return lax.dot_general(left, right, (((1,), (1,)), ((), ())), preferred_element_type=f32)


def gelu_and_slope(values):
    phi = 0.5 * (1.0 + lax.erf(values * 0.7071067811865476))
    return (
        values * phi,
        phi + values * jnp.exp(-0.5 * values * values) * 0.3989422804014327,
    )


def centred_rows(tokens_ref, rows):
    inputs = tokens_ref[...].reshape(rows, tokens_ref.shape[-1]).astype(f32)
    centred = inputs - jnp.mean(inputs, axis=1, keepdims=True)
    variance = jnp.mean(centred * centred, axis=1, keepdims=True)
    return inputs, centred, lax.rsqrt(variance + epsilon)


def channels_from_rows(ref, values, seqs, chunk, own):
    for place in range(ref.shape[0]):
        for s in range(seqs):
            ref[place, :, s * own : (s + 1) * own] = values[
                s * chunk : (s + 1) * chunk, place * own : (place + 1) * own
            ].astype(ref.dtype)


def rows_from_channels(ref, scratch, seqs, chunk, own):
    for place in range(ref.shape[0]):
        for s in range(seqs):
            scratch[s * chunk : (s + 1) * chunk, place * own : (place + 1) * own] = ref[
                place, :, s * own : (s + 1) * own
            ]


def reduce_body(dims, tokens_ref, gain_ref, bias_ref, weight_ref, normed_ref, out_ref, slope_ref):
    seqs, chunk, own = dims
    _, centred, inverse_std = centred_rows(tokens_ref, seqs * chunk)
    normed = (centred * inverse_std * gain_ref[...] + bias_ref[...]).astype(bf16)
    normed_ref[...] = normed
    reduced, slope = gelu_and_slope(matmul(normed, weight_ref[...]))
    slope_ref[...] = slope
    channels_from_rows(out_ref, reduced, seqs, chunk, own)


def gate_work(normed, weight):
    (rows, width), gate_width = normed[0].shape, weight.shape[1]
    micro_count, tile = len(normed), 512
    across, down = gate_width // tile, rows // tile
    count = micro_count * across * down

    def body(ins, outs, scratch):
        rows_refs, weight_ref = ins[:-1], ins[-1]
        rows_buf, weight_buf, out_buf, load_sem, store_sem = scratch
        loads = [
            pltpu.make_async_copy(rows_refs[m], rows_buf.at[pl.ds(m * rows, rows)], load_sem.at[m])
            for m in range(micro_count)
        ]
        loads.append(
            pltpu.make_async_copy(weight_ref, weight_buf, load_sem.at[micro_count])
        )
        loaded = []

        def stores(k):
            at = (
                pl.ds(pl.multiple_of(lax.div(k, across) * tile, tile), tile),
                pl.ds(pl.multiple_of(lax.rem(k, across) * tile, tile), tile),
            )
            slot = lax.rem(k, 2)
            return [
                pltpu.make_async_copy(out_buf.at[slot, r], outs[r].at[at], store_sem.at[slot, r])
                for r in range(2)
            ]

        def begin():
            for copy in loads:
                copy.start()

        def step(k, carry):
            @pl.when(k >= 2)
            def _():
                for copy in stores(k - 2):
                    copy.wait()

            slot = lax.rem(k, 2)
            left = rows_buf[pl.ds(pl.multiple_of(lax.div(k, across) * tile, tile), tile), :]
            right = weight_buf[:, pl.ds(pl.multiple_of(lax.rem(k, across) * tile, tile), tile)]
            gate, slope = gelu_and_slope(matmul(left, right))
            out_buf[slot, 0] = gate.astype(bf16)
            out_buf[slot, 1] = slope.astype(bf16)
            for copy in stores(k):
                copy.start()
            return carry

        def tick(group, groups):
            if not loaded:
                for copy in loads:
                    copy.wait()
                loaded.append(True)
            lax.fori_loop(count * group // groups, count * (group + 1) // groups, step, 0)

        def end():
            for k in (count - 2, count - 1):
                for copy in stores(k):
                    copy.wait()

        return begin, tick, end

    shape = jax.ShapeDtypeStruct((micro_count * rows, gate_width), bf16)
    scratch = [
        pltpu.VMEM((micro_count * rows, width), bf16),
        pltpu.VMEM((width, gate_width), bf16),
        pltpu.VMEM((2, 2, tile, tile), bf16),
        pltpu.SemaphoreType.DMA((micro_count + 1,)),
        pltpu.SemaphoreType.DMA((2, 2)),
    ]
    return [*normed, weight], [shape, shape], scratch, body


def middle_body(
    dims, teachers, tile, order_ref, scale_ref, state_ref, gate_ref, slope_ref, expand_ref, weight_ref,
    tokens_ref, cotangent_ref, weights_ref, *refs,
):
    seqs, chunk, own = dims
    teach_refs, refs = refs[:teachers], refs[teachers:]
    (state_out_ref, product_ref, branch_grad_ref, expanded_grad_ref, gate_grad_ref, out_ref,
     full_grad_ref, error_ref, mixed_grad_ref, expanded_ref) = refs[-10:]
    rows, width = seqs * chunk, tokens_ref.shape[-1]
    rows_from_channels(state_ref, state_out_ref, seqs, chunk, own)
    state_out = state_out_ref[...]
    tiles = [slice(j * tile, (j + 1) * tile) for j in range(gate_ref.shape[1] // tile)]
    branch = jnp.zeros((rows, width), f32)
    for at in tiles:
        expanded = matmul(state_out, expand_ref[:, at])
        expanded_ref[:, at] = expanded
        product = (expanded * gate_ref[:, at].astype(f32)).astype(bf16)
        product_ref[:, at] = product
        branch = branch + matmul(product, weight_ref[at, :])
    valid, keep = weights_ref[:, :1], weights_ref[:, 1:]
    full = tokens_ref[...].reshape(rows, width).astype(f32) + valid * branch
    out_ref[...] = full.astype(bf16).reshape(out_ref.shape)
    errors = full - jnp.concatenate([t[0] for t in teach_refs], axis=0).astype(f32)
    error_ref[0] = jnp.sum((keep * errors * errors).reshape(rows // 8, 8, width), axis=0)
    full_grad = cotangent_ref[...].reshape(rows, width).astype(f32) + keep * errors * scale_ref[0]
    full_grad_ref[...] = full_grad.astype(bf16)
    branch_grad = (valid * full_grad).astype(bf16)
    branch_grad_ref[...] = branch_grad
    mixed_grad = jnp.zeros((rows, state_out.shape[1]), f32)
    for at in tiles:
        product_grad = cols_inner(branch_grad, weight_ref[at, :])
        expanded_grad = (product_grad * gate_ref[:, at].astype(f32)).astype(bf16)
        expanded_grad_ref[:, at] = expanded_grad
        gate_grad_ref[:, at] = (
            product_grad * expanded_ref[:, at] * slope_ref[:, at].astype(f32)
        ).astype(bf16)
        mixed_grad = mixed_grad + cols_inner(expanded_grad, expand_ref[:, at])
    channels_from_rows(mixed_grad_ref, mixed_grad, seqs, chunk, own)


def input_body(
    dims, back_ref, slope_ref, gate_grad_ref, gate_weight_ref, reduce_weight_ref, tokens_ref,
    gain_ref, full_grad_ref, *refs,
):
    out_ref, reduced_grad_ref, gain_grad_ref, bias_grad_ref, back_rows_ref = refs[-5:]
    seqs, chunk, own = dims
    rows, width = seqs * chunk, tokens_ref.shape[-1]
    rows_from_channels(back_ref, back_rows_ref, seqs, chunk, own)
    reduced_grad = (back_rows_ref[...].astype(f32) * slope_ref[...]).astype(bf16)
    reduced_grad_ref[...] = reduced_grad
    normed_grad = cols_inner(gate_grad_ref[...], gate_weight_ref[...]) + cols_inner(
        reduced_grad, reduce_weight_ref[...]
    )
    _, centred, inverse_std = centred_rows(tokens_ref, rows)
    unit = centred * inverse_std
    gain_grad_ref[0] = jnp.sum((normed_grad * unit).reshape(rows // 8, 8, width), axis=0)
    bias_grad_ref[0] = jnp.sum(normed_grad.reshape(rows // 8, 8, width), axis=0)
    unit_grad = normed_grad * gain_ref[...]
    result = full_grad_ref[...].astype(f32) + inverse_std * (
        unit_grad
        - jnp.mean(unit_grad, axis=1, keepdims=True)
        - unit * jnp.mean(unit_grad * unit, axis=1, keepdims=True)
    )
    out_ref[...] = result.astype(bf16).reshape(out_ref.shape)


def product_scatter_body(dp_count, bits, plan, n_left, n_right, *refs):
    pieces, slots, lane, micros = plan["pieces"], plan["slots"], plan["lane"], plan["micros"]
    n = len(pieces)
    lefts, refs = refs[: n_left * micros], refs[n_left * micros :]
    rights, refs = refs[: n_right * micros], refs[n_right * micros :]
    ready_ref, small_ref, refs = refs[0], refs[1], refs[2:]
    outs, refs = refs[: plan["outputs"]], refs[plan["outputs"] :]
    left_bufs, refs = refs[:n_left], refs[n_left:]
    right_buf, left_sem, right_sem, load_sem, ready_sem, send, recv, store_sem = refs[:8]
    sets = [refs[8 : 8 + 5 + 3 * (bits - 1)], refs[8 + 5 + 3 * (bits - 1) :]]
    d, f = lax.axis_index("dp"), lax.axis_index("fsdp")
    my = [bit_of(f, b) for b in range(bits)]
    upper = list(range(bits - 1, 0, -1))
    small = n - 1

    def buffers(i):
        if i == small:
            return list(sets[1])
        _, rows, groups, _ = pieces[i]
        height, slot = rows * groups, i % slots
        views = []
        for k, ref in enumerate(sets[0]):
            arriving = k in (1, 3) or (k >= 5 and (k - 5) % 3 == 2)
            lead = (slice(None),) * (len(ref.shape) - 3)
            views.append(ref.at[(i if arriving else slot, *lead, pl.ds(0, height), slice(None))])
        return views

    bufs = [buffers(i) for i in range(n)]
    orders = [upper if i % 2 == 0 else upper[::-1] for i in range(n)]
    pushed, drained, waits, stores = {}, set(), [None] * n, {}

    def push(i, at, src, dst, device_id):
        copy = pltpu.make_async_remote_copy(
            src_ref=src,
            dst_ref=dst,
            send_sem=send.at[i, at],
            recv_sem=recv.at[i, at],
            device_id=device_id,
            device_id_type=MESH,
        )
        copy.start()
        pushed[(i, at)] = copy
        return copy

    def drain(i, *ats):
        for at in ats:
            if i >= 0 and i != small and (i, at) in pushed and (i, at) not in drained:
                pushed[(i, at)].wait_send()
                drained.add((i, at))

    ready = plan["ready"]
    jobs = [(i, *job) for i in range(ready, n - 1) for job in pieces[i][3]]
    loads = {}

    def fetch(j):
        if j < len(jobs):
            _, _, right, lo, cols, _ = jobs[j]
            loads[j] = [
                pltpu.make_async_copy(
                    rights[right * micros + m].at[:, pl.ds(lo, cols)],
                    right_buf.at[j % 2, m, :, pl.ds(0, cols)],
                    right_sem.at[j % 2, m],
                )
                for m in range(micros)
            ]
            for copy in loads[j]:
                copy.start()

    left_waited = set()
    left_loads = [
        [
            pltpu.make_async_copy(lefts[a * micros + m], left_bufs[a].at[m], left_sem.at[a, m])
            for m in range(micros)
        ]
        for a in range(n_left)
    ]
    small_load = pltpu.make_async_copy(small_ref, sets[1][0], load_sem)
    small_load.start()
    lead = (slice(None),) * (bits + 1)
    ready_loads = []
    for i in range(ready):
        _, rows, groups, piece_jobs = pieces[i]
        ready_loads.append(
            [
                pltpu.make_async_copy(
                    ready_ref.at[(*lead, slice(None), pl.ds(piece_jobs[0][2] + g * lane, lane))],
                    bufs[i][0].at[(*lead, pl.ds(g * rows, rows), slice(None))],
                    ready_sem.at[i, g],
                )
                for g in range(groups)
            ]
        )
        for copy in ready_loads[i]:
            copy.start()
    for a in range(n_left):
        for copy in left_loads[a]:
            copy.start()
        if a < 2:
            fetch(a)
    greet(dp_count, bits)

    def make(i):
        _, rows, groups, piece_jobs = pieces[i]
        made = bufs[i][0]
        drain(i - slots, 0)
        for j, job in enumerate(jobs):
            if job[0] != i:
                continue
            _, left, right, lo, cols, at_group = job
            if left not in left_waited:
                for copy in left_loads[left]:
                    copy.wait()
                left_waited.add(left)
            for copy in loads[j]:
                copy.wait()
            height = rows << bits

            def tile(p, carry, left=left, cols=cols, at_group=at_group, j=j, height=height):
                total = None
                for m in range(left_bufs[left].shape[0]):
                    part = rows_inner(
                        left_bufs[left][m, :, pl.ds(pl.multiple_of(p * height, 128), height)],
                        right_buf[j % 2, m, :, :cols],
                    )
                    total = part if total is None else total + part
                total = total.astype(bf16)
                for g in range(cols // lane):
                    block = total[:, g * lane : (g + 1) * lane].reshape(*(2,) * bits, rows, lane)
                    lead = (slice(None),) * bits
                    made[(p, *lead, pl.ds((at_group + g) * rows, rows), slice(None))] = block
                return carry

            lax.fori_loop(0, dp_count, tile, 0)
            fetch(j + 2)

    def first(i):
        made, got = bufs[i][0], bufs[i][1]
        if i == small:
            small_load.wait()
        elif i < ready:
            for copy in ready_loads[i]:
                copy.wait()
        else:
            make(i)
        lead = (slice(None),) * bits
        waits[i] = push(i, 0, made.at[(*lead, 1 - my[0])], got, {"fsdp": flip(f, 0)})

    def held(i, s):
        waits[i].wait_recv()
        if s == 0:
            lead = (slice(None),) * bits
            return bufs[i][0].at[(*lead, my[0])], bufs[i][1]
        return bufs[i][5 + 3 * (s - 1)], bufs[i][5 + 3 * (s - 1) + 2]

    def middle(i, s):
        own, more = held(i, s - 1)
        b = orders[i][s - 1]
        left = [q for q in upper if q not in orders[i][: s - 1]]
        kept, sent, arriving = bufs[i][5 + 3 * (s - 1) : 8 + 3 * (s - 1)]

        def side(value):
            return (slice(None),) + tuple(value if q == b else slice(None) for q in left)

        drain(i - slots, s)
        theirs, mine = side(1 - my[b]), side(my[b])
        sent[...] = (own[theirs].astype(f32) + more[theirs].astype(f32)).astype(sent.dtype)
        waits[i] = push(i, s, sent, arriving, {"fsdp": flip(f, b)})
        kept[...] = own[mine].astype(f32) + more[mine].astype(f32)

    def last(i):
        own, more = held(i, bits - 1)
        to_dp, from_dp = bufs[i][2], bufs[i][3]
        drain(i - slots, *range(bits, bits + dp_count - 1))
        copies = []
        for o in near_first(dp_count)[1:]:
            peer = lax.rem(d + o, dp_count)
            to_dp[o - 1] = (own[peer] + more[peer].astype(f32)).astype(to_dp.dtype)
            copies.append(
                push(i, bits - 1 + o, to_dp.at[o - 1], from_dp.at[o - 1], {"dp": peer})
            )
        waits[i] = copies
        for store in stores.pop(i - slots, []):
            store.wait()
        bufs[i][4][...] = own[d] + more[d].astype(f32)

    def finish(i):
        result, from_dp = bufs[i][4], bufs[i][3]
        for copy in waits[i]:
            copy.wait_recv()
        total = result[...]
        for o in range(1, dp_count):
            total = total + from_dp[o - 1].astype(f32)
        result[...] = total
        out, rows, groups, piece_jobs = pieces[i]
        stores[i] = []
        if i == small:
            stores[i].append(pltpu.make_async_copy(result, outs[out], store_sem.at[i, 0]))
        else:
            lo = piece_jobs[0][2]
            for g in range(groups):
                stores[i].append(
                    pltpu.make_async_copy(
                        result.at[pl.ds(g * rows, rows)],
                        outs[out].at[:, pl.ds(lo + g * lane, lane)],
                        store_sem.at[i, g],
                    )
                )
        for store in stores[i]:
            store.start()

    for t in range((n + 1) // 2 + bits + 1):
        for s in (*range(1, bits + 2), 0):
            for i in range(2 * (t - s), min(2 * (t - s) + 2, n)):
                if i < 0:
                    continue
                if s == 0:
                    first(i)
                elif s < bits:
                    middle(i, s)
                elif s == bits:
                    last(i)
                else:
                    finish(i)
    for key, copy in pushed.items():
        if key not in drained:
            copy.wait_send()
    for group in stores.values():
        for store in group:
            store.wait()


def product_scatter(lefts, rights, ready, small, collective_id):
    dp_count, fsdp_count = lax.axis_size("dp"), lax.axis_size("fsdp")
    bits = fsdp_count.bit_length() - 1
    devices = dp_count * fsdp_count
    lane, slots, height = 256, 4, 96
    unique = []
    for left in lefts:
        if not any(left is u for u in unique):
            unique.append(left)
    pieces = []
    for k, (left, right) in enumerate(zip(lefts, rights)):
        at = next(a for a, u in enumerate(unique) if u is left)
        rows, width = left[0].shape[1] // devices, right[0].shape[1]
        per_piece = min(height // rows, width // lane)
        for lo in range(0, width, per_piece * lane):
            groups = min(per_piece, (width - lo) // lane)
            jobs = [
                (at, k, lo + g * lane, min(3, groups - g) * lane, g) for g in range(0, groups, 3)
            ]
            pieces.append((k, rows, groups, jobs))
    pieces.append((len(lefts), small.shape[1], 1, []))
    n = len(pieces)
    plan = {
        "pieces": pieces,
        "slots": slots,
        "lane": lane,
        "outputs": len(lefts) + 1,
        "micros": len(lefts[0]),
        "ready": sum(1 for k, _, _, jobs in pieces[:-1] if k == 0 and jobs[-1][2] + jobs[-1][3] <= ready.shape[1]),
    }

    def buffer_set(count, lead, rows, columns, dtype):
        def shaped(many, *dims):
            return (many, *dims, rows, columns) if lead else (*dims, rows, columns)

        halved = [(2,) * (bits - 1 - s) for s in range(bits)]
        result = [
            pltpu.VMEM(shaped(slots, dp_count, *(2,) * bits), dtype),
            pltpu.VMEM(shaped(count, dp_count, *halved[0]), dtype),
            pltpu.VMEM(shaped(slots, dp_count - 1), dtype),
            pltpu.VMEM(shaped(count, dp_count - 1), dtype),
            pltpu.VMEM(shaped(slots), f32),
        ]
        for s in range(1, bits):
            result += [
                pltpu.VMEM(shaped(slots, dp_count, *halved[s]), f32),
                pltpu.VMEM(shaped(slots, dp_count, *halved[s]), dtype),
                pltpu.VMEM(shaped(count, dp_count, *halved[s]), dtype),
            ]
        return result

    micro_count, rows = len(lefts[0]), lefts[0][0].shape[0]
    steps = bits - 1 + dp_count
    small = small.reshape(dp_count, *(2,) * bits, *small.shape[1:])
    ready = ready.reshape(dp_count, *(2,) * bits, -1, ready.shape[1])
    widths = [(a[0].shape[1], b[0].shape[1]) for a, b in zip(lefts, rights)]
    flops = sum(2 * micro_count * rows * a * b for a, b in widths)
    return pl.pallas_call(
        functools.partial(product_scatter_body, dp_count, bits, plan, len(unique), len(rights)),
        out_shape=[jax.ShapeDtypeStruct((a // devices, b), f32) for a, b in widths]
        + [jax.ShapeDtypeStruct(small.shape[-2:], f32)],
        in_specs=[ANY] * ((len(unique) + len(rights)) * micro_count + 2),
        out_specs=[ANY] * (len(lefts) + 1),
        scratch_shapes=[pltpu.VMEM((micro_count, *u[0].shape), bf16) for u in unique]
        + [
            pltpu.VMEM((2, micro_count, rows, 3 * lane), bf16),
            pltpu.SemaphoreType.DMA((len(unique), micro_count)),
            pltpu.SemaphoreType.DMA((2, micro_count)),
            pltpu.SemaphoreType.DMA,
            pltpu.SemaphoreType.DMA((slots, height // 16)),
            pltpu.SemaphoreType.DMA((n, steps)),
            pltpu.SemaphoreType.DMA((n, steps)),
            pltpu.SemaphoreType.DMA((n, height // 16)),
        ]
        + buffer_set(n - 1, True, height, lane, bf16)
        + buffer_set(1, False, *small.shape[-2:], f32),
        compiler_params=pltpu.CompilerParams(
            collective_id=collective_id, has_side_effects=True, vmem_limit_bytes=62 << 20
        ),
        cost_estimate=pl.CostEstimate(flops=flops, bytes_accessed=100 << 20, transcendentals=0),
    )(*[x for u in unique for x in u], *[x for r in rights for x in r], ready, small)


def weight_grad_body(n, *refs):
    lefts, rights, out_ref = refs[:n], refs[n : 2 * n], refs[2 * n]
    total = rows_inner(lefts[0][...], rights[0][...])
    for left, right in zip(lefts[1:], rights[1:]):
        total = total + rows_inner(left[...], right[...])
    out_ref[...] = total.astype(out_ref.dtype)


def weight_grad(lefts, rights, row_tile, width=None):
    n, (rows, height), width = len(lefts), lefts[0].shape, width or rights[0].shape[1]
    return pl.pallas_call(
        functools.partial(weight_grad_body, n),
        grid=(height // row_tile,),
        out_shape=jax.ShapeDtypeStruct((height, width), bf16),
        in_specs=[pl.BlockSpec((rows, row_tile), lambda i: (0, i))] * n + [whole((rows, width))] * n,
        out_specs=pl.BlockSpec((row_tile, width), lambda i: (i, 0)),
        compiler_params=params(),
        cost_estimate=pl.CostEstimate(
            flops=2 * n * rows * height * width,
            bytes_accessed=2 * (n * rows * (height + width) + height * width),
            transcendentals=0,
        ),
    )(*lefts, *rights)


def fourier_table(chunk):
    freq = np.arange(chunk)[:, None]
    time = np.arange(chunk)[None, :]
    angle = (freq * time % (2 * chunk)) * (np.pi / chunk)
    sines = -np.sin(angle)
    sines[0] = 1.0 - 2.0 * (np.arange(chunk) % 2)
    table = np.concatenate([np.cos(angle), sines], axis=0)
    scaling = np.full((2 * chunk, 1), 1.0 / chunk)
    scaling[0] = scaling[chunk] = 0.5 / chunk
    sign = np.tile(1.0 - 2.0 * (np.arange(chunk) % 2), 2)
    sign[chunk] = 1.0 - 2.0 * (chunk % 2)
    return table.astype(np.float32), (table * scaling).astype(np.float32), sign.astype(np.float32)


def high_and_low(table):
    high = table.astype(jnp.bfloat16)
    return np.stack([high, (table - high.astype(np.float32)).astype(jnp.bfloat16)])


def spectrum(table_ref, values):
    return matmul(table_ref[0], values) + matmul(table_ref[1], values)


def to_time(inverse_ref, spec):
    high = spec.astype(bf16)
    low = (spec - high.astype(f32)).astype(bf16)
    return (
        rows_inner(inverse_ref[0], high)
        + rows_inner(inverse_ref[1], high)
        + rows_inner(inverse_ref[0], low)
    )


def packed_product(first, second, edge, conjugate):
    (a_re, a_im), (b_re, b_im) = first, second
    straight, crossed = a_re * b_re, a_im * b_im
    if conjugate:
        real = straight + jnp.where(edge, 0.0, crossed)
        imag = jnp.where(edge, crossed, a_re * b_im - a_im * b_re)
    else:
        real = straight - jnp.where(edge, 0.0, crossed)
        imag = jnp.where(edge, crossed, a_re * b_im + a_im * b_re)
    return real, imag


def pair_sum(pairs, edge, conjugate):
    real, imag = packed_product(*pairs[0], edge, conjugate)
    for first, second in pairs[1:]:
        more = packed_product(first, second, edge, conjugate)
        real, imag = real + more[0], imag + more[1]
    return real, imag


def halves(ref, block, at, chunk):
    return ref[block, :chunk, at], ref[block, chunk:, at]


def convolve_body(table_ref, inverse_ref, kernel_ref, rows_ref, out_ref, spec_ref, back_ref):
    blocks, chunk, columns = rows_ref.shape
    lanes = kernel_ref.shape[2]
    edge = lax.broadcasted_iota(jnp.int32, (chunk, lanes), 0) == 0
    for c in range(blocks):
        spec_ref[c] = spectrum(table_ref, rows_ref[c])
        for g in range(columns // lanes):
            at = slice(g * lanes, (g + 1) * lanes)
            everything = slice(None)
            real, imag = pair_sum(
                [
                    (halves(kernel_ref, k, everything, chunk), halves(spec_ref, c - k, at, chunk))
                    for k in range(c + 1)
                ],
                edge,
                False,
            )
            back_ref[:chunk, at], back_ref[chunk:, at] = real, imag
        out_ref[c] = to_time(inverse_ref, back_ref[...]).astype(out_ref.dtype)


def convolve_back_body(
    table_ref, inverse_ref, kernel_ref, rows_ref, grad_ref, out_ref, kernel_grad_ref,
    spec_ref, grad_spec_ref, back_ref,
):
    blocks, chunk, columns = rows_ref.shape
    lanes = kernel_ref.shape[2]
    edge = lax.broadcasted_iota(jnp.int32, (chunk, lanes), 0) == 0
    everything = slice(None)
    groups = [slice(g * lanes, (g + 1) * lanes) for g in range(columns // lanes)]
    for c in range(blocks):
        spec_ref[c] = spectrum(table_ref, rows_ref[c])
    for c in reversed(range(blocks)):
        grad_spec_ref[c] = spectrum(table_ref, grad_ref[c])
        for at in groups:
            real, imag = pair_sum(
                [
                    (
                        halves(kernel_ref, late - c, everything, chunk),
                        halves(grad_spec_ref, late, at, chunk),
                    )
                    for late in range(c, blocks)
                ],
                edge,
                True,
            )
            back_ref[:chunk, at], back_ref[chunk:, at] = real, imag
        out_ref[c] = to_time(inverse_ref, back_ref[...]).astype(out_ref.dtype)
    for k in range(blocks):
        real, imag = pair_sum(
            [
                (halves(spec_ref, c - k, at, chunk), halves(grad_spec_ref, c, at, chunk))
                for c in range(k, blocks)
                for at in groups
            ],
            edge,
            True,
        )
        kernel_grad_ref[k, :chunk], kernel_grad_ref[k, chunk:] = real, imag


def kernel_factors(decay, frequency, log_step, length):
    fine = 32
    coarse = length // fine
    step_size = jnp.exp(log_step)[:, None]
    real = (step_size * decay)[:, None, :]
    imag = (step_size * frequency)[:, None, :]
    far = (jnp.arange(coarse, dtype=jnp.int32) * fine).astype(f32)[None, :, None]
    near = jnp.arange(fine, dtype=jnp.int32).astype(f32)[None, :, None]
    far_damp, near_damp = jnp.exp(real * far), jnp.exp(real * near)
    return (
        (far_damp * jnp.cos(imag * far), far_damp * jnp.sin(imag * far)),
        (near_damp * jnp.cos(imag * near), near_damp * jnp.sin(imag * near)),
        step_size,
    )


def kernel_forward(weight_pair, factors):
    (far_re, far_im), (near_re, near_im), _ = factors
    w_re, w_im = weight_pair[0][:, None, :], weight_pair[1][:, None, :]
    left = jnp.concatenate([far_re, -far_im], axis=2)
    right = jnp.concatenate(
        [w_re * near_re - w_im * near_im, w_re * near_im + w_im * near_re], axis=2
    )
    rows = jnp.einsum("han,hbn->hab", left, right, precision=highest)
    return rows.reshape(rows.shape[0], -1)


def kernel_backward(grad_rows, weight_pair, decay, frequency, factors):
    (far_re, far_im), (near_re, near_im), step_size = factors
    channels, coarse, states = far_re.shape
    fine = near_re.shape[1]
    tiles = grad_rows.reshape(channels, coarse, fine)
    near_index = jnp.arange(fine, dtype=jnp.int32).astype(f32)
    far_index = (jnp.arange(coarse, dtype=jnp.int32) * fine).astype(f32)[None, :, None]
    stacked = jnp.concatenate([tiles, tiles * near_index], axis=1)
    part = jnp.einsum(
        "hab,hbn->han", stacked, jnp.concatenate([near_re, near_im], axis=2), precision=highest
    )
    u_re, u_im = part[:, :coarse, :states], part[:, :coarse, states:]
    v_re = part[:, coarse:, :states] + far_index * u_re
    v_im = part[:, coarse:, states:] + far_index * u_im
    s_re = jnp.sum(far_re * u_re - far_im * u_im, axis=1)
    s_im = jnp.sum(far_re * u_im + far_im * u_re, axis=1)
    t_re = jnp.sum(far_re * v_re - far_im * v_im, axis=1)
    t_im = jnp.sum(far_re * v_im + far_im * v_re, axis=1)
    w_re, w_im = weight_pair[0], weight_pair[1]
    along_re = step_size * (w_re * t_re - w_im * t_im)
    along_im = -step_size * (w_re * t_im + w_im * t_re)
    return (
        jnp.stack([s_re, -s_im]),
        along_re,
        along_im,
        jnp.sum(decay * along_re + frequency * along_im, axis=1),
    )


def shards(
    tokens,
    cotangent,
    teacher,
    lengths,
    dealing,
    loss_mask,
    norm_gain,
    norm_bias,
    gate_weight,
    reduce_weight,
    state_weight,
    decay_rate,
    frequency,
    log_step,
    expand_weight,
    out_weight,
):
    dp_count, fsdp_count = lax.axis_size("dp"), lax.axis_size("fsdp")
    devices = dp_count * fsdp_count
    group_index = lax.axis_index("fsdp")
    dp_place = lax.axis_index("dp")
    micro_count, seqs, chunk, width = tokens.shape
    rows = seqs * chunk
    seq_length = chunk * dp_count
    gate_width = gate_weight.shape[1]
    reduced_width = reduce_weight.shape[1]
    own = reduced_width // dp_count
    lanes = max(own, 128)
    share = norm_gain.shape[0]
    micros = range(micro_count)
    direct = own % 128 == 0

    small = jnp.zeros((16, 256), bf16).at[0, :share].set(norm_gain).at[1, :share].set(norm_bias)
    mask_rows = loss_mask.reshape(micro_count, dp_count, chunk).transpose(1, 0, 2)
    mask_rows = jnp.pad(mask_rows, ((0, 0), (0, 8 - micro_count), (0, 0)))
    teacher_rows = teacher.reshape(micro_count, dp_count, chunk, width)
    w_gate, w_reduce, small, *swapped = gather_all(
        [gate_weight, reduce_weight, small],
        [(0, mask_rows[None]), *[(m, teacher_rows) for m in micros[1:]]],
        1,
    )
    masked = swapped[0].transpose(1, 0, 2)[:micro_count]
    w_gate = w_gate.reshape(width, gate_width)
    w_reduce = w_reduce.reshape(width, reduced_width)
    gain_row = small[:, :, 0, :share].reshape(1, width).astype(f32)
    bias_row = small[:, :, 1, :share].reshape(1, width).astype(f32)

    per_block = max(1, 512 // chunk)
    steps = seqs // per_block
    middle_block = max(1, 256 // chunk)
    middle_steps = seqs // middle_block

    def row_spec(columns, count=per_block):
        return pl.BlockSpec((count * chunk, columns), lambda i, *_: (i, 0))

    def shared(shape, block):
        return pl.BlockSpec(shape, lambda i, *_: block, pipeline_mode=pl.Buffered(1))

    lane_shape = (dp_count, chunk, seqs * own)
    if not direct:
        lane_shape = (1, rows, reduced_width)

    def dims(count):
        return (count, chunk, own) if direct else (1, count * chunk, reduced_width)

    def lane_spec(count):
        if direct:
            return pl.BlockSpec((dp_count, chunk, count * own), lambda i, *_: (0, 0, i))
        return pl.BlockSpec((1, count * chunk, reduced_width), lambda i, *_: (0, i, 0))

    def tokens_spec(m, count):
        return pl.BlockSpec((None, count, chunk, width), lambda i, *_: (m, i, 0, 0))

    def send_lanes(values):
        if not direct:
            values = values.reshape(seqs, chunk, dp_count, own).transpose(2, 1, 0, 3)
            values = values.reshape(dp_count, chunk, seqs * own)
        return exchange(values)

    def receive_lanes(values):
        values = exchange(values)
        if not direct:
            values = values.reshape(dp_count, chunk, seqs, own).transpose(2, 1, 0, 3)
            values = values.reshape(1, rows, reduced_width)
        return values

    def reduce_rows(m, gain_row):
        return pl.pallas_call(
            functools.partial(reduce_body, dims(per_block)),
            grid=(steps,),
            out_shape=[
                jax.ShapeDtypeStruct((rows, width), bf16),
                jax.ShapeDtypeStruct(lane_shape, bf16),
                jax.ShapeDtypeStruct((rows, reduced_width), f32),
            ],
            in_specs=[
                tokens_spec(m, per_block),
                whole((1, width)),
                whole((1, width)),
                whole((width, reduced_width)),
            ],
            out_specs=[row_spec(width), lane_spec(per_block), row_spec(reduced_width)],
            compiler_params=params(),
            cost_estimate=pl.CostEstimate(
                flops=2 * rows * width * reduced_width,
                bytes_accessed=8 * rows * width,
                transcendentals=2 * rows * reduced_width,
            ),
        )(tokens, gain_row, bias_row, w_reduce)

    local_ids = group_index * seqs + jnp.arange(seqs, dtype=jnp.int32)
    targets = jnp.take(dealing, local_ids, axis=1)
    own_lengths = jnp.take(lengths, local_ids, axis=1)
    positions = dp_place * chunk + jnp.arange(chunk, dtype=jnp.int32)
    valid = (positions[None, None, :] < own_lengths[:, :, None]).astype(f32)
    keep = jnp.take_along_axis(masked, targets[:, :, None], axis=1).astype(f32) * valid
    own_count = jnp.sum(keep)
    row_weights = jnp.stack([valid, keep], axis=-1).reshape(micro_count, rows, 2)
    counts = jnp.full((8, 256), own_count, f32)
    row_weights = [row_weights[m] for m in micros]

    reduced_rows = [reduce_rows(0, gain_row)]
    held = lax.optimization_barrier((decay_rate, frequency, log_step, reduced_rows[0][1]))
    factors = kernel_factors(*held[:3], seq_length)
    own_kernel = kernel_forward(state_weight, factors)
    for m in micros[1:]:
        later_gain, own_kernel, row_weights, targets, counts = lax.optimization_barrier(
            (gain_row, own_kernel, row_weights, targets, counts)
        )
        reduced_rows.append(reduce_rows(m, later_gain))
    normed, lanes_out, slope_reduced = zip(*reduced_rows)
    lanes_in = [send_lanes(x) for x in lanes_out]


    table_np, inverse_np, sign_np = fourier_table(chunk)
    sign = jnp.asarray(sign_np)[:, None]
    table2, inverse2 = jnp.asarray(high_and_low(table_np)), jnp.asarray(high_and_low(inverse_np))
    kernel = lax.all_gather(own_kernel, "fsdp", axis=0, tiled=True)
    segments = jnp.einsum(
        "kt,hct->ckh", jnp.asarray(table_np), kernel.reshape(own, dp_count, chunk), precision=highest
    )
    previous = jnp.concatenate([jnp.zeros_like(segments[:1]), segments[:-1]], axis=0)
    kernel_spec = jnp.tile(segments + sign * previous, (1, 1, lanes // own))

    blocks = (dp_count, chunk, seqs * own)
    spec_scratch = pltpu.VMEM((dp_count, 2 * chunk, seqs * own), f32)
    back_scratch = pltpu.VMEM((2 * chunk, seqs * own), f32)
    transform_flops = 8 * chunk * chunk * dp_count * seqs * own

    def convolve(values):
        return pl.pallas_call(
            convolve_body,
            out_shape=jax.ShapeDtypeStruct(blocks, bf16),
            scratch_shapes=[spec_scratch, back_scratch],
            compiler_params=params(),
            cost_estimate=pl.CostEstimate(
                flops=5 * transform_flops // 2, bytes_accessed=8 << 20, transcendentals=0
            ),
        )(table2, inverse2, kernel_spec, values)

    def convolve_back(values, grads):
        return pl.pallas_call(
            convolve_back_body,
            out_shape=[
                jax.ShapeDtypeStruct(blocks, bf16),
                jax.ShapeDtypeStruct((dp_count, 2 * chunk, lanes), f32),
            ],
            scratch_shapes=[spec_scratch, spec_scratch, back_scratch],
            compiler_params=params(),
            cost_estimate=pl.CostEstimate(
                flops=7 * transform_flops // 2, bytes_accessed=8 << 20, transcendentals=0
            ),
        )(table2, inverse2, kernel_spec, values, grads)

    convolved = [convolve(x) for x in lanes_in]
    late = lax.optimization_barrier((expand_weight, out_weight, *convolved))
    w_expand, w_out, counts, *more, gate, slope = gather_all(
        [late[0], late[1], counts],
        [(0, teacher_rows)],
        2,
        gate_work(normed, w_gate),
    )
    teach = [*more, *swapped[1:]]
    w_expand = w_expand.reshape(reduced_width, gate_width)
    w_out = w_out.reshape(gate_width, width)
    count = jnp.sum(counts[:, :, 0, 0])
    error_scale = (2.0 / (width * count)).reshape(1)
    mixed = [receive_lanes(x) for x in convolved]
    def middle_rows(m, *earlier):
        teach_specs = [
            pl.BlockSpec((1, chunk, width), functools.partial(teach_block, s)) for s in range(middle_block)
        ]
        gate_spec = pl.BlockSpec(
            (middle_block * chunk, gate_width), lambda i, *_: (m * middle_steps + i, 0)
        )
        wide, narrow = row_spec(gate_width, middle_block), row_spec(width, middle_block)
        return pl.pallas_call(
            functools.partial(middle_body, dims(middle_block), middle_block, 768),
            grid_spec=pltpu.PrefetchScalarGridSpec(
                num_scalar_prefetch=2,
                grid=(middle_steps,),
                in_specs=[
                    lane_spec(middle_block),
                    gate_spec,
                    gate_spec,
                    shared((reduced_width, gate_width), (0, 0)),
                    shared((gate_width, width), (0, 0)),
                    tokens_spec(m, middle_block),
                    tokens_spec(m, middle_block),
                    row_spec(2, middle_block),
                    *teach_specs,
                    *[ANY] * len(earlier),
                ],
                out_specs=[
                    row_spec(reduced_width, middle_block),
                    wide,
                    narrow,
                    wide,
                    wide,
                    tokens_spec(m, middle_block),
                    narrow,
                    pl.BlockSpec((1, 8, width), lambda i, *_: (i, 0, 0)),
                    lane_spec(middle_block),
                ],
                scratch_shapes=[pltpu.VMEM((middle_block * chunk, gate_width), f32)],
            ),
            out_shape=[
                jax.ShapeDtypeStruct((rows, reduced_width), bf16),
                jax.ShapeDtypeStruct((rows, gate_width), bf16),
                jax.ShapeDtypeStruct((rows, width), bf16),
                jax.ShapeDtypeStruct((rows, gate_width), bf16),
                jax.ShapeDtypeStruct((rows, gate_width), bf16),
                jax.ShapeDtypeStruct(tokens.shape, bf16),
                jax.ShapeDtypeStruct((rows, width), bf16),
                jax.ShapeDtypeStruct((middle_steps, 8, width), f32),
                jax.ShapeDtypeStruct(lane_shape, bf16),
            ],
            input_output_aliases={10 + middle_block: 5} if earlier else {},
            compiler_params=params(),
            cost_estimate=pl.CostEstimate(
                flops=4 * rows * gate_width * (width + reduced_width),
                bytes_accessed=10 * rows * gate_width + 16 * rows * width,
                transcendentals=0,
            ),
        )(
            targets[m], error_scale, mixed[m], gate, slope, w_expand, w_out, tokens, cotangent,
            row_weights[m], *[teach[m]] * middle_block, *earlier,
        )

    def teach_block(s, i, order, scale):
        return (order[i * middle_block + s], 0, 0)

    def input_rows(m, back, gate_grad, full_grad, *earlier):
        eight = pl.BlockSpec((1, 8, width), lambda i, *_: (i, 0, 0))
        return pl.pallas_call(
            functools.partial(input_body, dims(per_block)),
            grid=(steps,),
            in_specs=[
                lane_spec(per_block),
                row_spec(reduced_width),
                row_spec(gate_width),
                shared((width, gate_width), (0, 0)),
                shared((width, reduced_width), (0, 0)),
                tokens_spec(m, per_block),
                whole((1, width)),
                row_spec(width),
                *[ANY] * len(earlier),
            ],
            out_specs=[tokens_spec(m, per_block), row_spec(reduced_width), eight, eight],
            out_shape=[
                jax.ShapeDtypeStruct(tokens.shape, bf16),
                jax.ShapeDtypeStruct((rows, reduced_width), bf16),
                jax.ShapeDtypeStruct((steps, 8, width), f32),
                jax.ShapeDtypeStruct((steps, 8, width), f32),
            ],
            scratch_shapes=[pltpu.VMEM((per_block * chunk, reduced_width), bf16)],
            input_output_aliases={8: 0} if earlier else {},
            compiler_params=params(),
            cost_estimate=pl.CostEstimate(
                flops=2 * rows * width * (gate_width + reduced_width),
                bytes_accessed=4 * rows * gate_width + 8 * rows * width,
                transcendentals=0,
            ),
        )(back, slope_reduced[m], gate_grad, w_gate, w_reduce, tokens, gain_row, full_grad, *earlier)

    middle = []
    for m in micros:
        middle.append(middle_rows(m, *[x[5] for x in middle[-1:]]))
    outputs = middle[-1][5]
    state_out, product, branch_grad, expanded_grad, gate_grad, _, full_grad, error_rows, lane_grad = zip(*middle)
    grads_in = [send_lanes(x) for x in lane_grad]
    back, kernel_grads = zip(*[convolve_back(lanes_in[m], grads_in[m]) for m in micros])
    ready = weight_grad(normed, gate_grad, 256, gate_width // 2)
    held_back, ready = lax.optimization_barrier((back[0], ready))
    back = [receive_lanes(x) for x in (held_back, *back[1:])]
    ends = []
    for m in micros:
        ends.append(input_rows(m, back[m], gate_grad[m], full_grad[m], *[x[0] for x in ends[-1:]]))
    returned = ends[-1][0]
    _, reduced_grad, gain_rows, bias_rows = zip(*ends)

    kernel_total = sum(kernel_grads)
    if not direct:
        kernel_total = kernel_total.reshape(dp_count, 2 * chunk, lanes // own, own).sum(axis=2)
    following = jnp.concatenate([kernel_total[1:], jnp.zeros_like(kernel_total[:1])], axis=0)
    kernel_grad = jnp.einsum(
        "kt,ckh->hct", jnp.asarray(inverse_np), kernel_total + sign * following, precision=highest
    ).reshape(own, seq_length)
    kernel_grad, _ = lax.optimization_barrier((kernel_grad, reduced_grad))
    kernel_grad = lax.psum_scatter(kernel_grad, "fsdp", scatter_dimension=0, tiled=True)
    pair_grad, decay_grad, frequency_grad, step_grad = kernel_backward(
        kernel_grad, state_weight, decay_rate, frequency, factors
    )

    gain_total = jnp.sum(sum(gain_rows), axis=(0, 1)).reshape(devices, 1, share)
    bias_total = jnp.sum(sum(bias_rows), axis=(0, 1)).reshape(devices, 1, share)
    error_total = jnp.full((devices, 1, share), jnp.sum(sum(error_rows)))
    sums = jnp.concatenate([gain_total, bias_total, error_total], axis=1)
    sums = jnp.pad(sums, ((0, 0), (0, 5), (0, 128 - share)))
    pairs = [
        (normed, gate_grad),
        (state_out, expanded_grad),
        (product, branch_grad),
        (normed, reduced_grad),
    ]
    if all(left[0].shape[1] // devices % 16 == 0 for left, _ in pairs):
        lefts, rights = zip(*pairs)
        gate_sum, expand_sum, out_sum, reduce_sum, sums = product_scatter(
            lefts, rights, ready, sums, 3
        )
    else:
        made = [weight_grad(left, right, 256) for left, right in pairs]
        gate_sum, expand_sum, out_sum, reduce_sum, sums = scatter_all(
            [x.reshape(devices, -1, x.shape[1]) for x in made] + [sums], [4, 2, 4, 1, 1], 3
        )
    loss_value = sums[2, 0] / (width * count)
    return (
        outputs,
        loss_value,
        returned,
        sums[0, :share],
        sums[1, :share],
        gate_sum,
        reduce_sum,
        pair_grad,
        decay_grad,
        frequency_grad,
        step_grad,
        expand_sum,
        out_sum,
    )


def solution(mesh):
    in_specs = (
        P(None, "fsdp", "dp", None),
        P(None, "fsdp", "dp", None),
        P(None, ("dp", "fsdp"), None, None),
        P(),
        P(),
        P(None, ("dp", "fsdp"), None),
        P(("dp", "fsdp")),
        P(("dp", "fsdp")),
        P(("dp", "fsdp"), None),
        P(("dp", "fsdp"), None),
        P(None, ("dp", "fsdp"), None),
        P(("dp", "fsdp"), None),
        P(("dp", "fsdp"), None),
        P(("dp", "fsdp")),
        P(("dp", "fsdp"), None),
        P(("dp", "fsdp"), None),
    )
    out_specs = (
        P(None, "fsdp", "dp", None),
        P(),
        P(None, "fsdp", "dp", None),
        P(("dp", "fsdp")),
        P(("dp", "fsdp")),
        P(("dp", "fsdp"), None),
        P(("dp", "fsdp"), None),
        P(None, ("dp", "fsdp"), None),
        P(("dp", "fsdp"), None),
        P(("dp", "fsdp"), None),
        P(("dp", "fsdp")),
        P(("dp", "fsdp"), None),
        P(("dp", "fsdp"), None),
    )
    return jax.shard_map(shards, mesh=mesh, in_specs=in_specs, out_specs=out_specs, check_vma=False)
```

```python
import functools

import numpy as np
import jax
import jax.numpy as jnp
from jax import lax
from jax.experimental import pallas as pl
from jax.experimental.pallas import tpu as pltpu
from jax.sharding import PartitionSpec as P

epsilon = 1e-05
high = lax.Precision.HIGH
bf16 = jnp.bfloat16
f32 = jnp.float32
MESH = pl.DeviceIdType.MESH
ANY = pl.BlockSpec(memory_space=pltpu.HBM)


def bit_of(index, bit):
    return lax.rem(lax.div(index, 1 << bit), 2)


def flip(index, bit):
    return index + (1 << bit) - 2 * (1 << bit) * bit_of(index, bit)


def greet(dp_count, bits):
    d, f = lax.axis_index("dp"), lax.axis_index("fsdp")
    barrier = pltpu.get_barrier_semaphore()
    for o in range(1, dp_count):
        peer = lax.rem(d + o, dp_count)
        pl.semaphore_signal(barrier, inc=1, device_id={"dp": peer}, device_id_type=MESH)
    for b in range(bits):
        pl.semaphore_signal(barrier, inc=1, device_id={"fsdp": flip(f, b)}, device_id_type=MESH)
    pl.semaphore_wait(barrier, dp_count - 1 + bits)


def near_first(count):
    order = [0]
    for k in range(1, count // 2 + 1):
        order += [k] if k == count - k else [k, count - k]
    return order


def gather_body(dp_count, bits, n, leads, work, *refs):
    n_swap = len(leads)
    n_work_in, n_work_out = work[0] if work else (0, 0)
    moved = n + n_swap
    ins, refs = list(refs[:moved]), refs[moved:]
    for e, lead in enumerate(leads):
        ins[n + e] = ins[n + e].at[lead]
    work_ins, refs = refs[:n_work_in], refs[n_work_in:]
    outs, refs = refs[:moved], refs[moved:]
    work_outs, refs = refs[:n_work_out], refs[n_work_out:]
    z_send, z_recv, send, recv, own_sem, swap_send, swap_recv = refs[:7]
    begin, tick, end = work[1](work_ins, work_outs, refs[7:]) if work else (None, None, None)
    d, f = lax.axis_index("dp"), lax.axis_index("fsdp")
    cuts = []
    for x in ins[:n]:
        cut = x.shape[1] // 256 * 128
        cuts.append(((0, cut), (cut, x.shape[1] - cut)))
    order = near_first(dp_count)
    if work:
        begin()
    greet(dp_count, bits)
    own = [pltpu.make_async_copy(ins[a], outs[a].at[d, f], own_sem.at[a]) for a in range(n)]
    own += [
        pltpu.make_async_copy(ins[a].at[d], outs[a].at[d], own_sem.at[a])
        for a in range(n, n + n_swap)
    ]
    for copy in own:
        copy.start()
    started, arrived, waited = [], {}, set()

    def push(src, dst, send_sem, recv_sem, device_id):
        copy = pltpu.make_async_remote_copy(
            src_ref=src,
            dst_ref=dst,
            send_sem=send_sem,
            recv_sem=recv_sem,
            device_id=device_id,
            device_id_type=MESH,
        )
        copy.start()
        started.append(copy)
        return copy

    for o in order[1:]:
        for h in range(2):
            for a in range(n):
                lo, size = cuts[a][h]
                arrived[(o, 0, h, a)] = push(
                    ins[a].at[:, pl.ds(lo, size)],
                    outs[a].at[d, f, :, pl.ds(lo, size)],
                    z_send.at[o - 1, h, a],
                    z_recv.at[o - 1, h, a],
                    {"dp": lax.rem(d + o, dp_count)},
                )
    for copy in own:
        copy.wait()
    upper = list(range(1, bits))
    stages = [upper + [0], upper[::-1] + [0]]
    masks = [[[0]], [[0]]]
    for h in range(2):
        for s in range(bits):
            masks[h].append(masks[h][s] + [m ^ (1 << stages[h][s]) for m in masks[h][s]])
    slot, group = 0, 0
    for t in range(dp_count + bits - 1):
        for i in range(dp_count):
            s, o = t - i, order[i]
            if not 0 <= s < bits:
                continue
            if work:
                tick(group, dp_count * bits)
                group += 1
            for k in range(len(masks[0][s])):
                for h in range(2):
                    mask, b = masks[h][s][k], stages[h][s]
                    src_f = f
                    for bb in range(bits):
                        if mask >> bb & 1:
                            src_f = flip(src_f, bb)
                    for a in range(n):
                        key = (o, mask, h, a)
                        if key in arrived and key not in waited:
                            arrived[key].wait_recv()
                            waited.add(key)
                        lo, size = cuts[a][h]
                        src_d = lax.rem(d - o + dp_count, dp_count)
                        piece = outs[a].at[src_d, src_f, :, pl.ds(lo, size)]
                        arrived[(o, mask ^ (1 << b), h, a)] = push(
                            piece, piece, send.at[slot], recv.at[slot], {"fsdp": flip(f, b)}
                        )
                        slot += 1
        if t == 0:
            for o in order[1:]:
                peer = lax.rem(d + o, dp_count)
                for e in range(n_swap):
                    arrived[(o, e)] = push(
                        ins[n + e].at[peer],
                        outs[n + e].at[d],
                        swap_send.at[o - 1, e],
                        swap_recv.at[o - 1, e],
                        {"dp": peer},
                    )
    if work:
        end()
    for key, copy in arrived.items():
        if key not in waited:
            copy.wait_recv()
    for copy in started:
        copy.wait_send()


def gather_all(arrays, swaps, collective_id, work=None):
    work_in, work_out, work_scratch, work_body = work or ((), (), (), None)
    sizes = (len(work_in), len(work_out))
    leads, swaps = [lead for lead, _ in swaps], [x for _, x in swaps]
    dp_count, fsdp_count = lax.axis_size("dp"), lax.axis_size("fsdp")
    bits = fsdp_count.bit_length() - 1
    n, n_swap = len(arrays), len(swaps)
    slots = 2 * dp_count * (fsdp_count - 1) * n
    total = dp_count * fsdp_count * sum(x.size * x.dtype.itemsize for x in arrays)
    return pl.pallas_call(
        functools.partial(gather_body, dp_count, bits, n, leads, (sizes, work_body) if work else None),
        out_shape=[
            jax.ShapeDtypeStruct((dp_count, fsdp_count, *x.shape), x.dtype) for x in arrays
        ]
        + [jax.ShapeDtypeStruct(x.shape[1:], x.dtype) for x in swaps]
        + list(work_out),
        in_specs=[ANY] * (n + n_swap + sizes[0]),
        out_specs=[ANY] * (n + n_swap + sizes[1]),
        scratch_shapes=[
            pltpu.SemaphoreType.DMA((dp_count - 1, 2, n)),
            pltpu.SemaphoreType.DMA((dp_count - 1, 2, n)),
            pltpu.SemaphoreType.DMA((slots,)),
            pltpu.SemaphoreType.DMA((slots,)),
            pltpu.SemaphoreType.DMA((n + n_swap,)),
            pltpu.SemaphoreType.DMA((dp_count - 1, max(n_swap, 1))),
            pltpu.SemaphoreType.DMA((dp_count - 1, max(n_swap, 1))),
            *work_scratch,
        ],
        compiler_params=pltpu.CompilerParams(
            collective_id=collective_id, has_side_effects=True, vmem_limit_bytes=62 << 20
        ),
        cost_estimate=pl.CostEstimate(flops=0, bytes_accessed=20 * total, transcendentals=0),
    )(*arrays, *swaps, *work_in)


def scatter_body(dp_count, bits, pieces, kinds, *refs):
    n_in, n = len(kinds), len(pieces)
    ins, outs = refs[:n_in], refs[n_in : 2 * n_in]
    per = 6 + 2 * (bits - 1)
    scratch = [refs[2 * n_in + i * per : 2 * n_in + (i + 1) * per] for i in range(n)]
    load_sem, send, recv, store_sem = refs[2 * n_in + n * per :]
    d, f = lax.axis_index("dp"), lax.axis_index("fsdp")
    my = [bit_of(f, b) for b in range(bits)]
    upper = list(range(bits - 1, 0, -1))
    waits, fixed, ends = [None] * n, [{} for _ in range(n)], []
    greet(dp_count, bits)

    def region(i, other=None):
        return (slice(None),) + tuple(
            1 - my[b] if b == other else fixed[i].get(b, slice(None)) for b in upper
        )

    def push(i, at, src, dst, device_id):
        copy = pltpu.make_async_remote_copy(
            src_ref=src,
            dst_ref=dst,
            send_sem=send.at[i, at],
            recv_sem=recv.at[i, at],
            device_id=device_id,
            device_id_type=MESH,
        )
        copy.start()
        ends.append(copy)
        return copy

    def first(i):
        op, lo, cols = pieces[i]
        lead = (slice(None),) * bits
        own = ins[op].at[(*lead, my[0], slice(None), pl.ds(lo, cols))]
        other = ins[op].at[(*lead, 1 - my[0], slice(None), pl.ds(lo, cols))]
        load = pltpu.make_async_copy(own, scratch[i][0], load_sem.at[i])
        load.start()
        waits[i] = (load, push(i, 0, other, scratch[i][1], {"fsdp": flip(f, 0)}))

    def arrive(i, s):
        acc = scratch[i][2]
        if s == 0:
            waits[i][0].wait()
            waits[i][1].wait_recv()
            acc[...] = scratch[i][0][...].astype(f32) + scratch[i][1][...].astype(f32)
        else:
            waits[i].wait_recv()
            here = region(i)
            acc[here] = acc[here] + scratch[i][5 + 2 * s][...].astype(f32)

    def middle(i, s):
        arrive(i, s - 1)
        b = (upper if i % 2 == 0 else upper[::-1])[s - 1]
        out_buf, in_buf = scratch[i][4 + 2 * s], scratch[i][5 + 2 * s]
        out_buf[...] = scratch[i][2][region(i, b)].astype(out_buf.dtype)
        waits[i] = push(i, s, out_buf, in_buf, {"fsdp": flip(f, b)})
        fixed[i][b] = my[b]

    def last(i):
        arrive(i, bits - 1)
        out_buf, in_buf = scratch[i][3], scratch[i][4]
        waits[i] = []
        for o in near_first(dp_count)[1:]:
            peer = lax.rem(d + o, dp_count)
            out_buf[o - 1] = scratch[i][2][(peer, *region(i)[1:])].astype(out_buf.dtype)
            waits[i].append(
                push(i, bits - 1 + o, out_buf.at[o - 1], in_buf.at[o - 1], {"dp": peer})
            )

    def finish(i):
        op, lo, cols = pieces[i]
        for copy in waits[i]:
            copy.wait_recv()
        total = scratch[i][2][(d, *region(i)[1:])]
        for o in range(1, dp_count):
            total = total + scratch[i][4][o - 1].astype(f32)
        scratch[i][5][...] = total
        store = pltpu.make_async_copy(
            scratch[i][5], outs[op].at[:, pl.ds(lo, cols)], store_sem.at[i]
        )
        store.start()
        return store

    stores = []
    for t in range((n + 1) // 2 + bits + 1):
        for i in range(n):
            s = t - i // 2
            if s == 0:
                first(i)
            elif 1 <= s < bits:
                middle(i, s)
            elif s == bits:
                last(i)
            elif s == bits + 1:
                stores.append(finish(i))
    for copy in ends:
        copy.wait_send()
    for store in stores:
        store.wait()


def scatter_all(arrays, splits, collective_id):
    dp_count, fsdp_count = lax.axis_size("dp"), lax.axis_size("fsdp")
    bits = fsdp_count.bit_length() - 1
    arrays = [a.reshape(dp_count, *(2,) * bits, *a.shape[1:]) for a in arrays]
    pieces, scratch = [], []
    for op, (a, k) in enumerate(zip(arrays, splits)):
        rows, cols = a.shape[-2], a.shape[-1] // k
        half = (dp_count, *(2,) * (bits - 1), rows, cols)
        for j in range(k):
            pieces.append((op, j * cols, cols))
            scratch += [pltpu.VMEM(half, a.dtype)] * 2 + [pltpu.VMEM(half, f32)]
            scratch += [pltpu.VMEM((dp_count - 1, rows, cols), a.dtype)] * 2
            scratch += [pltpu.VMEM((rows, cols), f32)]
            for s in range(1, bits):
                shape = (dp_count, *(2,) * (bits - 1 - s), rows, cols)
                scratch += [pltpu.VMEM(shape, a.dtype)] * 2
    n, steps = len(pieces), bits - 1 + dp_count
    return pl.pallas_call(
        functools.partial(scatter_body, dp_count, bits, pieces, [a.dtype for a in arrays]),
        out_shape=[jax.ShapeDtypeStruct(a.shape[-2:], f32) for a in arrays],
        in_specs=[ANY] * len(arrays),
        out_specs=[ANY] * len(arrays),
        scratch_shapes=scratch
        + [
            pltpu.SemaphoreType.DMA((n,)),
            pltpu.SemaphoreType.DMA((n, steps)),
            pltpu.SemaphoreType.DMA((n, steps)),
            pltpu.SemaphoreType.DMA((n,)),
        ],
        compiler_params=pltpu.CompilerParams(
            collective_id=collective_id, has_side_effects=True, vmem_limit_bytes=60 << 20
        ),
    )(*arrays)


def exchange(values):
    return lax.all_to_all(values, "dp", split_axis=0, concat_axis=0, tiled=True)


def params(limit_mib=60):
    return pltpu.CompilerParams(vmem_limit_bytes=limit_mib << 20)


def whole(shape):
    return pl.BlockSpec(shape, lambda i: (0,) * len(shape), pipeline_mode=pl.Buffered(1))


def matmul(left, right):
    return jnp.dot(left, right, preferred_element_type=f32)


def rows_inner(left, right):
    return lax.dot_general(left, right, (((0,), (0,)), ((), ())), preferred_element_type=f32)


def cols_inner(left, right):
    return lax.dot_general(left, right, (((1,), (1,)), ((), ())), preferred_element_type=f32)


def gelu_and_slope(values):
    phi = 0.5 * (1.0 + lax.erf(values * 0.7071067811865476))
    return (
        values * phi,
        phi + values * jnp.exp(-0.5 * values * values) * 0.3989422804014327,
    )


def centred_rows(tokens_ref, rows):
    inputs = tokens_ref[...].reshape(rows, tokens_ref.shape[-1]).astype(f32)
    centred = inputs - jnp.mean(inputs, axis=1, keepdims=True)
    variance = jnp.mean(centred * centred, axis=1, keepdims=True)
    return inputs, centred, lax.rsqrt(variance + epsilon)


def channels_from_rows(ref, values, seqs, chunk, own):
    for place in range(ref.shape[0]):
        for s in range(seqs):
            ref[place, :, s * own : (s + 1) * own] = values[
                s * chunk : (s + 1) * chunk, place * own : (place + 1) * own
            ].astype(ref.dtype)


def rows_from_channels(ref, scratch, seqs, chunk, own):
    for place in range(ref.shape[0]):
        for s in range(seqs):
            scratch[s * chunk : (s + 1) * chunk, place * own : (place + 1) * own] = ref[
                place, :, s * own : (s + 1) * own
            ]


def reduce_body(dims, tokens_ref, gain_ref, bias_ref, weight_ref, normed_ref, out_ref, slope_ref):
    seqs, chunk, own = dims
    _, centred, inverse_std = centred_rows(tokens_ref, seqs * chunk)
    normed = (centred * inverse_std * gain_ref[...] + bias_ref[...]).astype(bf16)
    normed_ref[...] = normed
    reduced, slope = gelu_and_slope(matmul(normed, weight_ref[...]))
    slope_ref[...] = slope
    channels_from_rows(out_ref, reduced, seqs, chunk, own)


def gate_work(normed, weight):
    (rows, width), gate_width = normed[0].shape, weight.shape[1]
    micro_count, tile = len(normed), 512
    across, down = gate_width // tile, rows // tile
    count = micro_count * across * down

    def body(ins, outs, scratch):
        rows_refs, weight_ref = ins[:-1], ins[-1]
        rows_buf, weight_buf, out_buf, load_sem, store_sem = scratch
        loads = [
            pltpu.make_async_copy(rows_refs[m], rows_buf.at[pl.ds(m * rows, rows)], load_sem.at[m])
            for m in range(micro_count)
        ]
        loads.append(
            pltpu.make_async_copy(weight_ref, weight_buf, load_sem.at[micro_count])
        )
        loaded = []

        def stores(k):
            at = (
                pl.ds(pl.multiple_of(lax.div(k, across) * tile, tile), tile),
                pl.ds(pl.multiple_of(lax.rem(k, across) * tile, tile), tile),
            )
            slot = lax.rem(k, 2)
            return [
                pltpu.make_async_copy(out_buf.at[slot, r], outs[r].at[at], store_sem.at[slot, r])
                for r in range(2)
            ]

        def begin():
            for copy in loads:
                copy.start()

        def step(k, carry):
            @pl.when(k >= 2)
            def _():
                for copy in stores(k - 2):
                    copy.wait()

            slot = lax.rem(k, 2)
            left = rows_buf[pl.ds(pl.multiple_of(lax.div(k, across) * tile, tile), tile), :]
            right = weight_buf[:, pl.ds(pl.multiple_of(lax.rem(k, across) * tile, tile), tile)]
            gate, slope = gelu_and_slope(matmul(left, right))
            out_buf[slot, 0] = gate.astype(bf16)
            out_buf[slot, 1] = slope.astype(bf16)
            for copy in stores(k):
                copy.start()
            return carry

        def tick(group, groups):
            if not loaded:
                for copy in loads:
                    copy.wait()
                loaded.append(True)
            lax.fori_loop(count * group // groups, count * (group + 1) // groups, step, 0)

        def end():
            for k in (count - 2, count - 1):
                for copy in stores(k):
                    copy.wait()

        return begin, tick, end

    shape = jax.ShapeDtypeStruct((micro_count * rows, gate_width), bf16)
    scratch = [
        pltpu.VMEM((micro_count * rows, width), bf16),
        pltpu.VMEM((width, gate_width), bf16),
        pltpu.VMEM((2, 2, tile, tile), bf16),
        pltpu.SemaphoreType.DMA((micro_count + 1,)),
        pltpu.SemaphoreType.DMA((2, 2)),
    ]
    return [*normed, weight], [shape, shape], scratch, body


def middle_body(
    dims, teachers, tile, order_ref, scale_ref, state_ref, gate_ref, slope_ref, expand_ref, weight_ref,
    tokens_ref, cotangent_ref, weights_ref, *refs,
):
    seqs, chunk, own = dims
    teach_refs, refs = refs[:teachers], refs[teachers:]
    (state_out_ref, product_ref, branch_grad_ref, expanded_grad_ref, gate_grad_ref, out_ref,
     full_grad_ref, error_ref, mixed_grad_ref, expanded_ref) = refs[-10:]
    rows, width = seqs * chunk, tokens_ref.shape[-1]
    rows_from_channels(state_ref, state_out_ref, seqs, chunk, own)
    state_out = state_out_ref[...]
    tiles = [slice(j * tile, (j + 1) * tile) for j in range(gate_ref.shape[1] // tile)]
    branch = jnp.zeros((rows, width), f32)
    for at in tiles:
        expanded = matmul(state_out, expand_ref[:, at])
        expanded_ref[:, at] = expanded
        product = (expanded * gate_ref[:, at].astype(f32)).astype(bf16)
        product_ref[:, at] = product
        branch = branch + matmul(product, weight_ref[at, :])
    valid, keep = weights_ref[:, :1], weights_ref[:, 1:]
    full = tokens_ref[...].reshape(rows, width).astype(f32) + valid * branch
    out_ref[...] = full.astype(bf16).reshape(out_ref.shape)
    errors = full - jnp.concatenate([t[0] for t in teach_refs], axis=0).astype(f32)
    error_ref[0] = jnp.sum((keep * errors * errors).reshape(rows // 8, 8, width), axis=0)
    full_grad = cotangent_ref[...].reshape(rows, width).astype(f32) + keep * errors * scale_ref[0]
    full_grad_ref[...] = full_grad.astype(bf16)
    branch_grad = (valid * full_grad).astype(bf16)
    branch_grad_ref[...] = branch_grad
    mixed_grad = jnp.zeros((rows, state_out.shape[1]), f32)
    for at in tiles:
        product_grad = cols_inner(branch_grad, weight_ref[at, :])
        expanded_grad = (product_grad * gate_ref[:, at].astype(f32)).astype(bf16)
        expanded_grad_ref[:, at] = expanded_grad
        gate_grad_ref[:, at] = (
            product_grad * expanded_ref[:, at] * slope_ref[:, at].astype(f32)
        ).astype(bf16)
        mixed_grad = mixed_grad + cols_inner(expanded_grad, expand_ref[:, at])
    channels_from_rows(mixed_grad_ref, mixed_grad, seqs, chunk, own)


def input_body(
    dims, back_ref, slope_ref, gate_grad_ref, gate_weight_ref, reduce_weight_ref, tokens_ref,
    gain_ref, full_grad_ref, *refs,
):
    out_ref, reduced_grad_ref, gain_grad_ref, bias_grad_ref, back_rows_ref = refs[-5:]
    seqs, chunk, own = dims
    rows, width = seqs * chunk, tokens_ref.shape[-1]
    rows_from_channels(back_ref, back_rows_ref, seqs, chunk, own)
    reduced_grad = (back_rows_ref[...].astype(f32) * slope_ref[...]).astype(bf16)
    reduced_grad_ref[...] = reduced_grad
    normed_grad = cols_inner(gate_grad_ref[...], gate_weight_ref[...]) + cols_inner(
        reduced_grad, reduce_weight_ref[...]
    )
    _, centred, inverse_std = centred_rows(tokens_ref, rows)
    unit = centred * inverse_std
    gain_grad_ref[0] = jnp.sum((normed_grad * unit).reshape(rows // 8, 8, width), axis=0)
    bias_grad_ref[0] = jnp.sum(normed_grad.reshape(rows // 8, 8, width), axis=0)
    unit_grad = normed_grad * gain_ref[...]
    result = full_grad_ref[...].astype(f32) + inverse_std * (
        unit_grad
        - jnp.mean(unit_grad, axis=1, keepdims=True)
        - unit * jnp.mean(unit_grad * unit, axis=1, keepdims=True)
    )
    out_ref[...] = result.astype(bf16).reshape(out_ref.shape)


def product_scatter_body(dp_count, bits, plan, n_left, n_right, *refs):
    pieces, slots, lane, micros = plan["pieces"], plan["slots"], plan["lane"], plan["micros"]
    n = len(pieces)
    lefts, refs = refs[: n_left * micros], refs[n_left * micros :]
    rights, refs = refs[: n_right * micros], refs[n_right * micros :]
    ready_ref, small_ref, refs = refs[0], refs[1], refs[2:]
    outs, refs = refs[: plan["outputs"]], refs[plan["outputs"] :]
    left_bufs, refs = refs[:n_left], refs[n_left:]
    right_buf, left_sem, right_sem, load_sem, ready_sem, send, recv, store_sem = refs[:8]
    sets = [refs[8 : 8 + 5 + 3 * (bits - 1)], refs[8 + 5 + 3 * (bits - 1) :]]
    d, f = lax.axis_index("dp"), lax.axis_index("fsdp")
    my = [bit_of(f, b) for b in range(bits)]
    upper = list(range(bits - 1, 0, -1))
    small = n - 1

    def buffers(i):
        if i == small:
            return list(sets[1])
        _, rows, groups, _ = pieces[i]
        height, slot = rows * groups, i % slots
        views = []
        for k, ref in enumerate(sets[0]):
            arriving = k in (1, 3) or (k >= 5 and (k - 5) % 3 == 2)
            lead = (slice(None),) * (len(ref.shape) - 3)
            views.append(ref.at[(i if arriving else slot, *lead, pl.ds(0, height), slice(None))])
        return views

    bufs = [buffers(i) for i in range(n)]
    orders = [upper if i % 2 == 0 else upper[::-1] for i in range(n)]
    pushed, drained, waits, stores = {}, set(), [None] * n, {}

    def push(i, at, src, dst, device_id):
        copy = pltpu.make_async_remote_copy(
            src_ref=src,
            dst_ref=dst,
            send_sem=send.at[i, at],
            recv_sem=recv.at[i, at],
            device_id=device_id,
            device_id_type=MESH,
        )
        copy.start()
        pushed[(i, at)] = copy
        return copy

    def drain(i, *ats):
        for at in ats:
            if i >= 0 and i != small and (i, at) in pushed and (i, at) not in drained:
                pushed[(i, at)].wait_send()
                drained.add((i, at))

    ready = plan["ready"]
    jobs = [(i, *job) for i in range(ready, n - 1) for job in pieces[i][3]]
    loads = {}

    def fetch(j):
        if j < len(jobs):
            _, _, right, lo, cols, _ = jobs[j]
            loads[j] = [
                pltpu.make_async_copy(
                    rights[right * micros + m].at[:, pl.ds(lo, cols)],
                    right_buf.at[j % 2, m, :, pl.ds(0, cols)],
                    right_sem.at[j % 2, m],
                )
                for m in range(micros)
            ]
            for copy in loads[j]:
                copy.start()

    left_waited = set()
    left_loads = [
        [
            pltpu.make_async_copy(lefts[a * micros + m], left_bufs[a].at[m], left_sem.at[a, m])
            for m in range(micros)
        ]
        for a in range(n_left)
    ]
    small_load = pltpu.make_async_copy(small_ref, sets[1][0], load_sem)
    small_load.start()
    lead = (slice(None),) * (bits + 1)
    ready_loads = []
    for i in range(ready):
        _, rows, groups, piece_jobs = pieces[i]
        ready_loads.append(
            [
                pltpu.make_async_copy(
                    ready_ref.at[(*lead, slice(None), pl.ds(piece_jobs[0][2] + g * lane, lane))],
                    bufs[i][0].at[(*lead, pl.ds(g * rows, rows), slice(None))],
                    ready_sem.at[i, g],
                )
                for g in range(groups)
            ]
        )
        for copy in ready_loads[i]:
            copy.start()
    for a in range(n_left):
        for copy in left_loads[a]:
            copy.start()
        if a < 2:
            fetch(a)
    greet(dp_count, bits)

    def make(i):
        _, rows, groups, piece_jobs = pieces[i]
        made = bufs[i][0]
        drain(i - slots, 0)
        for j, job in enumerate(jobs):
            if job[0] != i:
                continue
            _, left, right, lo, cols, at_group = job
            if left not in left_waited:
                for copy in left_loads[left]:
                    copy.wait()
                left_waited.add(left)
            for copy in loads[j]:
                copy.wait()
            height = rows << bits

            def tile(p, carry, left=left, cols=cols, at_group=at_group, j=j, height=height):
                total = None
                for m in range(left_bufs[left].shape[0]):
                    part = rows_inner(
                        left_bufs[left][m, :, pl.ds(pl.multiple_of(p * height, 128), height)],
                        right_buf[j % 2, m, :, :cols],
                    )
                    total = part if total is None else total + part
                total = total.astype(bf16)
                for g in range(cols // lane):
                    block = total[:, g * lane : (g + 1) * lane].reshape(*(2,) * bits, rows, lane)
                    lead = (slice(None),) * bits
                    made[(p, *lead, pl.ds((at_group + g) * rows, rows), slice(None))] = block
                return carry

            lax.fori_loop(0, dp_count, tile, 0)
            fetch(j + 2)

    def first(i):
        made, got = bufs[i][0], bufs[i][1]
        if i == small:
            small_load.wait()
        elif i < ready:
            for copy in ready_loads[i]:
                copy.wait()
        else:
            make(i)
        lead = (slice(None),) * bits
        waits[i] = push(i, 0, made.at[(*lead, 1 - my[0])], got, {"fsdp": flip(f, 0)})

    def held(i, s):
        waits[i].wait_recv()
        if s == 0:
            lead = (slice(None),) * bits
            return bufs[i][0].at[(*lead, my[0])], bufs[i][1]
        return bufs[i][5 + 3 * (s - 1)], bufs[i][5 + 3 * (s - 1) + 2]

    def middle(i, s):
        own, more = held(i, s - 1)
        b = orders[i][s - 1]
        left = [q for q in upper if q not in orders[i][: s - 1]]
        kept, sent, arriving = bufs[i][5 + 3 * (s - 1) : 8 + 3 * (s - 1)]

        def side(value):
            return (slice(None),) + tuple(value if q == b else slice(None) for q in left)

        drain(i - slots, s)
        theirs, mine = side(1 - my[b]), side(my[b])
        sent[...] = (own[theirs].astype(f32) + more[theirs].astype(f32)).astype(sent.dtype)
        waits[i] = push(i, s, sent, arriving, {"fsdp": flip(f, b)})
        kept[...] = own[mine].astype(f32) + more[mine].astype(f32)

    def last(i):
        own, more = held(i, bits - 1)
        to_dp, from_dp = bufs[i][2], bufs[i][3]
        drain(i - slots, *range(bits, bits + dp_count - 1))
        copies = []
        for o in near_first(dp_count)[1:]:
            peer = lax.rem(d + o, dp_count)
            to_dp[o - 1] = (own[peer] + more[peer].astype(f32)).astype(to_dp.dtype)
            copies.append(
                push(i, bits - 1 + o, to_dp.at[o - 1], from_dp.at[o - 1], {"dp": peer})
            )
        waits[i] = copies
        for store in stores.pop(i - slots, []):
            store.wait()
        bufs[i][4][...] = own[d] + more[d].astype(f32)

    def finish(i):
        result, from_dp = bufs[i][4], bufs[i][3]
        for copy in waits[i]:
            copy.wait_recv()
        total = result[...]
        for o in range(1, dp_count):
            total = total + from_dp[o - 1].astype(f32)
        result[...] = total
        out, rows, groups, piece_jobs = pieces[i]
        stores[i] = []
        if i == small:
            stores[i].append(pltpu.make_async_copy(result, outs[out], store_sem.at[i, 0]))
        else:
            lo = piece_jobs[0][2]
            for g in range(groups):
                stores[i].append(
                    pltpu.make_async_copy(
                        result.at[pl.ds(g * rows, rows)],
                        outs[out].at[:, pl.ds(lo + g * lane, lane)],
                        store_sem.at[i, g],
                    )
                )
        for store in stores[i]:
            store.start()

    for t in range((n + 1) // 2 + bits + 1):
        for s in (*range(1, bits + 2), 0):
            for i in range(2 * (t - s), min(2 * (t - s) + 2, n)):
                if i < 0:
                    continue
                if s == 0:
                    first(i)
                elif s < bits:
                    middle(i, s)
                elif s == bits:
                    last(i)
                else:
                    finish(i)
    for key, copy in pushed.items():
        if key not in drained:
            copy.wait_send()
    for group in stores.values():
        for store in group:
            store.wait()


def product_scatter(lefts, rights, ready, small, collective_id):
    dp_count, fsdp_count = lax.axis_size("dp"), lax.axis_size("fsdp")
    bits = fsdp_count.bit_length() - 1
    devices = dp_count * fsdp_count
    lane, slots, height = 256, 4, 96
    unique = []
    for left in lefts:
        if not any(left is u for u in unique):
            unique.append(left)
    pieces = []
    for k, (left, right) in enumerate(zip(lefts, rights)):
        at = next(a for a, u in enumerate(unique) if u is left)
        rows, width = left[0].shape[1] // devices, right[0].shape[1]
        per_piece = min(height // rows, width // lane)
        for lo in range(0, width, per_piece * lane):
            groups = min(per_piece, (width - lo) // lane)
            jobs = [
                (at, k, lo + g * lane, min(3, groups - g) * lane, g) for g in range(0, groups, 3)
            ]
            pieces.append((k, rows, groups, jobs))
    pieces.append((len(lefts), small.shape[1], 1, []))
    n = len(pieces)
    plan = {
        "pieces": pieces,
        "slots": slots,
        "lane": lane,
        "outputs": len(lefts) + 1,
        "micros": len(lefts[0]),
        "ready": sum(1 for k, _, _, jobs in pieces[:-1] if k == 0 and jobs[-1][2] + jobs[-1][3] <= ready.shape[1]),
    }

    def buffer_set(count, lead, rows, columns, dtype):
        def shaped(many, *dims):
            return (many, *dims, rows, columns) if lead else (*dims, rows, columns)

        halved = [(2,) * (bits - 1 - s) for s in range(bits)]
        result = [
            pltpu.VMEM(shaped(slots, dp_count, *(2,) * bits), dtype),
            pltpu.VMEM(shaped(count, dp_count, *halved[0]), dtype),
            pltpu.VMEM(shaped(slots, dp_count - 1), dtype),
            pltpu.VMEM(shaped(count, dp_count - 1), dtype),
            pltpu.VMEM(shaped(slots), f32),
        ]
        for s in range(1, bits):
            result += [
                pltpu.VMEM(shaped(slots, dp_count, *halved[s]), f32),
                pltpu.VMEM(shaped(slots, dp_count, *halved[s]), dtype),
                pltpu.VMEM(shaped(count, dp_count, *halved[s]), dtype),
            ]
        return result

    micro_count, rows = len(lefts[0]), lefts[0][0].shape[0]
    steps = bits - 1 + dp_count
    small = small.reshape(dp_count, *(2,) * bits, *small.shape[1:])
    ready = ready.reshape(dp_count, *(2,) * bits, -1, ready.shape[1])
    widths = [(a[0].shape[1], b[0].shape[1]) for a, b in zip(lefts, rights)]
    flops = sum(2 * micro_count * rows * a * b for a, b in widths)
    return pl.pallas_call(
        functools.partial(product_scatter_body, dp_count, bits, plan, len(unique), len(rights)),
        out_shape=[jax.ShapeDtypeStruct((a // devices, b), f32) for a, b in widths]
        + [jax.ShapeDtypeStruct(small.shape[-2:], f32)],
        in_specs=[ANY] * ((len(unique) + len(rights)) * micro_count + 2),
        out_specs=[ANY] * (len(lefts) + 1),
        scratch_shapes=[pltpu.VMEM((micro_count, *u[0].shape), bf16) for u in unique]
        + [
            pltpu.VMEM((2, micro_count, rows, 3 * lane), bf16),
            pltpu.SemaphoreType.DMA((len(unique), micro_count)),
            pltpu.SemaphoreType.DMA((2, micro_count)),
            pltpu.SemaphoreType.DMA,
            pltpu.SemaphoreType.DMA((slots, height // 16)),
            pltpu.SemaphoreType.DMA((n, steps)),
            pltpu.SemaphoreType.DMA((n, steps)),
            pltpu.SemaphoreType.DMA((n, height // 16)),
        ]
        + buffer_set(n - 1, True, height, lane, bf16)
        + buffer_set(1, False, *small.shape[-2:], f32),
        compiler_params=pltpu.CompilerParams(
            collective_id=collective_id, has_side_effects=True, vmem_limit_bytes=62 << 20
        ),
        cost_estimate=pl.CostEstimate(flops=flops, bytes_accessed=100 << 20, transcendentals=0),
    )(*[x for u in unique for x in u], *[x for r in rights for x in r], ready, small)


def weight_grad_body(n, *refs):
    lefts, rights, out_ref = refs[:n], refs[n : 2 * n], refs[2 * n]
    total = rows_inner(lefts[0][...], rights[0][...])
    for left, right in zip(lefts[1:], rights[1:]):
        total = total + rows_inner(left[...], right[...])
    out_ref[...] = total.astype(out_ref.dtype)


def weight_grad(lefts, rights, row_tile, width=None):
    n, (rows, height), width = len(lefts), lefts[0].shape, width or rights[0].shape[1]
    return pl.pallas_call(
        functools.partial(weight_grad_body, n),
        grid=(height // row_tile,),
        out_shape=jax.ShapeDtypeStruct((height, width), bf16),
        in_specs=[pl.BlockSpec((rows, row_tile), lambda i: (0, i))] * n + [whole((rows, width))] * n,
        out_specs=pl.BlockSpec((row_tile, width), lambda i: (i, 0)),
        compiler_params=params(),
        cost_estimate=pl.CostEstimate(
            flops=2 * n * rows * height * width,
            bytes_accessed=2 * (n * rows * (height + width) + height * width),
            transcendentals=0,
        ),
    )(*lefts, *rights)


def fourier_table(chunk):
    freq = np.arange(chunk)[:, None]
    time = np.arange(chunk)[None, :]
    angle = (freq * time % (2 * chunk)) * (np.pi / chunk)
    sines = -np.sin(angle)
    sines[0] = 1.0 - 2.0 * (np.arange(chunk) % 2)
    table = np.concatenate([np.cos(angle), sines], axis=0)
    scaling = np.full((2 * chunk, 1), 1.0 / chunk)
    scaling[0] = scaling[chunk] = 0.5 / chunk
    sign = np.tile(1.0 - 2.0 * (np.arange(chunk) % 2), 2)
    sign[chunk] = 1.0 - 2.0 * (chunk % 2)
    return table.astype(np.float32), (table * scaling).astype(np.float32), sign.astype(np.float32)


def high_and_low(table):
    high = table.astype(jnp.bfloat16)
    return np.stack([high, (table - high.astype(np.float32)).astype(jnp.bfloat16)])


def spectrum(table_ref, values):
    return matmul(table_ref[0], values) + matmul(table_ref[1], values)


def to_time(inverse_ref, spec):
    high = spec.astype(bf16)
    low = (spec - high.astype(f32)).astype(bf16)
    return (
        rows_inner(inverse_ref[0], high)
        + rows_inner(inverse_ref[1], high)
        + rows_inner(inverse_ref[0], low)
    )


def packed_product(first, second, edge, conjugate):
    (a_re, a_im), (b_re, b_im) = first, second
    straight, crossed = a_re * b_re, a_im * b_im
    if conjugate:
        real = straight + jnp.where(edge, 0.0, crossed)
        imag = jnp.where(edge, crossed, a_re * b_im - a_im * b_re)
    else:
        real = straight - jnp.where(edge, 0.0, crossed)
        imag = jnp.where(edge, crossed, a_re * b_im + a_im * b_re)
    return real, imag


def pair_sum(pairs, edge, conjugate):
    real, imag = packed_product(*pairs[0], edge, conjugate)
    for first, second in pairs[1:]:
        more = packed_product(first, second, edge, conjugate)
        real, imag = real + more[0], imag + more[1]
    return real, imag


def halves(ref, block, at, chunk):
    return ref[block, :chunk, at], ref[block, chunk:, at]


def convolve_body(table_ref, inverse_ref, kernel_ref, rows_ref, out_ref, spec_ref, back_ref):
    blocks, chunk, columns = rows_ref.shape
    lanes = kernel_ref.shape[2]
    edge = lax.broadcasted_iota(jnp.int32, (chunk, lanes), 0) == 0
    for c in range(blocks):
        spec_ref[c] = spectrum(table_ref, rows_ref[c])
        for g in range(columns // lanes):
            at = slice(g * lanes, (g + 1) * lanes)
            everything = slice(None)
            real, imag = pair_sum(
                [
                    (halves(kernel_ref, k, everything, chunk), halves(spec_ref, c - k, at, chunk))
                    for k in range(c + 1)
                ],
                edge,
                False,
            )
            back_ref[:chunk, at], back_ref[chunk:, at] = real, imag
        out_ref[c] = to_time(inverse_ref, back_ref[...]).astype(out_ref.dtype)


def convolve_back_body(
    table_ref, inverse_ref, kernel_ref, rows_ref, grad_ref, out_ref, kernel_grad_ref,
    spec_ref, grad_spec_ref, back_ref,
):
    blocks, chunk, columns = rows_ref.shape
    lanes = kernel_ref.shape[2]
    edge = lax.broadcasted_iota(jnp.int32, (chunk, lanes), 0) == 0
    everything = slice(None)
    groups = [slice(g * lanes, (g + 1) * lanes) for g in range(columns // lanes)]
    for c in range(blocks):
        spec_ref[c] = spectrum(table_ref, rows_ref[c])
    for c in reversed(range(blocks)):
        grad_spec_ref[c] = spectrum(table_ref, grad_ref[c])
        for at in groups:
            real, imag = pair_sum(
                [
                    (
                        halves(kernel_ref, late - c, everything, chunk),
                        halves(grad_spec_ref, late, at, chunk),
                    )
                    for late in range(c, blocks)
                ],
                edge,
                True,
            )
            back_ref[:chunk, at], back_ref[chunk:, at] = real, imag
        out_ref[c] = to_time(inverse_ref, back_ref[...]).astype(out_ref.dtype)
    for k in range(blocks):
        real, imag = pair_sum(
            [
                (halves(spec_ref, c - k, at, chunk), halves(grad_spec_ref, c, at, chunk))
                for c in range(k, blocks)
                for at in groups
            ],
            edge,
            True,
        )
        kernel_grad_ref[k, :chunk], kernel_grad_ref[k, chunk:] = real, imag


def kernel_factors(decay, frequency, log_step, length):
    fine = 32
    coarse = length // fine
    step_size = jnp.exp(log_step)[:, None]
    real = (step_size * decay)[:, None, :]
    imag = (step_size * frequency)[:, None, :]
    far = (jnp.arange(coarse, dtype=jnp.int32) * fine).astype(f32)[None, :, None]
    near = jnp.arange(fine, dtype=jnp.int32).astype(f32)[None, :, None]
    far_damp, near_damp = jnp.exp(real * far), jnp.exp(real * near)
    return (
        (far_damp * jnp.cos(imag * far), far_damp * jnp.sin(imag * far)),
        (near_damp * jnp.cos(imag * near), near_damp * jnp.sin(imag * near)),
        step_size,
    )


def kernel_forward(weight_pair, factors):
    (far_re, far_im), (near_re, near_im), _ = factors
    w_re, w_im = weight_pair[0][:, None, :], weight_pair[1][:, None, :]
    left = jnp.concatenate([far_re, -far_im], axis=2)
    right = jnp.concatenate(
        [w_re * near_re - w_im * near_im, w_re * near_im + w_im * near_re], axis=2
    )
    rows = jnp.einsum("han,hbn->hab", left, right, precision=high)
    return rows.reshape(rows.shape[0], -1)


def kernel_backward(grad_rows, weight_pair, decay, frequency, factors):
    (far_re, far_im), (near_re, near_im), step_size = factors
    channels, coarse, states = far_re.shape
    fine = near_re.shape[1]
    tiles = grad_rows.reshape(channels, coarse, fine)
    near_index = jnp.arange(fine, dtype=jnp.int32).astype(f32)
    far_index = (jnp.arange(coarse, dtype=jnp.int32) * fine).astype(f32)[None, :, None]
    stacked = jnp.concatenate([tiles, tiles * near_index], axis=1)
    part = jnp.einsum(
        "hab,hbn->han", stacked, jnp.concatenate([near_re, near_im], axis=2), precision=high
    )
    u_re, u_im = part[:, :coarse, :states], part[:, :coarse, states:]
    v_re = part[:, coarse:, :states] + far_index * u_re
    v_im = part[:, coarse:, states:] + far_index * u_im
    s_re = jnp.sum(far_re * u_re - far_im * u_im, axis=1)
    s_im = jnp.sum(far_re * u_im + far_im * u_re, axis=1)
    t_re = jnp.sum(far_re * v_re - far_im * v_im, axis=1)
    t_im = jnp.sum(far_re * v_im + far_im * v_re, axis=1)
    w_re, w_im = weight_pair[0], weight_pair[1]
    along_re = step_size * (w_re * t_re - w_im * t_im)
    along_im = -step_size * (w_re * t_im + w_im * t_re)
    return (
        jnp.stack([s_re, -s_im]),
        along_re,
        along_im,
        jnp.sum(decay * along_re + frequency * along_im, axis=1),
    )


def shards(
    tokens,
    cotangent,
    teacher,
    lengths,
    dealing,
    loss_mask,
    norm_gain,
    norm_bias,
    gate_weight,
    reduce_weight,
    state_weight,
    decay_rate,
    frequency,
    log_step,
    expand_weight,
    out_weight,
):
    dp_count, fsdp_count = lax.axis_size("dp"), lax.axis_size("fsdp")
    devices = dp_count * fsdp_count
    group_index = lax.axis_index("fsdp")
    dp_place = lax.axis_index("dp")
    micro_count, seqs, chunk, width = tokens.shape
    rows = seqs * chunk
    seq_length = chunk * dp_count
    gate_width = gate_weight.shape[1]
    reduced_width = reduce_weight.shape[1]
    own = reduced_width // dp_count
    lanes = max(own, 128)
    share = norm_gain.shape[0]
    micros = range(micro_count)
    direct = own % 128 == 0

    small = jnp.pad(jnp.stack([norm_gain, norm_bias]), ((0, 14), (0, 256 - share)))
    mask_rows = loss_mask.reshape(micro_count, dp_count, chunk).transpose(1, 0, 2)
    mask_rows = jnp.pad(mask_rows, ((0, 0), (0, 8 - micro_count), (0, 0)))
    teacher_rows = teacher.reshape(micro_count, dp_count, chunk, width)
    w_gate, w_reduce, small, *swapped = gather_all(
        [gate_weight, reduce_weight, small],
        [(0, mask_rows[None]), *[(m, teacher_rows) for m in micros[1:]]],
        1,
    )
    masked = swapped[0].transpose(1, 0, 2)[:micro_count]
    w_gate = w_gate.reshape(width, gate_width)
    w_reduce = w_reduce.reshape(width, reduced_width)
    gain_row = small[:, :, 0, :share].reshape(1, width).astype(f32)
    bias_row = small[:, :, 1, :share].reshape(1, width).astype(f32)

    per_block = max(1, 512 // chunk)
    steps = seqs // per_block
    middle_block = max(1, 256 // chunk)
    middle_steps = seqs // middle_block

    def row_spec(columns, count=per_block):
        return pl.BlockSpec((count * chunk, columns), lambda i, *_: (i, 0))

    def shared(shape, block):
        return pl.BlockSpec(shape, lambda i, *_: block, pipeline_mode=pl.Buffered(1))

    lane_shape = (dp_count, chunk, seqs * own)
    if not direct:
        lane_shape = (1, rows, reduced_width)

    def dims(count):
        return (count, chunk, own) if direct else (1, count * chunk, reduced_width)

    def lane_spec(count):
        if direct:
            return pl.BlockSpec((dp_count, chunk, count * own), lambda i, *_: (0, 0, i))
        return pl.BlockSpec((1, count * chunk, reduced_width), lambda i, *_: (0, i, 0))

    def tokens_spec(m, count):
        return pl.BlockSpec((None, count, chunk, width), lambda i, *_: (m, i, 0, 0))

    def send_lanes(values):
        if not direct:
            values = values.reshape(seqs, chunk, dp_count, own).transpose(2, 1, 0, 3)
            values = values.reshape(dp_count, chunk, seqs * own)
        return exchange(values)

    def receive_lanes(values):
        values = exchange(values)
        if not direct:
            values = values.reshape(dp_count, chunk, seqs, own).transpose(2, 1, 0, 3)
            values = values.reshape(1, rows, reduced_width)
        return values

    def reduce_rows(m, gain_row):
        return pl.pallas_call(
            functools.partial(reduce_body, dims(per_block)),
            grid=(steps,),
            out_shape=[
                jax.ShapeDtypeStruct((rows, width), bf16),
                jax.ShapeDtypeStruct(lane_shape, bf16),
                jax.ShapeDtypeStruct((rows, reduced_width), f32),
            ],
            in_specs=[
                tokens_spec(m, per_block),
                whole((1, width)),
                whole((1, width)),
                whole((width, reduced_width)),
            ],
            out_specs=[row_spec(width), lane_spec(per_block), row_spec(reduced_width)],
            compiler_params=params(),
            cost_estimate=pl.CostEstimate(
                flops=2 * rows * width * reduced_width,
                bytes_accessed=8 * rows * width,
                transcendentals=2 * rows * reduced_width,
            ),
        )(tokens, gain_row, bias_row, w_reduce)

    local_ids = group_index * seqs + jnp.arange(seqs, dtype=jnp.int32)
    targets = jnp.take(dealing, local_ids, axis=1)
    own_lengths = jnp.take(lengths, local_ids, axis=1)
    positions = dp_place * chunk + jnp.arange(chunk, dtype=jnp.int32)
    valid = (positions[None, None, :] < own_lengths[:, :, None]).astype(f32)
    keep = jnp.take_along_axis(masked, targets[:, :, None], axis=1).astype(f32) * valid
    own_count = jnp.sum(keep)
    row_weights = jnp.stack([valid, keep], axis=-1).reshape(micro_count, rows, 2)
    counts = jnp.full((8, 256), own_count, f32)
    row_weights = [row_weights[m] for m in micros]

    reduced_rows = [reduce_rows(0, gain_row)]
    held = lax.optimization_barrier((decay_rate, frequency, log_step, reduced_rows[0][1]))
    factors = kernel_factors(*held[:3], seq_length)
    own_kernel = kernel_forward(state_weight, factors)
    for m in micros[1:]:
        later_gain, own_kernel, row_weights, targets, counts = lax.optimization_barrier(
            (gain_row, own_kernel, row_weights, targets, counts)
        )
        reduced_rows.append(reduce_rows(m, later_gain))
    normed, lanes_out, slope_reduced = zip(*reduced_rows)
    lanes_in = [send_lanes(x) for x in lanes_out]


    table_np, inverse_np, sign_np = fourier_table(chunk)
    sign = jnp.asarray(sign_np)[:, None]
    table2, inverse2 = jnp.asarray(high_and_low(table_np)), jnp.asarray(high_and_low(inverse_np))
    kernel = lax.all_gather(own_kernel, "fsdp", axis=0, tiled=True)
    segments = jnp.einsum(
        "kt,hct->ckh", jnp.asarray(table_np), kernel.reshape(own, dp_count, chunk), precision=high
    )
    previous = jnp.concatenate([jnp.zeros_like(segments[:1]), segments[:-1]], axis=0)
    kernel_spec = jnp.tile(segments + sign * previous, (1, 1, lanes // own))

    blocks = (dp_count, chunk, seqs * own)
    spec_scratch = pltpu.VMEM((dp_count, 2 * chunk, seqs * own), f32)
    back_scratch = pltpu.VMEM((2 * chunk, seqs * own), f32)
    transform_flops = 8 * chunk * chunk * dp_count * seqs * own

    def convolve(values):
        return pl.pallas_call(
            convolve_body,
            out_shape=jax.ShapeDtypeStruct(blocks, bf16),
            scratch_shapes=[spec_scratch, back_scratch],
            compiler_params=params(),
            cost_estimate=pl.CostEstimate(
                flops=5 * transform_flops // 2, bytes_accessed=8 << 20, transcendentals=0
            ),
        )(table2, inverse2, kernel_spec, values)

    def convolve_back(values, grads):
        return pl.pallas_call(
            convolve_back_body,
            out_shape=[
                jax.ShapeDtypeStruct(blocks, bf16),
                jax.ShapeDtypeStruct((dp_count, 2 * chunk, lanes), f32),
            ],
            scratch_shapes=[spec_scratch, spec_scratch, back_scratch],
            compiler_params=params(),
            cost_estimate=pl.CostEstimate(
                flops=7 * transform_flops // 2, bytes_accessed=8 << 20, transcendentals=0
            ),
        )(table2, inverse2, kernel_spec, values, grads)

    convolved = [convolve(x) for x in lanes_in]
    late = lax.optimization_barrier((expand_weight, out_weight, *convolved))
    w_expand, w_out, counts, *more, gate, slope = gather_all(
        [late[0], late[1], counts],
        [(0, teacher_rows)],
        2,
        gate_work(normed, w_gate),
    )
    teach = [*more, *swapped[1:]]
    w_expand = w_expand.reshape(reduced_width, gate_width)
    w_out = w_out.reshape(gate_width, width)
    count = jnp.sum(counts[:, :, 0, 0])
    error_scale = (2.0 / (width * count)).reshape(1)
    mixed = [receive_lanes(x) for x in convolved]
    def middle_rows(m, *earlier):
        teach_specs = [
            pl.BlockSpec((1, chunk, width), functools.partial(teach_block, s)) for s in range(middle_block)
        ]
        gate_spec = pl.BlockSpec(
            (middle_block * chunk, gate_width), lambda i, *_: (m * middle_steps + i, 0)
        )
        wide, narrow = row_spec(gate_width, middle_block), row_spec(width, middle_block)
        return pl.pallas_call(
            functools.partial(middle_body, dims(middle_block), middle_block, 768),
            grid_spec=pltpu.PrefetchScalarGridSpec(
                num_scalar_prefetch=2,
                grid=(middle_steps,),
                in_specs=[
                    lane_spec(middle_block),
                    gate_spec,
                    gate_spec,
                    shared((reduced_width, gate_width), (0, 0)),
                    shared((gate_width, width), (0, 0)),
                    tokens_spec(m, middle_block),
                    tokens_spec(m, middle_block),
                    row_spec(2, middle_block),
                    *teach_specs,
                    *[ANY] * len(earlier),
                ],
                out_specs=[
                    row_spec(reduced_width, middle_block),
                    wide,
                    narrow,
                    wide,
                    wide,
                    tokens_spec(m, middle_block),
                    narrow,
                    pl.BlockSpec((1, 8, width), lambda i, *_: (i, 0, 0)),
                    lane_spec(middle_block),
                ],
                scratch_shapes=[pltpu.VMEM((middle_block * chunk, gate_width), f32)],
            ),
            out_shape=[
                jax.ShapeDtypeStruct((rows, reduced_width), bf16),
                jax.ShapeDtypeStruct((rows, gate_width), bf16),
                jax.ShapeDtypeStruct((rows, width), bf16),
                jax.ShapeDtypeStruct((rows, gate_width), bf16),
                jax.ShapeDtypeStruct((rows, gate_width), bf16),
                jax.ShapeDtypeStruct(tokens.shape, bf16),
                jax.ShapeDtypeStruct((rows, width), bf16),
                jax.ShapeDtypeStruct((middle_steps, 8, width), f32),
                jax.ShapeDtypeStruct(lane_shape, bf16),
            ],
            input_output_aliases={10 + middle_block: 5} if earlier else {},
            compiler_params=params(),
            cost_estimate=pl.CostEstimate(
                flops=4 * rows * gate_width * (width + reduced_width),
                bytes_accessed=10 * rows * gate_width + 16 * rows * width,
                transcendentals=0,
            ),
        )(
            targets[m], error_scale, mixed[m], gate, slope, w_expand, w_out, tokens, cotangent,
            row_weights[m], *[teach[m]] * middle_block, *earlier,
        )

    def teach_block(s, i, order, scale):
        return (order[i * middle_block + s], 0, 0)

    def input_rows(m, back, gate_grad, full_grad, *earlier):
        eight = pl.BlockSpec((1, 8, width), lambda i, *_: (i, 0, 0))
        return pl.pallas_call(
            functools.partial(input_body, dims(middle_block)),
            grid=(middle_steps,),
            in_specs=[
                lane_spec(middle_block),
                row_spec(reduced_width, middle_block),
                row_spec(gate_width, middle_block),
                shared((width, gate_width), (0, 0)),
                shared((width, reduced_width), (0, 0)),
                tokens_spec(m, middle_block),
                whole((1, width)),
                row_spec(width, middle_block),
                *[ANY] * len(earlier),
            ],
            out_specs=[tokens_spec(m, middle_block), row_spec(reduced_width, middle_block), eight, eight],
            out_shape=[
                jax.ShapeDtypeStruct(tokens.shape, bf16),
                jax.ShapeDtypeStruct((rows, reduced_width), bf16),
                jax.ShapeDtypeStruct((middle_steps, 8, width), f32),
                jax.ShapeDtypeStruct((middle_steps, 8, width), f32),
            ],
            scratch_shapes=[pltpu.VMEM((middle_block * chunk, reduced_width), bf16)],
            input_output_aliases={8: 0} if earlier else {},
            compiler_params=params(),
            cost_estimate=pl.CostEstimate(
                flops=2 * rows * width * (gate_width + reduced_width),
                bytes_accessed=4 * rows * gate_width + 8 * rows * width,
                transcendentals=0,
            ),
        )(back, slope_reduced[m], gate_grad, w_gate, w_reduce, tokens, gain_row, full_grad, *earlier)

    middle = []
    for m in micros:
        middle.append(middle_rows(m, *[x[5] for x in middle[-1:]]))
    outputs = middle[-1][5]
    state_out, product, branch_grad, expanded_grad, gate_grad, _, full_grad, error_rows, lane_grad = zip(*middle)
    grads_in = [send_lanes(x) for x in lane_grad]
    back, kernel_grads = zip(*[convolve_back(lanes_in[m], grads_in[m]) for m in micros])
    ready = weight_grad(normed, gate_grad, 256, gate_width // 2)
    held_back, ready = lax.optimization_barrier((back[0], ready))
    back = [receive_lanes(x) for x in (held_back, *back[1:])]
    ends = []
    for m in micros:
        ends.append(input_rows(m, back[m], gate_grad[m], full_grad[m], *[x[0] for x in ends[-1:]]))
    returned = ends[-1][0]
    _, reduced_grad, gain_rows, bias_rows = zip(*ends)

    kernel_total = sum(kernel_grads)
    if not direct:
        kernel_total = kernel_total.reshape(dp_count, 2 * chunk, lanes // own, own).sum(axis=2)
    following = jnp.concatenate([kernel_total[1:], jnp.zeros_like(kernel_total[:1])], axis=0)
    kernel_grad = jnp.einsum(
        "kt,ckh->hct", jnp.asarray(inverse_np), kernel_total + sign * following, precision=high
    ).reshape(own, seq_length)
    kernel_grad, _ = lax.optimization_barrier((kernel_grad, reduced_grad))
    kernel_grad = lax.psum_scatter(kernel_grad, "fsdp", scatter_dimension=0, tiled=True)
    pair_grad, decay_grad, frequency_grad, step_grad = kernel_backward(
        kernel_grad, state_weight, decay_rate, frequency, factors
    )

    gain_total = jnp.sum(sum(gain_rows), axis=(0, 1)).reshape(devices, 1, share)
    bias_total = jnp.sum(sum(bias_rows), axis=(0, 1)).reshape(devices, 1, share)
    error_total = jnp.full((devices, 1, share), jnp.sum(sum(error_rows)))
    sums = jnp.concatenate([gain_total, bias_total, error_total], axis=1)
    sums = jnp.pad(sums, ((0, 0), (0, 5), (0, 128 - share)))
    pairs = [
        (normed, gate_grad),
        (state_out, expanded_grad),
        (product, branch_grad),
        (normed, reduced_grad),
    ]
    if all(left[0].shape[1] // devices % 16 == 0 for left, _ in pairs):
        lefts, rights = zip(*pairs)
        gate_sum, expand_sum, out_sum, reduce_sum, sums = product_scatter(
            lefts, rights, ready, sums, 3
        )
    else:
        made = [weight_grad(left, right, 256) for left, right in pairs]
        gate_sum, expand_sum, out_sum, reduce_sum, sums = scatter_all(
            [x.reshape(devices, -1, x.shape[1]) for x in made] + [sums], [4, 2, 4, 1, 1], 3
        )
    loss_value = sums[2, 0] / (width * count)
    return (
        outputs,
        loss_value,
        returned,
        sums[0, :share],
        sums[1, :share],
        gate_sum,
        reduce_sum,
        pair_grad,
        decay_grad,
        frequency_grad,
        step_grad,
        expand_sum,
        out_sum,
    )


def solution(mesh):
    in_specs = (
        P(None, "fsdp", "dp", None),
        P(None, "fsdp", "dp", None),
        P(None, ("dp", "fsdp"), None, None),
        P(),
        P(),
        P(None, ("dp", "fsdp"), None),
        P(("dp", "fsdp")),
        P(("dp", "fsdp")),
        P(("dp", "fsdp"), None),
        P(("dp", "fsdp"), None),
        P(None, ("dp", "fsdp"), None),
        P(("dp", "fsdp"), None),
        P(("dp", "fsdp"), None),
        P(("dp", "fsdp")),
        P(("dp", "fsdp"), None),
        P(("dp", "fsdp"), None),
    )
    out_specs = (
        P(None, "fsdp", "dp", None),
        P(),
        P(None, "fsdp", "dp", None),
        P(("dp", "fsdp")),
        P(("dp", "fsdp")),
        P(("dp", "fsdp"), None),
        P(("dp", "fsdp"), None),
        P(None, ("dp", "fsdp"), None),
        P(("dp", "fsdp"), None),
        P(("dp", "fsdp"), None),
        P(("dp", "fsdp")),
        P(("dp", "fsdp"), None),
        P(("dp", "fsdp"), None),
    )
    return jax.shard_map(shards, mesh=mesh, in_specs=in_specs, out_specs=out_specs, check_vma=False)
```

```python
import functools

import numpy as np
import jax
import jax.numpy as jnp
from jax import lax
from jax.experimental import pallas as pl
from jax.experimental.pallas import tpu as pltpu
from jax.sharding import PartitionSpec as P

epsilon = 1e-05
high = lax.Precision.HIGH
bf16 = jnp.bfloat16
f32 = jnp.float32
MESH = pl.DeviceIdType.MESH
ANY = pl.BlockSpec(memory_space=pltpu.HBM)


def bit_of(index, bit):
    return lax.rem(lax.div(index, 1 << bit), 2)


def flip(index, bit):
    return index + (1 << bit) - 2 * (1 << bit) * bit_of(index, bit)


def greet(dp_count, bits):
    d, f = lax.axis_index("dp"), lax.axis_index("fsdp")
    barrier = pltpu.get_barrier_semaphore()
    for o in range(1, dp_count):
        peer = lax.rem(d + o, dp_count)
        pl.semaphore_signal(barrier, inc=1, device_id={"dp": peer}, device_id_type=MESH)
    for b in range(bits):
        pl.semaphore_signal(barrier, inc=1, device_id={"fsdp": flip(f, b)}, device_id_type=MESH)
    pl.semaphore_wait(barrier, dp_count - 1 + bits)


def near_first(count):
    order = [0]
    for k in range(1, count // 2 + 1):
        order += [k] if k == count - k else [k, count - k]
    return order


def far_first(count):
    return sorted(range(count), key=lambda o: (o > 0, -min(o, count - o)))


def gather_body(dp_count, bits, n, leads, order, work, *refs):
    n_swap = len(leads)
    n_work_in, n_work_out = work[0] if work else (0, 0)
    moved = n + n_swap
    ins, refs = list(refs[:moved]), refs[moved:]
    for e, lead in enumerate(leads):
        ins[n + e] = ins[n + e].at[lead]
    work_ins, refs = refs[:n_work_in], refs[n_work_in:]
    outs, refs = refs[:moved], refs[moved:]
    work_outs, refs = refs[:n_work_out], refs[n_work_out:]
    z_send, z_recv, send, recv, own_sem, swap_send, swap_recv = refs[:7]
    begin, tick, end = work[1](work_ins, work_outs, refs[7:]) if work else (None, None, None)
    d, f = lax.axis_index("dp"), lax.axis_index("fsdp")
    cuts = []
    for x in ins[:n]:
        cut = x.shape[1] // 256 * 128
        cuts.append(((0, cut), (cut, x.shape[1] - cut)))
    if work:
        begin()
    greet(dp_count, bits)
    own = [pltpu.make_async_copy(ins[a], outs[a].at[d, f], own_sem.at[a]) for a in range(n)]
    own += [
        pltpu.make_async_copy(ins[a].at[d], outs[a].at[d], own_sem.at[a])
        for a in range(n, n + n_swap)
    ]
    for copy in own:
        copy.start()
    started, arrived, waited = [], {}, set()

    def push(src, dst, send_sem, recv_sem, device_id):
        copy = pltpu.make_async_remote_copy(
            src_ref=src,
            dst_ref=dst,
            send_sem=send_sem,
            recv_sem=recv_sem,
            device_id=device_id,
            device_id_type=MESH,
        )
        copy.start()
        started.append(copy)
        return copy

    for o in order[1:]:
        for h in range(2):
            for a in range(n):
                lo, size = cuts[a][h]
                arrived[(o, 0, h, a)] = push(
                    ins[a].at[:, pl.ds(lo, size)],
                    outs[a].at[d, f, :, pl.ds(lo, size)],
                    z_send.at[o - 1, h, a],
                    z_recv.at[o - 1, h, a],
                    {"dp": lax.rem(d + o, dp_count)},
                )
    for copy in own:
        copy.wait()
    upper = list(range(1, bits))
    stages = [upper + [0], upper[::-1] + [0]]
    masks = [[[0]], [[0]]]
    for h in range(2):
        for s in range(bits):
            masks[h].append(masks[h][s] + [m ^ (1 << stages[h][s]) for m in masks[h][s]])
    slot, group = 0, 0
    for t in range(dp_count + bits - 1):
        for i in range(dp_count):
            s, o = t - i, order[i]
            if not 0 <= s < bits:
                continue
            if work:
                tick(group, dp_count * bits)
                group += 1
            for k in range(len(masks[0][s])):
                for h in range(2):
                    mask, b = masks[h][s][k], stages[h][s]
                    src_f = f
                    for bb in range(bits):
                        if mask >> bb & 1:
                            src_f = flip(src_f, bb)
                    for a in range(n):
                        key = (o, mask, h, a)
                        if key in arrived and key not in waited:
                            arrived[key].wait_recv()
                            waited.add(key)
                        lo, size = cuts[a][h]
                        src_d = lax.rem(d - o + dp_count, dp_count)
                        piece = outs[a].at[src_d, src_f, :, pl.ds(lo, size)]
                        arrived[(o, mask ^ (1 << b), h, a)] = push(
                            piece, piece, send.at[slot], recv.at[slot], {"fsdp": flip(f, b)}
                        )
                        slot += 1
        if t == 0:
            for o in order[1:]:
                peer = lax.rem(d + o, dp_count)
                for e in range(n_swap):
                    arrived[(o, e)] = push(
                        ins[n + e].at[peer],
                        outs[n + e].at[d],
                        swap_send.at[o - 1, e],
                        swap_recv.at[o - 1, e],
                        {"dp": peer},
                    )
    if work:
        end()
    for key, copy in arrived.items():
        if key not in waited:
            copy.wait_recv()
    for copy in started:
        copy.wait_send()


def gather_all(arrays, swaps, collective_id, work=None):
    work_in, work_out, work_scratch, work_body = work or ((), (), (), None)
    sizes = (len(work_in), len(work_out))
    leads, swaps = [lead for lead, _ in swaps], [x for _, x in swaps]
    dp_count, fsdp_count = lax.axis_size("dp"), lax.axis_size("fsdp")
    bits = fsdp_count.bit_length() - 1
    n, n_swap = len(arrays), len(swaps)
    order = near_first(dp_count) if work else far_first(dp_count)
    slots = 2 * dp_count * (fsdp_count - 1) * n
    total = dp_count * fsdp_count * sum(x.size * x.dtype.itemsize for x in arrays)
    return pl.pallas_call(
        functools.partial(
            gather_body, dp_count, bits, n, leads, order, (sizes, work_body) if work else None
        ),
        out_shape=[
            jax.ShapeDtypeStruct((dp_count, fsdp_count, *x.shape), x.dtype) for x in arrays
        ]
        + [jax.ShapeDtypeStruct(x.shape[1:], x.dtype) for x in swaps]
        + list(work_out),
        in_specs=[ANY] * (n + n_swap + sizes[0]),
        out_specs=[ANY] * (n + n_swap + sizes[1]),
        scratch_shapes=[
            pltpu.SemaphoreType.DMA((dp_count - 1, 2, n)),
            pltpu.SemaphoreType.DMA((dp_count - 1, 2, n)),
            pltpu.SemaphoreType.DMA((slots,)),
            pltpu.SemaphoreType.DMA((slots,)),
            pltpu.SemaphoreType.DMA((n + n_swap,)),
            pltpu.SemaphoreType.DMA((dp_count - 1, max(n_swap, 1))),
            pltpu.SemaphoreType.DMA((dp_count - 1, max(n_swap, 1))),
            *work_scratch,
        ],
        compiler_params=pltpu.CompilerParams(
            collective_id=collective_id, has_side_effects=True, vmem_limit_bytes=62 << 20
        ),
        cost_estimate=pl.CostEstimate(flops=0, bytes_accessed=20 * total, transcendentals=0),
    )(*arrays, *swaps, *work_in)


def scatter_body(dp_count, bits, pieces, kinds, *refs):
    n_in, n = len(kinds), len(pieces)
    ins, outs = refs[:n_in], refs[n_in : 2 * n_in]
    per = 6 + 2 * (bits - 1)
    scratch = [refs[2 * n_in + i * per : 2 * n_in + (i + 1) * per] for i in range(n)]
    load_sem, send, recv, store_sem = refs[2 * n_in + n * per :]
    d, f = lax.axis_index("dp"), lax.axis_index("fsdp")
    my = [bit_of(f, b) for b in range(bits)]
    upper = list(range(bits - 1, 0, -1))
    waits, fixed, ends = [None] * n, [{} for _ in range(n)], []
    greet(dp_count, bits)

    def region(i, other=None):
        return (slice(None),) + tuple(
            1 - my[b] if b == other else fixed[i].get(b, slice(None)) for b in upper
        )

    def push(i, at, src, dst, device_id):
        copy = pltpu.make_async_remote_copy(
            src_ref=src,
            dst_ref=dst,
            send_sem=send.at[i, at],
            recv_sem=recv.at[i, at],
            device_id=device_id,
            device_id_type=MESH,
        )
        copy.start()
        ends.append(copy)
        return copy

    def first(i):
        op, lo, cols = pieces[i]
        lead = (slice(None),) * bits
        own = ins[op].at[(*lead, my[0], slice(None), pl.ds(lo, cols))]
        other = ins[op].at[(*lead, 1 - my[0], slice(None), pl.ds(lo, cols))]
        load = pltpu.make_async_copy(own, scratch[i][0], load_sem.at[i])
        load.start()
        waits[i] = (load, push(i, 0, other, scratch[i][1], {"fsdp": flip(f, 0)}))

    def arrive(i, s):
        acc = scratch[i][2]
        if s == 0:
            waits[i][0].wait()
            waits[i][1].wait_recv()
            acc[...] = scratch[i][0][...].astype(f32) + scratch[i][1][...].astype(f32)
        else:
            waits[i].wait_recv()
            here = region(i)
            acc[here] = acc[here] + scratch[i][5 + 2 * s][...].astype(f32)

    def middle(i, s):
        arrive(i, s - 1)
        b = (upper if i % 2 == 0 else upper[::-1])[s - 1]
        out_buf, in_buf = scratch[i][4 + 2 * s], scratch[i][5 + 2 * s]
        out_buf[...] = scratch[i][2][region(i, b)].astype(out_buf.dtype)
        waits[i] = push(i, s, out_buf, in_buf, {"fsdp": flip(f, b)})
        fixed[i][b] = my[b]

    def last(i):
        arrive(i, bits - 1)
        out_buf, in_buf = scratch[i][3], scratch[i][4]
        waits[i] = []
        for o in near_first(dp_count)[1:]:
            peer = lax.rem(d + o, dp_count)
            out_buf[o - 1] = scratch[i][2][(peer, *region(i)[1:])].astype(out_buf.dtype)
            waits[i].append(
                push(i, bits - 1 + o, out_buf.at[o - 1], in_buf.at[o - 1], {"dp": peer})
            )

    def finish(i):
        op, lo, cols = pieces[i]
        for copy in waits[i]:
            copy.wait_recv()
        total = scratch[i][2][(d, *region(i)[1:])]
        for o in range(1, dp_count):
            total = total + scratch[i][4][o - 1].astype(f32)
        scratch[i][5][...] = total
        store = pltpu.make_async_copy(
            scratch[i][5], outs[op].at[:, pl.ds(lo, cols)], store_sem.at[i]
        )
        store.start()
        return store

    stores = []
    for t in range((n + 1) // 2 + bits + 1):
        for i in range(n):
            s = t - i // 2
            if s == 0:
                first(i)
            elif 1 <= s < bits:
                middle(i, s)
            elif s == bits:
                last(i)
            elif s == bits + 1:
                stores.append(finish(i))
    for copy in ends:
        copy.wait_send()
    for store in stores:
        store.wait()


def scatter_all(arrays, splits, collective_id):
    dp_count, fsdp_count = lax.axis_size("dp"), lax.axis_size("fsdp")
    bits = fsdp_count.bit_length() - 1
    arrays = [a.reshape(dp_count, *(2,) * bits, *a.shape[1:]) for a in arrays]
    pieces, scratch = [], []
    for op, (a, k) in enumerate(zip(arrays, splits)):
        rows, cols = a.shape[-2], a.shape[-1] // k
        half = (dp_count, *(2,) * (bits - 1), rows, cols)
        for j in range(k):
            pieces.append((op, j * cols, cols))
            scratch += [pltpu.VMEM(half, a.dtype)] * 2 + [pltpu.VMEM(half, f32)]
            scratch += [pltpu.VMEM((dp_count - 1, rows, cols), a.dtype)] * 2
            scratch += [pltpu.VMEM((rows, cols), f32)]
            for s in range(1, bits):
                shape = (dp_count, *(2,) * (bits - 1 - s), rows, cols)
                scratch += [pltpu.VMEM(shape, a.dtype)] * 2
    n, steps = len(pieces), bits - 1 + dp_count
    return pl.pallas_call(
        functools.partial(scatter_body, dp_count, bits, pieces, [a.dtype for a in arrays]),
        out_shape=[jax.ShapeDtypeStruct(a.shape[-2:], f32) for a in arrays],
        in_specs=[ANY] * len(arrays),
        out_specs=[ANY] * len(arrays),
        scratch_shapes=scratch
        + [
            pltpu.SemaphoreType.DMA((n,)),
            pltpu.SemaphoreType.DMA((n, steps)),
            pltpu.SemaphoreType.DMA((n, steps)),
            pltpu.SemaphoreType.DMA((n,)),
        ],
        compiler_params=pltpu.CompilerParams(
            collective_id=collective_id, has_side_effects=True, vmem_limit_bytes=60 << 20
        ),
    )(*arrays)


def exchange(values):
    return lax.all_to_all(values, "dp", split_axis=0, concat_axis=0, tiled=True)


def params(limit_mib=60):
    return pltpu.CompilerParams(vmem_limit_bytes=limit_mib << 20)


def whole(shape):
    return pl.BlockSpec(shape, lambda i: (0,) * len(shape), pipeline_mode=pl.Buffered(1))


def matmul(left, right):
    return jnp.dot(left, right, preferred_element_type=f32)


def rows_inner(left, right):
    return lax.dot_general(left, right, (((0,), (0,)), ((), ())), preferred_element_type=f32)


def cols_inner(left, right):
    return lax.dot_general(left, right, (((1,), (1,)), ((), ())), preferred_element_type=f32)


def gelu_and_slope(values):
    phi = 0.5 * (1.0 + lax.erf(values * 0.7071067811865476))
    return (
        values * phi,
        phi + values * jnp.exp(-0.5 * values * values) * 0.3989422804014327,
    )


def centred_rows(tokens_ref, rows):
    inputs = tokens_ref[...].reshape(rows, tokens_ref.shape[-1]).astype(f32)
    centred = inputs - jnp.mean(inputs, axis=1, keepdims=True)
    variance = jnp.mean(centred * centred, axis=1, keepdims=True)
    return inputs, centred, lax.rsqrt(variance + epsilon)


def channels_from_rows(ref, values, seqs, chunk, own):
    for place in range(ref.shape[0]):
        for s in range(seqs):
            ref[place, :, s * own : (s + 1) * own] = values[
                s * chunk : (s + 1) * chunk, place * own : (place + 1) * own
            ].astype(ref.dtype)


def rows_from_channels(ref, scratch, seqs, chunk, own):
    for place in range(ref.shape[0]):
        for s in range(seqs):
            scratch[s * chunk : (s + 1) * chunk, place * own : (place + 1) * own] = ref[
                place, :, s * own : (s + 1) * own
            ]


def reduce_body(dims, tokens_ref, gain_ref, bias_ref, weight_ref, normed_ref, out_ref, slope_ref):
    seqs, chunk, own = dims
    _, centred, inverse_std = centred_rows(tokens_ref, seqs * chunk)
    normed = (centred * inverse_std * gain_ref[...] + bias_ref[...]).astype(bf16)
    normed_ref[...] = normed
    reduced, slope = gelu_and_slope(matmul(normed, weight_ref[...]))
    slope_ref[...] = slope
    channels_from_rows(out_ref, reduced, seqs, chunk, own)


def gate_work(normed, weight):
    (rows, width), gate_width = normed[0].shape, weight.shape[1]
    micro_count, tile = len(normed), 512
    across, down = gate_width // tile, rows // tile
    count = micro_count * across * down

    def body(ins, outs, scratch):
        rows_refs, weight_ref = ins[:-1], ins[-1]
        rows_buf, weight_buf, out_buf, load_sem, store_sem = scratch
        loads = [
            pltpu.make_async_copy(rows_refs[m], rows_buf.at[pl.ds(m * rows, rows)], load_sem.at[m])
            for m in range(micro_count)
        ]
        loads.append(
            pltpu.make_async_copy(weight_ref, weight_buf, load_sem.at[micro_count])
        )
        loaded = []

        def stores(k):
            at = (
                pl.ds(pl.multiple_of(lax.div(k, across) * tile, tile), tile),
                pl.ds(pl.multiple_of(lax.rem(k, across) * tile, tile), tile),
            )
            slot = lax.rem(k, 2)
            return [
                pltpu.make_async_copy(out_buf.at[slot, r], outs[r].at[at], store_sem.at[slot, r])
                for r in range(2)
            ]

        def begin():
            for copy in loads:
                copy.start()

        def step(k, carry):
            @pl.when(k >= 2)
            def _():
                for copy in stores(k - 2):
                    copy.wait()

            slot = lax.rem(k, 2)
            left = rows_buf[pl.ds(pl.multiple_of(lax.div(k, across) * tile, tile), tile), :]
            right = weight_buf[:, pl.ds(pl.multiple_of(lax.rem(k, across) * tile, tile), tile)]
            gate, slope = gelu_and_slope(matmul(left, right))
            out_buf[slot, 0] = gate.astype(bf16)
            out_buf[slot, 1] = slope.astype(bf16)
            for copy in stores(k):
                copy.start()
            return carry

        def tick(group, groups):
            if not loaded:
                for copy in loads:
                    copy.wait()
                loaded.append(True)
            lax.fori_loop(count * group // groups, count * (group + 1) // groups, step, 0)

        def end():
            for k in (count - 2, count - 1):
                for copy in stores(k):
                    copy.wait()

        return begin, tick, end

    shape = jax.ShapeDtypeStruct((micro_count * rows, gate_width), bf16)
    scratch = [
        pltpu.VMEM((micro_count * rows, width), bf16),
        pltpu.VMEM((width, gate_width), bf16),
        pltpu.VMEM((2, 2, tile, tile), bf16),
        pltpu.SemaphoreType.DMA((micro_count + 1,)),
        pltpu.SemaphoreType.DMA((2, 2)),
    ]
    return [*normed, weight], [shape, shape], scratch, body


def middle_body(
    dims, teachers, tile, order_ref, scale_ref, state_ref, gate_ref, slope_ref, expand_ref, weight_ref,
    tokens_ref, cotangent_ref, weights_ref, *refs,
):
    seqs, chunk, own = dims
    teach_refs, refs = refs[:teachers], refs[teachers:]
    (state_out_ref, product_ref, branch_grad_ref, expanded_grad_ref, gate_grad_ref, out_ref,
     full_grad_ref, error_ref, mixed_grad_ref, expanded_ref) = refs[-10:]
    rows, width = seqs * chunk, tokens_ref.shape[-1]
    rows_from_channels(state_ref, state_out_ref, seqs, chunk, own)
    state_out = state_out_ref[...]
    tiles = [slice(j * tile, (j + 1) * tile) for j in range(gate_ref.shape[1] // tile)]
    branch = jnp.zeros((rows, width), f32)
    for at in tiles:
        expanded = matmul(state_out, expand_ref[:, at])
        expanded_ref[:, at] = expanded
        product = (expanded * gate_ref[:, at].astype(f32)).astype(bf16)
        product_ref[:, at] = product
        branch = branch + matmul(product, weight_ref[at, :])
    valid, keep = weights_ref[:, :1], weights_ref[:, 1:]
    full = tokens_ref[...].reshape(rows, width).astype(f32) + valid * branch
    out_ref[...] = full.astype(bf16).reshape(out_ref.shape)
    errors = full - jnp.concatenate([t[0] for t in teach_refs], axis=0).astype(f32)
    error_ref[0] = jnp.sum((keep * errors * errors).reshape(rows // 8, 8, width), axis=0)
    full_grad = cotangent_ref[...].reshape(rows, width).astype(f32) + keep * errors * scale_ref[0]
    full_grad_ref[...] = full_grad.astype(bf16)
    branch_grad = (valid * full_grad).astype(bf16)
    branch_grad_ref[...] = branch_grad
    mixed_grad = jnp.zeros((rows, state_out.shape[1]), f32)
    for at in tiles:
        product_grad = cols_inner(branch_grad, weight_ref[at, :])
        expanded_grad = (product_grad * gate_ref[:, at].astype(f32)).astype(bf16)
        expanded_grad_ref[:, at] = expanded_grad
        gate_grad_ref[:, at] = (
            product_grad * expanded_ref[:, at] * slope_ref[:, at].astype(f32)
        ).astype(bf16)
        mixed_grad = mixed_grad + cols_inner(expanded_grad, expand_ref[:, at])
    channels_from_rows(mixed_grad_ref, mixed_grad, seqs, chunk, own)


def input_body(
    dims, back_ref, slope_ref, gate_grad_ref, gate_weight_ref, reduce_weight_ref, tokens_ref,
    gain_ref, full_grad_ref, *refs,
):
    out_ref, reduced_grad_ref, gain_grad_ref, bias_grad_ref, back_rows_ref = refs[-5:]
    seqs, chunk, own = dims
    rows, width = seqs * chunk, tokens_ref.shape[-1]
    rows_from_channels(back_ref, back_rows_ref, seqs, chunk, own)
    reduced_grad = (back_rows_ref[...].astype(f32) * slope_ref[...]).astype(bf16)
    reduced_grad_ref[...] = reduced_grad
    normed_grad = cols_inner(gate_grad_ref[...], gate_weight_ref[...]) + cols_inner(
        reduced_grad, reduce_weight_ref[...]
    )
    _, centred, inverse_std = centred_rows(tokens_ref, rows)
    unit = centred * inverse_std
    gain_grad_ref[0] = jnp.sum((normed_grad * unit).reshape(rows // 8, 8, width), axis=0)
    bias_grad_ref[0] = jnp.sum(normed_grad.reshape(rows // 8, 8, width), axis=0)
    unit_grad = normed_grad * gain_ref[...]
    result = full_grad_ref[...].astype(f32) + inverse_std * (
        unit_grad
        - jnp.mean(unit_grad, axis=1, keepdims=True)
        - unit * jnp.mean(unit_grad * unit, axis=1, keepdims=True)
    )
    out_ref[...] = result.astype(bf16).reshape(out_ref.shape)


def product_scatter_body(dp_count, bits, plan, n_left, n_right, *refs):
    pieces, slots, lane, micros = plan["pieces"], plan["slots"], plan["lane"], plan["micros"]
    n = len(pieces)
    lefts, refs = refs[: n_left * micros], refs[n_left * micros :]
    rights, refs = refs[: n_right * micros], refs[n_right * micros :]
    parts = plan["parts"]
    ready_refs, small_ref, refs = refs[:parts], refs[parts], refs[parts + 1 :]
    part_width = ready_refs[0].shape[-1]
    outs, refs = refs[: plan["outputs"]], refs[plan["outputs"] :]
    left_bufs, refs = refs[:n_left], refs[n_left:]
    right_buf, left_sem, right_sem, load_sem, ready_sem, send, recv, store_sem = refs[:8]
    sets = [refs[8 : 8 + 5 + 3 * (bits - 1)], refs[8 + 5 + 3 * (bits - 1) :]]
    d, f = lax.axis_index("dp"), lax.axis_index("fsdp")
    my = [bit_of(f, b) for b in range(bits)]
    upper = list(range(bits - 1, 0, -1))
    small = n - 1

    def buffers(i):
        if i == small:
            return list(sets[1])
        _, rows, groups, _ = pieces[i]
        height, slot = rows * groups, i % slots
        views = []
        for k, ref in enumerate(sets[0]):
            arriving = k in (1, 3) or (k >= 5 and (k - 5) % 3 == 2)
            lead = (slice(None),) * (len(ref.shape) - 3)
            views.append(ref.at[(i if arriving else slot, *lead, pl.ds(0, height), slice(None))])
        return views

    bufs = [buffers(i) for i in range(n)]
    orders = [upper if i % 2 == 0 else upper[::-1] for i in range(n)]
    pushed, drained, waits, stores = {}, set(), [None] * n, {}

    def push(i, at, src, dst, device_id):
        copy = pltpu.make_async_remote_copy(
            src_ref=src,
            dst_ref=dst,
            send_sem=send.at[i, at],
            recv_sem=recv.at[i, at],
            device_id=device_id,
            device_id_type=MESH,
        )
        copy.start()
        pushed[(i, at)] = copy
        return copy

    def drain(i, *ats):
        for at in ats:
            if i >= 0 and i != small and (i, at) in pushed and (i, at) not in drained:
                pushed[(i, at)].wait_send()
                drained.add((i, at))

    ready = plan["ready"]
    jobs = [(i, *job) for i in range(ready, n - 1) for job in pieces[i][3]]
    loads = {}

    def fetch(j):
        if j < len(jobs):
            _, _, right, lo, cols, _ = jobs[j]
            loads[j] = [
                pltpu.make_async_copy(
                    rights[right * micros + m].at[:, pl.ds(lo, cols)],
                    right_buf.at[j % 2, m, :, pl.ds(0, cols)],
                    right_sem.at[j % 2, m],
                )
                for m in range(micros)
            ]
            for copy in loads[j]:
                copy.start()

    left_waited = set()
    left_loads = [
        [
            pltpu.make_async_copy(lefts[a * micros + m], left_bufs[a].at[m], left_sem.at[a, m])
            for m in range(micros)
        ]
        for a in range(n_left)
    ]
    small_load = pltpu.make_async_copy(small_ref, sets[1][0], load_sem)
    small_load.start()
    lead = (slice(None),) * (bits + 1)
    ready_loads = []
    for i in range(ready):
        _, rows, groups, piece_jobs = pieces[i]
        ready_loads.append(
            [
                pltpu.make_async_copy(
                    ready_refs[piece_jobs[0][2] // part_width].at[
                        (*lead, slice(None), pl.ds(piece_jobs[0][2] % part_width + g * lane, lane))
                    ],
                    bufs[i][0].at[(*lead, pl.ds(g * rows, rows), slice(None))],
                    ready_sem.at[i, g],
                )
                for g in range(groups)
            ]
        )
        for copy in ready_loads[i]:
            copy.start()
    for a in range(n_left):
        for copy in left_loads[a]:
            copy.start()
        if a < 2:
            fetch(a)
    greet(dp_count, bits)

    def make(i):
        _, rows, groups, piece_jobs = pieces[i]
        made = bufs[i][0]
        drain(i - slots, 0)
        for j, job in enumerate(jobs):
            if job[0] != i:
                continue
            _, left, right, lo, cols, at_group = job
            if left not in left_waited:
                for copy in left_loads[left]:
                    copy.wait()
                left_waited.add(left)
            for copy in loads[j]:
                copy.wait()
            height = rows << bits

            def tile(p, carry, left=left, cols=cols, at_group=at_group, j=j, height=height):
                total = None
                for m in range(left_bufs[left].shape[0]):
                    part = rows_inner(
                        left_bufs[left][m, :, pl.ds(pl.multiple_of(p * height, 128), height)],
                        right_buf[j % 2, m, :, :cols],
                    )
                    total = part if total is None else total + part
                total = total.astype(bf16)
                for g in range(cols // lane):
                    block = total[:, g * lane : (g + 1) * lane].reshape(*(2,) * bits, rows, lane)
                    lead = (slice(None),) * bits
                    made[(p, *lead, pl.ds((at_group + g) * rows, rows), slice(None))] = block
                return carry

            lax.fori_loop(0, dp_count, tile, 0)
            fetch(j + 2)

    def first(i):
        made, got = bufs[i][0], bufs[i][1]
        if i == small:
            small_load.wait()
        elif i < ready:
            for copy in ready_loads[i]:
                copy.wait()
        else:
            make(i)
        lead = (slice(None),) * bits
        waits[i] = push(i, 0, made.at[(*lead, 1 - my[0])], got, {"fsdp": flip(f, 0)})

    def held(i, s):
        waits[i].wait_recv()
        if s == 0:
            lead = (slice(None),) * bits
            return bufs[i][0].at[(*lead, my[0])], bufs[i][1]
        return bufs[i][5 + 3 * (s - 1)], bufs[i][5 + 3 * (s - 1) + 2]

    def middle(i, s):
        own, more = held(i, s - 1)
        b = orders[i][s - 1]
        left = [q for q in upper if q not in orders[i][: s - 1]]
        kept, sent, arriving = bufs[i][5 + 3 * (s - 1) : 8 + 3 * (s - 1)]

        def side(value):
            return (slice(None),) + tuple(value if q == b else slice(None) for q in left)

        drain(i - slots, s)
        theirs, mine = side(1 - my[b]), side(my[b])
        sent[...] = (own[theirs].astype(f32) + more[theirs].astype(f32)).astype(sent.dtype)
        waits[i] = push(i, s, sent, arriving, {"fsdp": flip(f, b)})
        kept[...] = own[mine].astype(f32) + more[mine].astype(f32)

    def last(i):
        own, more = held(i, bits - 1)
        to_dp, from_dp = bufs[i][2], bufs[i][3]
        drain(i - slots, *range(bits, bits + dp_count - 1))
        copies = []
        for o in near_first(dp_count)[1:]:
            peer = lax.rem(d + o, dp_count)
            to_dp[o - 1] = (own[peer] + more[peer].astype(f32)).astype(to_dp.dtype)
            copies.append(
                push(i, bits - 1 + o, to_dp.at[o - 1], from_dp.at[o - 1], {"dp": peer})
            )
        waits[i] = copies
        for store in stores.pop(i - slots, []):
            store.wait()
        bufs[i][4][...] = own[d] + more[d].astype(f32)

    def finish(i):
        result, from_dp = bufs[i][4], bufs[i][3]
        for copy in waits[i]:
            copy.wait_recv()
        total = result[...]
        for o in range(1, dp_count):
            total = total + from_dp[o - 1].astype(f32)
        result[...] = total
        out, rows, groups, piece_jobs = pieces[i]
        stores[i] = []
        if i == small:
            stores[i].append(pltpu.make_async_copy(result, outs[out], store_sem.at[i, 0]))
        else:
            lo = piece_jobs[0][2]
            for g in range(groups):
                stores[i].append(
                    pltpu.make_async_copy(
                        result.at[pl.ds(g * rows, rows)],
                        outs[out].at[:, pl.ds(lo + g * lane, lane)],
                        store_sem.at[i, g],
                    )
                )
        for store in stores[i]:
            store.start()

    for t in range((n + 1) // 2 + bits + 1):
        for s in (*range(1, bits + 2), 0):
            for i in range(2 * (t - s), min(2 * (t - s) + 2, n)):
                if i < 0:
                    continue
                if s == 0:
                    first(i)
                elif s < bits:
                    middle(i, s)
                elif s == bits:
                    last(i)
                else:
                    finish(i)
    for key, copy in pushed.items():
        if key not in drained:
            copy.wait_send()
    for group in stores.values():
        for store in group:
            store.wait()


def product_scatter(lefts, rights, ready, small, collective_id):
    dp_count, fsdp_count = lax.axis_size("dp"), lax.axis_size("fsdp")
    bits = fsdp_count.bit_length() - 1
    devices = dp_count * fsdp_count
    lane, slots, height = 256, 4, 96
    unique = []
    for left in lefts:
        if not any(left is u for u in unique):
            unique.append(left)
    pieces = []
    for k, (left, right) in enumerate(zip(lefts, rights)):
        at = next(a for a, u in enumerate(unique) if u is left)
        rows, width = left[0].shape[1] // devices, right[0].shape[1]
        per_piece = min(height // rows, width // lane)
        for lo in range(0, width, per_piece * lane):
            groups = min(per_piece, (width - lo) // lane)
            jobs = [
                (at, k, lo + g * lane, min(3, groups - g) * lane, g) for g in range(0, groups, 3)
            ]
            pieces.append((k, rows, groups, jobs))
    pieces.append((len(lefts), small.shape[1], 1, []))
    n = len(pieces)
    plan = {
        "pieces": pieces,
        "slots": slots,
        "lane": lane,
        "outputs": len(lefts) + 1,
        "micros": len(lefts[0]),
        "ready": sum(1 for k, _, _, jobs in pieces[:-1] if k == 0 and jobs[-1][2] + jobs[-1][3] <= sum(x.shape[1] for x in ready)),
        "parts": len(ready),
    }

    def buffer_set(count, lead, rows, columns, dtype):
        def shaped(many, *dims):
            return (many, *dims, rows, columns) if lead else (*dims, rows, columns)

        halved = [(2,) * (bits - 1 - s) for s in range(bits)]
        result = [
            pltpu.VMEM(shaped(slots, dp_count, *(2,) * bits), dtype),
            pltpu.VMEM(shaped(count, dp_count, *halved[0]), dtype),
            pltpu.VMEM(shaped(slots, dp_count - 1), dtype),
            pltpu.VMEM(shaped(count, dp_count - 1), dtype),
            pltpu.VMEM(shaped(slots), f32),
        ]
        for s in range(1, bits):
            result += [
                pltpu.VMEM(shaped(slots, dp_count, *halved[s]), f32),
                pltpu.VMEM(shaped(slots, dp_count, *halved[s]), dtype),
                pltpu.VMEM(shaped(count, dp_count, *halved[s]), dtype),
            ]
        return result

    micro_count, rows = len(lefts[0]), lefts[0][0].shape[0]
    steps = bits - 1 + dp_count
    small = small.reshape(dp_count, *(2,) * bits, *small.shape[1:])
    ready = [x.reshape(dp_count, *(2,) * bits, -1, x.shape[1]) for x in ready]
    widths = [(a[0].shape[1], b[0].shape[1]) for a, b in zip(lefts, rights)]
    flops = sum(2 * micro_count * rows * a * b for a, b in widths)
    return pl.pallas_call(
        functools.partial(product_scatter_body, dp_count, bits, plan, len(unique), len(rights)),
        out_shape=[jax.ShapeDtypeStruct((a // devices, b), f32) for a, b in widths]
        + [jax.ShapeDtypeStruct(small.shape[-2:], f32)],
        in_specs=[ANY] * ((len(unique) + len(rights)) * micro_count + len(ready) + 1),
        out_specs=[ANY] * (len(lefts) + 1),
        scratch_shapes=[pltpu.VMEM((micro_count, *u[0].shape), bf16) for u in unique]
        + [
            pltpu.VMEM((2, micro_count, rows, 3 * lane), bf16),
            pltpu.SemaphoreType.DMA((len(unique), micro_count)),
            pltpu.SemaphoreType.DMA((2, micro_count)),
            pltpu.SemaphoreType.DMA,
            pltpu.SemaphoreType.DMA((slots, height // 16)),
            pltpu.SemaphoreType.DMA((n, steps)),
            pltpu.SemaphoreType.DMA((n, steps)),
            pltpu.SemaphoreType.DMA((n, height // 16)),
        ]
        + buffer_set(n - 1, True, height, lane, bf16)
        + buffer_set(1, False, *small.shape[-2:], f32),
        compiler_params=pltpu.CompilerParams(
            collective_id=collective_id, has_side_effects=True, vmem_limit_bytes=62 << 20
        ),
        cost_estimate=pl.CostEstimate(flops=flops, bytes_accessed=100 << 20, transcendentals=0),
    )(*[x for u in unique for x in u], *[x for r in rights for x in r], *ready, small)


def weight_grad_body(n, *refs):
    lefts, rights, out_ref = refs[:n], refs[n : 2 * n], refs[2 * n]
    total = rows_inner(lefts[0][...], rights[0][...])
    for left, right in zip(lefts[1:], rights[1:]):
        total = total + rows_inner(left[...], right[...])
    out_ref[...] = total.astype(out_ref.dtype)


def weight_grad(lefts, rights, row_tile, width=None, part=0):
    n, (rows, height), width = len(lefts), lefts[0].shape, width or rights[0].shape[1]
    return pl.pallas_call(
        functools.partial(weight_grad_body, n),
        grid=(height // row_tile,),
        out_shape=jax.ShapeDtypeStruct((height, width), bf16),
        in_specs=[pl.BlockSpec((rows, row_tile), lambda i: (0, i))] * n
        + [pl.BlockSpec((rows, width), lambda i: (0, part), pipeline_mode=pl.Buffered(1))] * n,
        out_specs=pl.BlockSpec((row_tile, width), lambda i: (i, 0)),
        compiler_params=params(),
        cost_estimate=pl.CostEstimate(
            flops=2 * n * rows * height * width,
            bytes_accessed=2 * (n * rows * (height + width) + height * width),
            transcendentals=0,
        ),
    )(*lefts, *rights)


def fourier_table(chunk):
    freq = np.arange(chunk)[:, None]
    time = np.arange(chunk)[None, :]
    angle = (freq * time % (2 * chunk)) * (np.pi / chunk)
    sines = -np.sin(angle)
    sines[0] = 1.0 - 2.0 * (np.arange(chunk) % 2)
    table = np.concatenate([np.cos(angle), sines], axis=0)
    scaling = np.full((2 * chunk, 1), 1.0 / chunk)
    scaling[0] = scaling[chunk] = 0.5 / chunk
    sign = np.tile(1.0 - 2.0 * (np.arange(chunk) % 2), 2)
    sign[chunk] = 1.0 - 2.0 * (chunk % 2)
    return table.astype(np.float32), (table * scaling).astype(np.float32), sign.astype(np.float32)


def high_and_low(table):
    high = table.astype(jnp.bfloat16)
    return np.stack([high, (table - high.astype(np.float32)).astype(jnp.bfloat16)])


def spectrum(table_ref, values):
    return matmul(table_ref[0], values) + matmul(table_ref[1], values)


def to_time(inverse_ref, spec):
    high = spec.astype(bf16)
    low = (spec - high.astype(f32)).astype(bf16)
    return (
        rows_inner(inverse_ref[0], high)
        + rows_inner(inverse_ref[1], high)
        + rows_inner(inverse_ref[0], low)
    )


def packed_product(first, second, edge, conjugate):
    (a_re, a_im), (b_re, b_im) = first, second
    straight, crossed = a_re * b_re, a_im * b_im
    if conjugate:
        real = straight + jnp.where(edge, 0.0, crossed)
        imag = jnp.where(edge, crossed, a_re * b_im - a_im * b_re)
    else:
        real = straight - jnp.where(edge, 0.0, crossed)
        imag = jnp.where(edge, crossed, a_re * b_im + a_im * b_re)
    return real, imag


def pair_sum(pairs, edge, conjugate):
    real, imag = packed_product(*pairs[0], edge, conjugate)
    for first, second in pairs[1:]:
        more = packed_product(first, second, edge, conjugate)
        real, imag = real + more[0], imag + more[1]
    return real, imag


def halves(ref, block, at, chunk):
    return ref[block, :chunk, at], ref[block, chunk:, at]


def convolve_body(table_ref, inverse_ref, kernel_ref, rows_ref, out_ref, spec_ref, back_ref):
    blocks, chunk, columns = rows_ref.shape
    lanes = kernel_ref.shape[2]
    edge = lax.broadcasted_iota(jnp.int32, (chunk, lanes), 0) == 0
    for c in range(blocks):
        spec_ref[c] = spectrum(table_ref, rows_ref[c])
        for g in range(columns // lanes):
            at = slice(g * lanes, (g + 1) * lanes)
            everything = slice(None)
            real, imag = pair_sum(
                [
                    (halves(kernel_ref, k, everything, chunk), halves(spec_ref, c - k, at, chunk))
                    for k in range(c + 1)
                ],
                edge,
                False,
            )
            back_ref[:chunk, at], back_ref[chunk:, at] = real, imag
        out_ref[c] = to_time(inverse_ref, back_ref[...]).astype(out_ref.dtype)


def convolve_back_body(
    table_ref, inverse_ref, kernel_ref, rows_ref, grad_ref, out_ref, kernel_grad_ref,
    spec_ref, grad_spec_ref, back_ref,
):
    blocks, chunk, columns = rows_ref.shape
    lanes = kernel_ref.shape[2]
    edge = lax.broadcasted_iota(jnp.int32, (chunk, lanes), 0) == 0
    everything = slice(None)
    groups = [slice(g * lanes, (g + 1) * lanes) for g in range(columns // lanes)]
    for c in range(blocks):
        spec_ref[c] = spectrum(table_ref, rows_ref[c])
    for c in reversed(range(blocks)):
        grad_spec_ref[c] = spectrum(table_ref, grad_ref[c])
        for at in groups:
            real, imag = pair_sum(
                [
                    (
                        halves(kernel_ref, late - c, everything, chunk),
                        halves(grad_spec_ref, late, at, chunk),
                    )
                    for late in range(c, blocks)
                ],
                edge,
                True,
            )
            back_ref[:chunk, at], back_ref[chunk:, at] = real, imag
        out_ref[c] = to_time(inverse_ref, back_ref[...]).astype(out_ref.dtype)
    for k in range(blocks):
        real, imag = pair_sum(
            [
                (halves(spec_ref, c - k, at, chunk), halves(grad_spec_ref, c, at, chunk))
                for c in range(k, blocks)
                for at in groups
            ],
            edge,
            True,
        )
        kernel_grad_ref[k, :chunk], kernel_grad_ref[k, chunk:] = real, imag


def kernel_factors(decay, frequency, log_step, length):
    fine = 32
    coarse = length // fine
    step_size = jnp.exp(log_step)[:, None]
    real = (step_size * decay)[:, None, :]
    imag = (step_size * frequency)[:, None, :]
    far = (jnp.arange(coarse, dtype=jnp.int32) * fine).astype(f32)[None, :, None]
    near = jnp.arange(fine, dtype=jnp.int32).astype(f32)[None, :, None]
    far_damp, near_damp = jnp.exp(real * far), jnp.exp(real * near)
    return (
        (far_damp * jnp.cos(imag * far), far_damp * jnp.sin(imag * far)),
        (near_damp * jnp.cos(imag * near), near_damp * jnp.sin(imag * near)),
        step_size,
    )


def kernel_forward(weight_pair, factors):
    (far_re, far_im), (near_re, near_im), _ = factors
    w_re, w_im = weight_pair[0][:, None, :], weight_pair[1][:, None, :]
    left = jnp.concatenate([far_re, -far_im], axis=2)
    right = jnp.concatenate(
        [w_re * near_re - w_im * near_im, w_re * near_im + w_im * near_re], axis=2
    )
    rows = jnp.einsum("han,hbn->hab", left, right, precision=high)
    return rows.reshape(rows.shape[0], -1)


def kernel_backward(grad_rows, weight_pair, decay, frequency, factors):
    (far_re, far_im), (near_re, near_im), step_size = factors
    channels, coarse, states = far_re.shape
    fine = near_re.shape[1]
    tiles = grad_rows.reshape(channels, coarse, fine)
    near_index = jnp.arange(fine, dtype=jnp.int32).astype(f32)
    far_index = (jnp.arange(coarse, dtype=jnp.int32) * fine).astype(f32)[None, :, None]
    stacked = jnp.concatenate([tiles, tiles * near_index], axis=1)
    part = jnp.einsum(
        "hab,hbn->han", stacked, jnp.concatenate([near_re, near_im], axis=2), precision=high
    )
    u_re, u_im = part[:, :coarse, :states], part[:, :coarse, states:]
    v_re = part[:, coarse:, :states] + far_index * u_re
    v_im = part[:, coarse:, states:] + far_index * u_im
    s_re = jnp.sum(far_re * u_re - far_im * u_im, axis=1)
    s_im = jnp.sum(far_re * u_im + far_im * u_re, axis=1)
    t_re = jnp.sum(far_re * v_re - far_im * v_im, axis=1)
    t_im = jnp.sum(far_re * v_im + far_im * v_re, axis=1)
    w_re, w_im = weight_pair[0], weight_pair[1]
    along_re = step_size * (w_re * t_re - w_im * t_im)
    along_im = -step_size * (w_re * t_im + w_im * t_re)
    return (
        jnp.stack([s_re, -s_im]),
        along_re,
        along_im,
        jnp.sum(decay * along_re + frequency * along_im, axis=1),
    )


def shards(
    tokens,
    cotangent,
    teacher,
    lengths,
    dealing,
    loss_mask,
    norm_gain,
    norm_bias,
    gate_weight,
    reduce_weight,
    state_weight,
    decay_rate,
    frequency,
    log_step,
    expand_weight,
    out_weight,
):
    dp_count, fsdp_count = lax.axis_size("dp"), lax.axis_size("fsdp")
    devices = dp_count * fsdp_count
    group_index = lax.axis_index("fsdp")
    dp_place = lax.axis_index("dp")
    micro_count, seqs, chunk, width = tokens.shape
    rows = seqs * chunk
    seq_length = chunk * dp_count
    gate_width = gate_weight.shape[1]
    reduced_width = reduce_weight.shape[1]
    own = reduced_width // dp_count
    lanes = max(own, 128)
    share = norm_gain.shape[0]
    micros = range(micro_count)
    direct = own % 128 == 0

    small = jnp.pad(jnp.stack([norm_gain, norm_bias]), ((0, 14), (0, 256 - share)))
    mask_rows = loss_mask.reshape(micro_count, dp_count, chunk).transpose(1, 0, 2)
    mask_rows = jnp.pad(mask_rows, ((0, 0), (0, 8 - micro_count), (0, 0)))
    teacher_rows = teacher.reshape(micro_count, dp_count, chunk, width)
    w_gate, w_reduce, small, *swapped = gather_all(
        [gate_weight, reduce_weight, small],
        [(0, mask_rows[None]), *[(m, teacher_rows) for m in micros[1:]]],
        1,
    )
    masked = swapped[0].transpose(1, 0, 2)[:micro_count]
    w_gate = w_gate.reshape(width, gate_width)
    w_reduce = w_reduce.reshape(width, reduced_width)
    gain_row = small[:, :, 0, :share].reshape(1, width).astype(f32)
    bias_row = small[:, :, 1, :share].reshape(1, width).astype(f32)

    per_block = max(1, 512 // chunk)
    steps = seqs // per_block
    middle_block = max(1, 256 // chunk)
    middle_steps = seqs // middle_block

    def row_spec(columns, count=per_block):
        return pl.BlockSpec((count * chunk, columns), lambda i, *_: (i, 0))

    def shared(shape, block):
        return pl.BlockSpec(shape, lambda i, *_: block, pipeline_mode=pl.Buffered(1))

    lane_shape = (dp_count, chunk, seqs * own)
    if not direct:
        lane_shape = (1, rows, reduced_width)

    def dims(count):
        return (count, chunk, own) if direct else (1, count * chunk, reduced_width)

    def lane_spec(count):
        if direct:
            return pl.BlockSpec((dp_count, chunk, count * own), lambda i, *_: (0, 0, i))
        return pl.BlockSpec((1, count * chunk, reduced_width), lambda i, *_: (0, i, 0))

    def tokens_spec(m, count):
        return pl.BlockSpec((None, count, chunk, width), lambda i, *_: (m, i, 0, 0))

    def send_lanes(values):
        if not direct:
            values = values.reshape(seqs, chunk, dp_count, own).transpose(2, 1, 0, 3)
            values = values.reshape(dp_count, chunk, seqs * own)
        return exchange(values)

    def receive_lanes(values):
        values = exchange(values)
        if not direct:
            values = values.reshape(dp_count, chunk, seqs, own).transpose(2, 1, 0, 3)
            values = values.reshape(1, rows, reduced_width)
        return values

    def reduce_rows(m, gain_row):
        return pl.pallas_call(
            functools.partial(reduce_body, dims(per_block)),
            grid=(steps,),
            out_shape=[
                jax.ShapeDtypeStruct((rows, width), bf16),
                jax.ShapeDtypeStruct(lane_shape, bf16),
                jax.ShapeDtypeStruct((rows, reduced_width), f32),
            ],
            in_specs=[
                tokens_spec(m, per_block),
                whole((1, width)),
                whole((1, width)),
                whole((width, reduced_width)),
            ],
            out_specs=[row_spec(width), lane_spec(per_block), row_spec(reduced_width)],
            compiler_params=params(),
            cost_estimate=pl.CostEstimate(
                flops=2 * rows * width * reduced_width,
                bytes_accessed=8 * rows * width,
                transcendentals=2 * rows * reduced_width,
            ),
        )(tokens, gain_row, bias_row, w_reduce)

    local_ids = group_index * seqs + jnp.arange(seqs, dtype=jnp.int32)
    targets = jnp.take(dealing, local_ids, axis=1)
    own_lengths = jnp.take(lengths, local_ids, axis=1)
    positions = dp_place * chunk + jnp.arange(chunk, dtype=jnp.int32)
    valid = (positions[None, None, :] < own_lengths[:, :, None]).astype(f32)
    keep = jnp.take_along_axis(masked, targets[:, :, None], axis=1).astype(f32) * valid
    own_count = jnp.sum(keep)
    row_weights = jnp.stack([valid, keep], axis=-1).reshape(micro_count, rows, 2)
    counts = jnp.full((8, 256), own_count, f32)
    row_weights = [row_weights[m] for m in micros]

    reduced_rows = [reduce_rows(0, gain_row)]
    held = lax.optimization_barrier((decay_rate, frequency, log_step, reduced_rows[0][1]))
    factors = kernel_factors(*held[:3], seq_length)
    own_kernel = kernel_forward(state_weight, factors)
    for m in micros[1:]:
        later_gain, own_kernel, row_weights, targets, counts = lax.optimization_barrier(
            (gain_row, own_kernel, row_weights, targets, counts)
        )
        reduced_rows.append(reduce_rows(m, later_gain))
    normed, lanes_out, slope_reduced = zip(*reduced_rows)
    lanes_in = [send_lanes(x) for x in lanes_out]


    table_np, inverse_np, sign_np = fourier_table(chunk)
    sign = jnp.asarray(sign_np)[:, None]
    table2, inverse2 = jnp.asarray(high_and_low(table_np)), jnp.asarray(high_and_low(inverse_np))
    kernel = lax.all_gather(own_kernel, "fsdp", axis=0, tiled=True)
    segments = jnp.einsum(
        "kt,hct->ckh", jnp.asarray(table_np), kernel.reshape(own, dp_count, chunk), precision=high
    )
    previous = jnp.concatenate([jnp.zeros_like(segments[:1]), segments[:-1]], axis=0)
    kernel_spec = jnp.tile(segments + sign * previous, (1, 1, lanes // own))

    blocks = (dp_count, chunk, seqs * own)
    spec_scratch = pltpu.VMEM((dp_count, 2 * chunk, seqs * own), f32)
    back_scratch = pltpu.VMEM((2 * chunk, seqs * own), f32)
    transform_flops = 8 * chunk * chunk * dp_count * seqs * own

    def convolve(values):
        return pl.pallas_call(
            convolve_body,
            out_shape=jax.ShapeDtypeStruct(blocks, bf16),
            scratch_shapes=[spec_scratch, back_scratch],
            compiler_params=params(),
            cost_estimate=pl.CostEstimate(
                flops=5 * transform_flops // 2, bytes_accessed=8 << 20, transcendentals=0
            ),
        )(table2, inverse2, kernel_spec, values)

    def convolve_back(values, grads):
        return pl.pallas_call(
            convolve_back_body,
            out_shape=[
                jax.ShapeDtypeStruct(blocks, bf16),
                jax.ShapeDtypeStruct((dp_count, 2 * chunk, lanes), f32),
            ],
            scratch_shapes=[spec_scratch, spec_scratch, back_scratch],
            compiler_params=params(),
            cost_estimate=pl.CostEstimate(
                flops=7 * transform_flops // 2, bytes_accessed=8 << 20, transcendentals=0
            ),
        )(table2, inverse2, kernel_spec, values, grads)

    convolved = [convolve(x) for x in lanes_in]
    late = lax.optimization_barrier((expand_weight, out_weight, *convolved))
    w_expand, w_out, counts, *more, gate, slope = gather_all(
        [late[0], late[1], counts],
        [(0, teacher_rows)],
        2,
        gate_work(normed, w_gate),
    )
    teach = [*more, *swapped[1:]]
    w_expand = w_expand.reshape(reduced_width, gate_width)
    w_out = w_out.reshape(gate_width, width)
    count = jnp.sum(counts[:, :, 0, 0])
    error_scale = (2.0 / (width * count)).reshape(1)
    mixed = [receive_lanes(x) for x in convolved]
    def middle_rows(m, *earlier):
        teach_specs = [
            pl.BlockSpec((1, chunk, width), functools.partial(teach_block, s)) for s in range(middle_block)
        ]
        gate_spec = pl.BlockSpec(
            (middle_block * chunk, gate_width), lambda i, *_: (m * middle_steps + i, 0)
        )
        wide, narrow = row_spec(gate_width, middle_block), row_spec(width, middle_block)
        return pl.pallas_call(
            functools.partial(middle_body, dims(middle_block), middle_block, 768),
            grid_spec=pltpu.PrefetchScalarGridSpec(
                num_scalar_prefetch=2,
                grid=(middle_steps,),
                in_specs=[
                    lane_spec(middle_block),
                    gate_spec,
                    gate_spec,
                    shared((reduced_width, gate_width), (0, 0)),
                    shared((gate_width, width), (0, 0)),
                    tokens_spec(m, middle_block),
                    tokens_spec(m, middle_block),
                    row_spec(2, middle_block),
                    *teach_specs,
                    *[ANY] * len(earlier),
                ],
                out_specs=[
                    row_spec(reduced_width, middle_block),
                    wide,
                    narrow,
                    wide,
                    wide,
                    tokens_spec(m, middle_block),
                    narrow,
                    pl.BlockSpec((1, 8, width), lambda i, *_: (i, 0, 0)),
                    lane_spec(middle_block),
                ],
                scratch_shapes=[pltpu.VMEM((middle_block * chunk, gate_width), f32)],
            ),
            out_shape=[
                jax.ShapeDtypeStruct((rows, reduced_width), bf16),
                jax.ShapeDtypeStruct((rows, gate_width), bf16),
                jax.ShapeDtypeStruct((rows, width), bf16),
                jax.ShapeDtypeStruct((rows, gate_width), bf16),
                jax.ShapeDtypeStruct((rows, gate_width), bf16),
                jax.ShapeDtypeStruct(tokens.shape, bf16),
                jax.ShapeDtypeStruct((rows, width), bf16),
                jax.ShapeDtypeStruct((middle_steps, 8, width), f32),
                jax.ShapeDtypeStruct(lane_shape, bf16),
            ],
            input_output_aliases={10 + middle_block: 5} if earlier else {},
            compiler_params=params(),
            cost_estimate=pl.CostEstimate(
                flops=4 * rows * gate_width * (width + reduced_width),
                bytes_accessed=10 * rows * gate_width + 16 * rows * width,
                transcendentals=0,
            ),
        )(
            targets[m], error_scale, mixed[m], gate, slope, w_expand, w_out, tokens, cotangent,
            row_weights[m], *[teach[m]] * middle_block, *earlier,
        )

    def teach_block(s, i, order, scale):
        return (order[i * middle_block + s], 0, 0)

    def input_rows(m, back, gate_grad, full_grad, *earlier):
        eight = pl.BlockSpec((1, 8, width), lambda i, *_: (i, 0, 0))
        return pl.pallas_call(
            functools.partial(input_body, dims(middle_block)),
            grid=(middle_steps,),
            in_specs=[
                lane_spec(middle_block),
                row_spec(reduced_width, middle_block),
                row_spec(gate_width, middle_block),
                shared((width, gate_width), (0, 0)),
                shared((width, reduced_width), (0, 0)),
                tokens_spec(m, middle_block),
                whole((1, width)),
                row_spec(width, middle_block),
                *[ANY] * len(earlier),
            ],
            out_specs=[tokens_spec(m, middle_block), row_spec(reduced_width, middle_block), eight, eight],
            out_shape=[
                jax.ShapeDtypeStruct(tokens.shape, bf16),
                jax.ShapeDtypeStruct((rows, reduced_width), bf16),
                jax.ShapeDtypeStruct((middle_steps, 8, width), f32),
                jax.ShapeDtypeStruct((middle_steps, 8, width), f32),
            ],
            scratch_shapes=[pltpu.VMEM((middle_block * chunk, reduced_width), bf16)],
            input_output_aliases={8: 0} if earlier else {},
            compiler_params=params(),
            cost_estimate=pl.CostEstimate(
                flops=2 * rows * width * (gate_width + reduced_width),
                bytes_accessed=4 * rows * gate_width + 8 * rows * width,
                transcendentals=0,
            ),
        )(back, slope_reduced[m], gate_grad, w_gate, w_reduce, tokens, gain_row, full_grad, *earlier)

    middle = []
    for m in micros:
        middle.append(middle_rows(m, *[x[5] for x in middle[-1:]]))
    outputs = middle[-1][5]
    state_out, product, branch_grad, expanded_grad, gate_grad, _, full_grad, error_rows, lane_grad = zip(*middle)
    grads_in = [send_lanes(x) for x in lane_grad]
    back, kernel_grads = zip(*[convolve_back(lanes_in[m], grads_in[m]) for m in micros])
    ready, held_back = [], []
    for m in micros:
        part = weight_grad(normed, gate_grad, 256, gate_width // micro_count, m)
        held, part = lax.optimization_barrier((back[m], part))
        held_back.append(held)
        ready.append(part)
    back = [receive_lanes(x) for x in held_back]
    ends = []
    for m in micros:
        ends.append(input_rows(m, back[m], gate_grad[m], full_grad[m], *[x[0] for x in ends[-1:]]))
    returned = ends[-1][0]
    _, reduced_grad, gain_rows, bias_rows = zip(*ends)

    kernel_total = sum(kernel_grads)
    if not direct:
        kernel_total = kernel_total.reshape(dp_count, 2 * chunk, lanes // own, own).sum(axis=2)
    following = jnp.concatenate([kernel_total[1:], jnp.zeros_like(kernel_total[:1])], axis=0)
    kernel_grad = jnp.einsum(
        "kt,ckh->hct", jnp.asarray(inverse_np), kernel_total + sign * following, precision=high
    ).reshape(own, seq_length)
    kernel_grad, _ = lax.optimization_barrier((kernel_grad, reduced_grad))
    kernel_grad = lax.psum_scatter(kernel_grad, "fsdp", scatter_dimension=0, tiled=True)
    pair_grad, decay_grad, frequency_grad, step_grad = kernel_backward(
        kernel_grad, state_weight, decay_rate, frequency, factors
    )

    gain_total = jnp.sum(sum(gain_rows), axis=(0, 1)).reshape(devices, 1, share)
    bias_total = jnp.sum(sum(bias_rows), axis=(0, 1)).reshape(devices, 1, share)
    error_total = jnp.full((devices, 1, share), jnp.sum(sum(error_rows)))
    sums = jnp.concatenate([gain_total, bias_total, error_total], axis=1)
    sums = jnp.pad(sums, ((0, 0), (0, 5), (0, 128 - share)))
    pairs = [
        (normed, gate_grad),
        (state_out, expanded_grad),
        (product, branch_grad),
        (normed, reduced_grad),
    ]
    if all(left[0].shape[1] // devices % 16 == 0 for left, _ in pairs):
        lefts, rights = zip(*pairs)
        gate_sum, expand_sum, out_sum, reduce_sum, sums = product_scatter(
            lefts, rights, ready, sums, 3
        )
    else:
        made = [weight_grad(left, right, 256) for left, right in pairs]
        gate_sum, expand_sum, out_sum, reduce_sum, sums = scatter_all(
            [x.reshape(devices, -1, x.shape[1]) for x in made] + [sums], [4, 2, 4, 1, 1], 3
        )
    loss_value = sums[2, 0] / (width * count)
    return (
        outputs,
        loss_value,
        returned,
        sums[0, :share],
        sums[1, :share],
        gate_sum,
        reduce_sum,
        pair_grad,
        decay_grad,
        frequency_grad,
        step_grad,
        expand_sum,
        out_sum,
    )


def solution(mesh):
    in_specs = (
        P(None, "fsdp", "dp", None),
        P(None, "fsdp", "dp", None),
        P(None, ("dp", "fsdp"), None, None),
        P(),
        P(),
        P(None, ("dp", "fsdp"), None),
        P(("dp", "fsdp")),
        P(("dp", "fsdp")),
        P(("dp", "fsdp"), None),
        P(("dp", "fsdp"), None),
        P(None, ("dp", "fsdp"), None),
        P(("dp", "fsdp"), None),
        P(("dp", "fsdp"), None),
        P(("dp", "fsdp")),
        P(("dp", "fsdp"), None),
        P(("dp", "fsdp"), None),
    )
    out_specs = (
        P(None, "fsdp", "dp", None),
        P(),
        P(None, "fsdp", "dp", None),
        P(("dp", "fsdp")),
        P(("dp", "fsdp")),
        P(("dp", "fsdp"), None),
        P(("dp", "fsdp"), None),
        P(None, ("dp", "fsdp"), None),
        P(("dp", "fsdp"), None),
        P(("dp", "fsdp"), None),
        P(("dp", "fsdp")),
        P(("dp", "fsdp"), None),
        P(("dp", "fsdp"), None),
    )
    return jax.shard_map(shards, mesh=mesh, in_specs=in_specs, out_specs=out_specs, check_vma=False)
```
